32 devices in a mesh: seq: 2 (over x), ctx: 16 (over z, y, core).
Axes of the slice: x: 2, y: 2, z: 4, core: 2. Of those that a mesh axis runs over, the one named last changes fastest.
Arguments:
- layer_input: bfloat16 [2, 2048, 768], P('seq', 'ctx'), may hold values from -6 to 6
- cotangent: bfloat16 [2, 2048, 768], P('seq', 'ctx'), may hold values from -6 to 6
- lengths: int32 [2], P('seq'), may hold values from 1024 to 2048, as said below
- query_weight: bfloat16 [768, 768], P(('seq', 'ctx')), may hold values from -0.4375 to 0.4375
- query_bias: bfloat16 [768], P(('seq', 'ctx')), may hold values from -3 to 3
- key_weight: bfloat16 [768, 768], P(('seq', 'ctx')), may hold values from -0.21875 to 0.21875
- value_weight: bfloat16 [768, 768], P(('seq', 'ctx')), may hold values from -0.21875 to 0.21875
- value_bias: bfloat16 [768], P(('seq', 'ctx')), may hold values from -0.1796875 to 0.1796875
- output_weight: bfloat16 [768, 768], P(('seq', 'ctx')), may hold values from -1.25 to 1.25
- output_bias: bfloat16 [768], P(('seq', 'ctx')), may hold values from -1.796875 to 1.796875
- attn_gain: bfloat16 [768], P(('seq', 'ctx')), may hold values from 0.099609375 to 1.8984375
- attn_shift: bfloat16 [768], P(('seq', 'ctx')), may hold values from -1.796875 to 1.796875
- expand_weight: bfloat16 [768, 3072], P(('seq', 'ctx')), may hold values from -0.21875 to 0.21875
- expand_bias: bfloat16 [3072], P(('seq', 'ctx')), may hold values from -1.796875 to 1.796875
- reduce_weight: bfloat16 [3072, 768], P(('seq', 'ctx')), may hold values from -0.109375 to 0.109375
- reduce_bias: bfloat16 [768], P(('seq', 'ctx')), may hold values from -1.796875 to 1.796875
- final_gain: bfloat16 [768], P(('seq', 'ctx')), may hold values from 0.099609375 to 1.8984375
- final_shift: bfloat16 [768], P(('seq', 'ctx')), may hold values from -1.796875 to 1.796875
Outputs:
- layer_output: bfloat16 [2, 2048, 768], P('seq', 'ctx')
- input_grad: float32 [2, 2048, 768], P('seq', 'ctx')
- query_weight_grad: float32 [768, 768], P(('seq', 'ctx'))
- query_bias_grad: float32 [768], P(('seq', 'ctx'))
- key_weight_grad: float32 [768, 768], P(('seq', 'ctx'))
- value_weight_grad: float32 [768, 768], P(('seq', 'ctx'))
- value_bias_grad: float32 [768], P(('seq', 'ctx'))
- output_weight_grad: float32 [768, 768], P(('seq', 'ctx'))
- output_bias_grad: float32 [768], P(('seq', 'ctx'))
- attn_gain_grad: float32 [768], P(('seq', 'ctx'))
- attn_shift_grad: float32 [768], P(('seq', 'ctx'))
- expand_weight_grad: float32 [768, 3072], P(('seq', 'ctx'))
- expand_bias_grad: float32 [3072], P(('seq', 'ctx'))
- reduce_weight_grad: float32 [3072, 768], P(('seq', 'ctx'))
- reduce_bias_grad: float32 [768], P(('seq', 'ctx'))
- final_gain_grad: float32 [768], P(('seq', 'ctx'))
- final_shift_grad: float32 [768], P(('seq', 'ctx'))
The draws below stay inside these ranges and needn't reach their ends.
Inputs may be any that keep to these rules, and one draw needn't show every extreme that they name: `lengths`: the number of valid tokens of each sequence; slots from it on are padding; some sequence is full in every draw.
All inputs are finite; a program needn't handle non-finite values.
Results may differ from the reference program's by a relative error of at most 0.025.
Values may be sent and summed in bfloat16 or wider, within the bound.
No kernel may reach another device: no remote copies, remote signals or barrier semaphores. Data moves between devices by JAX's collectives and lax.ppermute only.
A program may use at most 576 MiB of HBM per device.

```python
import jax
import jax.numpy as jnp
from jax import lax

D = 768
HEADS = 12
HEAD_DIM = 64
FF = 3072
SEQS = 2
SLOTS = 2048


def draw_lengths(key, part):
    first = jax.random.fold_in(key, 11)
    second = jax.random.fold_in(key, 12)
    drawn = jax.random.randint(first, (SEQS,), SLOTS // 2, SLOTS + 1)
    chosen = jax.random.randint(second, (), 0, SEQS)
    return jnp.where(jnp.arange(SEQS) == chosen, SLOTS, drawn).astype(jnp.int32)


def shard_levels(rng, shape, split, smallest, high):
    level = 1.0
    for axis_at, shards_of in split:
        steps = jax.random.uniform(jax.random.fold_in(jax.random.fold_in(rng, 6), axis_at), (shards_of,), jnp.float32, smallest / len(split), high / len(split))
        level = level * jnp.repeat(jnp.exp(steps), shape[axis_at] // shards_of).reshape((-1,) + (1,) * (len(shape) - 1 - axis_at))
    return level


def bell_draw(stream_key, shape, deviation, most, pieces=(), held_as=jnp.bfloat16):
    result = deviation * jax.random.normal(stream_key, shape, jnp.float32)
    if pieces:
        result = result * shard_levels(stream_key, shape, pieces, -0.22, 0.18)
    return jnp.clip(result, -most, most).astype(held_as)


def setup_inputs(seed: int = 0) -> dict:
    splits = jax.random.split(jax.random.key(seed), 19)
    layer_input = bell_draw(splits[0], (SEQS, SLOTS, D), 1.0, 6.0, ((0, 2), (1, 16)))
    cotangent = bell_draw(splits[1], (SEQS, SLOTS, D), 1.0, 6.0, ((0, 2), (1, 16)))
    lengths = draw_lengths(jax.random.fold_in(splits[18], 71), 0)
    query_weight = bell_draw(splits[3], (D, D), (D // 4) ** -0.5, 0.4375, ((0, 32),))
    query_bias = bell_draw(splits[4], (D,), 0.5, 3.0, ((0, 32),))
    key_weight = bell_draw(splits[5], (D, D), D ** -0.5, 0.21875, ((0, 32),))
    value_weight = bell_draw(splits[6], (D, D), D ** -0.5, 0.21875, ((0, 32),))
    value_bias = bell_draw(splits[7], (D,), 0.03, 0.1796875, ((0, 32),))
    output_weight = bell_draw(splits[8], (D, D), (max(1, D * 64 // SLOTS)) ** -0.5, 1.25, ((0, 32),))
    output_bias = bell_draw(splits[9], (D,), 0.3, 1.796875, ((0, 32),))
    attn_gain = jnp.clip(1.0 + 0.18 * jax.random.normal(splits[10], (D,), jnp.float32), 0.099609375, 1.8984375).astype(jnp.bfloat16)
    attn_shift = bell_draw(splits[11], (D,), 0.3, 1.796875, ((0, 32),))
    expand_weight = bell_draw(splits[12], (D, FF), D ** -0.5, 0.21875, ((0, 32),))
    expand_bias = bell_draw(splits[13], (FF,), 0.3, 1.796875, ((0, 32),))
    reduce_weight = bell_draw(splits[14], (FF, D), FF ** -0.5, 0.109375, ((0, 32),))
    reduce_bias = bell_draw(splits[15], (D,), 0.3, 1.796875, ((0, 32),))
    final_gain = jnp.clip(1.0 + 0.18 * jax.random.normal(splits[16], (D,), jnp.float32), 0.099609375, 1.8984375).astype(jnp.bfloat16)
    final_shift = bell_draw(splits[17], (D,), 0.3, 1.796875, ((0, 32),))
    return {"layer_input": layer_input, "cotangent": cotangent, "lengths": lengths, "query_weight": query_weight, "query_bias": query_bias, "key_weight": key_weight, "value_weight": value_weight, "value_bias": value_bias, "output_weight": output_weight, "output_bias": output_bias, "attn_gain": attn_gain, "attn_shift": attn_shift, "expand_weight": expand_weight, "expand_bias": expand_bias, "reduce_weight": reduce_weight, "reduce_bias": reduce_bias, "final_gain": final_gain, "final_shift": final_shift}


EPSILON = 1e-12
HIGH = lax.Precision.HIGHEST

@jax.custom_vjp
def low(v):
    return lax.optimization_barrier(v.astype(jnp.bfloat16)).astype(jnp.float32)

@jax.custom_vjp
def low_back(v):
    return v

def low_keep(v):
    return (low(v), None)

def low_pass(kept, grad):
    return (grad,)

def back_keep(v):
    return (v, None)

def back_low(kept, grad):
    return (low(grad),)
low.defvjp(low_keep, low_pass)
low_back.defvjp(back_keep, back_low)

def layer_norm(values, gain, shift):
    center = values - lax.optimization_barrier(jnp.mean(values, axis=-1, keepdims=True))
    variance = lax.optimization_barrier(jnp.mean(center * center, axis=-1, keepdims=True))
    return center * lax.rsqrt(variance + EPSILON) * gain + shift

def attend_block(queries, keys, values, valid):
    scores = jnp.einsum('qhd,khd->hqk', queries, keys, precision=HIGH) * 0.125
    scores = jnp.where(valid[None, None, :], scores, -1000000000.0)
    scores = low_back(scores)
    top = lax.optimization_barrier(jnp.max(scores, axis=-1, keepdims=True))
    weights = jnp.exp(scores - top)
    probs = weights / lax.optimization_barrier(jnp.sum(weights, axis=-1, keepdims=True))
    return jnp.einsum('hqk,khd->qhd', low(probs), values, precision=HIGH)

def sequence_forward(params, inputs, length):
    query_w, query_b, key_w, value_w, value_b, output_w, output_b, gain_one, shift_one, expand_w, expand_b, reduce_w, reduce_b, gain_two, shift_two = params
    positions = jnp.arange(SLOTS, dtype=jnp.int32)
    valid = positions < length
    query = low_back(low(jnp.dot(inputs, query_w, precision=HIGH) + query_b))
    key = low_back(low(jnp.dot(inputs, key_w, precision=HIGH)))
    value = low_back(low(jnp.dot(inputs, value_w, precision=HIGH) + value_b))
    key3 = key.reshape(SLOTS, HEADS, HEAD_DIM)
    value3 = value.reshape(SLOTS, HEADS, HEAD_DIM)
    block = min(512, SLOTS)
    query_blocks = query.reshape(SLOTS // block, block, HEADS, HEAD_DIM)

    def one_block(query_part):
        return attend_block(query_part, key3, value3, valid)
    attended = lax.map(jax.checkpoint(one_block), query_blocks)
    attended = low_back(low(attended.reshape(SLOTS, D)))
    hidden = inputs + low_back(jnp.dot(attended, output_w, precision=HIGH)) + output_b
    middle = layer_norm(hidden, gain_one, shift_one)
    expanded = low_back(jnp.dot(low(middle), expand_w, precision=HIGH) + expand_b)
    active = low_back(low(jax.nn.gelu(expanded, approximate=False)))
    combined = middle + low_back(jnp.dot(active, reduce_w, precision=HIGH)) + reduce_b
    return layer_norm(combined, gain_two, shift_two)

def reference(layer_input, cotangent, lengths, query_weight, query_bias, key_weight, value_weight, value_bias, output_weight, output_bias, attn_gain, attn_shift, expand_weight, expand_bias, reduce_weight, reduce_bias, final_gain, final_shift):
    raw = (query_weight, query_bias, key_weight, value_weight, value_bias, output_weight, output_bias, attn_gain, attn_shift, expand_weight, expand_bias, reduce_weight, reduce_bias, final_gain, final_shift)
    params = tuple((item.astype(jnp.float32) for item in raw))
    inputs = layer_input.astype(jnp.float32)
    positions = jnp.arange(SLOTS, dtype=jnp.int32)
    valid_rows = (positions[None, :] < lengths[:, None]).astype(jnp.float32)
    upstream = cotangent.astype(jnp.float32) * valid_rows[:, :, None]

    def forward(weights, activations):

        def advance(carry, pair):
            return (carry, sequence_forward(weights, pair[0], pair[1]))
        unused, outputs = lax.scan(advance, jnp.zeros((), jnp.int32), (activations, lengths))
        return outputs
    outputs, pullback = jax.vjp(forward, params, inputs)
    grads, input_grad = pullback(upstream)
    return (outputs.astype(jnp.bfloat16), input_grad, grads[0], grads[1], grads[2], grads[3], grads[4], grads[5], grads[6], grads[7], grads[8], grads[9], grads[10], grads[11], grads[12], grads[13], grads[14])
```

```python
import functools

import jax
import jax.numpy as jnp
from jax import lax
from jax.experimental import pallas as pl
from jax.experimental.pallas import tpu as pltpu
from jax.sharding import PartitionSpec as P

HEADS = 12
HEAD_DIM = 64
EPSILON = 1e-12
MASKED = -1000000000.0
EVERY = ("seq", "ctx")
F32 = jnp.float32
BF16 = jnp.bfloat16


def dot(left, right):
    return jnp.dot(left, right, preferred_element_type=F32)


def contract_rows(left, right):
    return lax.dot_general(left, right, (((0,), (0,)), ((), ())), preferred_element_type=F32)


def times_transpose(left, right):
    return lax.dot_general(left, right, (((1,), (1,)), ((), ())), preferred_element_type=F32)


def take(array, index, axis=0):
    return lax.dynamic_index_in_dim(array, index, axis, keepdims=False)


class Place:
    def __init__(self):
        self.seqs = lax.axis_size("seq")
        self.ctx = lax.axis_size("ctx")
        self.count = self.seqs * self.ctx
        self.bits = self.count.bit_length() - 1
        self.number = lax.axis_index("seq") * self.ctx + lax.axis_index("ctx")
        self.core = self.number & 1
        self.top = self.bits - 1
        self.middle = self.count // 8
        self.middle_bits = list(range(2, self.top))

    def bit(self, which):
        return (self.number >> which) & 1

    def swap(self, array, even, odd=None):
        odd = even if odd is None else odd
        pairs = [(i, i ^ (1 << (odd if i & 1 else even))) for i in range(self.count)]
        return lax.ppermute(array, EVERY, pairs)

    def join(self, mine, other, which, axis):
        first = self.bit(which) == 0
        return jnp.stack([jnp.where(first, mine, other), jnp.where(first, other, mine)], axis)

    def gather_middle(self, array):
        for at in reversed(self.middle_bits):
            if at == self.middle_bits[-1]:
                array = self.join(array, self.swap(array, at), at, 0)
            else:
                got = self.join(array, self.swap(array, at), at, 1)
                array = got.reshape((-1,) + got.shape[2:])
        return array

    def gather_chips(self, array):
        block = self.gather_middle(array)
        near = self.swap(block, 1, self.top)
        far = self.swap(jnp.stack([block, near]), self.top, 1)
        x, y = self.bit(self.top), self.bit(1)
        even = self.core == 0
        nx, ny = jnp.where(even, x, 1 - x), jnp.where(even, 1 - y, y)
        fx, fy = jnp.where(even, 1 - x, x), jnp.where(even, y, 1 - y)
        out = jnp.zeros((2, self.middle, 2) + array.shape, array.dtype)
        zero = (0,) * array.ndim
        for part, px, py in (
            (block, x, y),
            (near, nx, ny),
            (far[0], fx, fy),
            (far[1], 1 - x, 1 - y),
        ):
            out = lax.dynamic_update_slice(out, part[None, :, None], (px, 0, py) + zero)
        return out

    def scatter_middle(self, array):
        for at in self.middle_bits:
            half = array.reshape((-1, 2) + array.shape[1:])
            mine, theirs = take(half, self.bit(at), 1), take(half, 1 - self.bit(at), 1)
            got = self.swap(theirs.astype(BF16), at)
            array = mine.astype(F32) + got.astype(F32)
        return array[0]

    def scatter_chips(self, array):
        x, y = self.bit(self.top), self.bit(1)
        even = self.core == 0
        nx, ny = jnp.where(even, x, 1 - x), jnp.where(even, 1 - y, y)
        fx, fy = jnp.where(even, 1 - x, x), jnp.where(even, y, 1 - y)

        def block(px, py):
            size = (1, self.middle, 1) + array.shape[3:]
            part = lax.dynamic_slice(array, (px, 0, py) + (0,) * (array.ndim - 3), size)
            return part.reshape((self.middle,) + array.shape[3:])

        sent = jnp.stack([block(fx, fy), block(1 - x, 1 - y)]).astype(BF16)
        got = self.swap(sent, self.top, 1)
        kept = block(x, y).astype(F32) + got[0].astype(F32)
        passed = (block(nx, ny).astype(F32) + got[1].astype(F32)).astype(BF16)
        kept = kept + self.swap(passed, 1, self.top).astype(F32)
        return self.scatter_middle(kept)


def split_pair(ref):
    return ref[:, :HEAD_DIM], ref[:, HEAD_DIM:]


def masked_scores(query, key, valid):
    scores = times_transpose(query, key) * 0.125
    return jnp.where(valid, scores, MASKED)


def attend_kernel(length_ref, q_ref, k_ref, v_ref, out_ref, logs_ref):
    tokens = k_ref.shape[0]
    rows = q_ref.shape[0]
    valid = lax.broadcasted_iota(jnp.int32, (rows, tokens), 1) < length_ref[0]
    for half in range(2):
        at = slice(half * HEAD_DIM, (half + 1) * HEAD_DIM)
        scores = masked_scores(q_ref[:, at], k_ref[:, at], valid)
        top = jnp.max(scores, axis=-1, keepdims=True)
        weights = jnp.exp(scores - top)
        total = jnp.sum(weights, axis=-1, keepdims=True)
        summed = dot(weights.astype(BF16), v_ref[:, at])
        out_ref[:, at] = summed / total
        logs_ref[:, at] = jnp.broadcast_to(top + jnp.log(total), (rows, HEAD_DIM))


def attend(length, query, key, value):
    rows, width = query.shape
    tokens = key.shape[0]
    step = rows if tokens <= 4096 else 16
    pair = 2 * HEAD_DIM
    spec_q = pl.BlockSpec((step, pair), lambda h, i, n: (i, h))
    spec_k = pl.BlockSpec((tokens, pair), lambda h, i, n: (0, h))
    cost = 4 * rows * tokens * width
    return pl.pallas_call(
        attend_kernel,
        out_shape=(
            jax.ShapeDtypeStruct((rows, width), F32),
            jax.ShapeDtypeStruct((rows, width), F32),
        ),
        grid_spec=pltpu.PrefetchScalarGridSpec(
            num_scalar_prefetch=1,
            grid=(width // pair, rows // step),
            in_specs=[spec_q, spec_k, spec_k],
            out_specs=[spec_q, spec_q],
        ),
        cost_estimate=pl.CostEstimate(
            flops=4 * cost, bytes_accessed=4 * tokens * width, transcendentals=rows * tokens * 6
        ),
        name="attend",
    )(length, query, key, value)


def attend_back_kernel(
    length_ref, q_ref, k_ref, v_ref, g_ref, o_ref, logs_ref, dq_ref, dk_ref, dv_ref, dk_sum, dv_sum
):
    tokens = k_ref.shape[0]
    rows = q_ref.shape[0]
    step = pl.program_id(1)
    valid = lax.broadcasted_iota(jnp.int32, (rows, tokens), 1) < length_ref[0]

    @pl.when(step == 0)
    def _():
        dk_sum[...] = jnp.zeros_like(dk_sum)
        dv_sum[...] = jnp.zeros_like(dv_sum)

    for half in range(2):
        at = slice(half * HEAD_DIM, (half + 1) * HEAD_DIM)
        query, key, value, grad = q_ref[:, at], k_ref[:, at], v_ref[:, at], g_ref[:, at]
        scores = masked_scores(query, key, valid)
        probs = jnp.exp(scores - logs_ref[:, half * HEAD_DIM : half * HEAD_DIM + 1])
        dots = jnp.sum(grad.astype(F32) * o_ref[:, at], axis=-1, keepdims=True)
        grad_scores = (probs * (times_transpose(grad, value) - dots)).astype(BF16)
        dq_ref[:, at] = (dot(grad_scores, key) * 0.125).astype(BF16)
        dk_sum[:, at] += contract_rows(grad_scores, query)
        dv_sum[:, at] += contract_rows(probs.astype(BF16), grad)

    @pl.when(step == pl.num_programs(1) - 1)
    def _():
        dk_ref[...] = (dk_sum[...] * 0.125).astype(BF16)
        dv_ref[...] = dv_sum[...].astype(BF16)


def attend_back(length, query, key, value, grad, attended, logs):
    rows, width = query.shape
    tokens = key.shape[0]
    step = rows if tokens <= 4096 else 16
    pair = 2 * HEAD_DIM
    spec_q = pl.BlockSpec((step, pair), lambda h, i, n: (i, h))
    spec_k = pl.BlockSpec((tokens, pair), lambda h, i, n: (0, h))
    cost = 10 * rows * tokens * width
    return pl.pallas_call(
        attend_back_kernel,
        out_shape=(
            jax.ShapeDtypeStruct((rows, width), BF16),
            jax.ShapeDtypeStruct((tokens, width), BF16),
            jax.ShapeDtypeStruct((tokens, width), BF16),
        ),
        grid_spec=pltpu.PrefetchScalarGridSpec(
            num_scalar_prefetch=1,
            grid=(width // pair, rows // step),
            in_specs=[spec_q, spec_k, spec_k, spec_q, spec_q, spec_q],
            out_specs=[spec_q, spec_k, spec_k],
            scratch_shapes=[pltpu.VMEM((tokens, pair), F32), pltpu.VMEM((tokens, pair), F32)],
        ),
        cost_estimate=pl.CostEstimate(
            flops=4 * cost, bytes_accessed=8 * tokens * width, transcendentals=rows * tokens * 6
        ),
        name="attend_back",
    )(length, query, key, value, grad, attended, logs)


def normalize(values):
    center = values - jnp.mean(values, axis=-1, keepdims=True)
    scale = lax.rsqrt(jnp.mean(center * center, axis=-1, keepdims=True) + EPSILON)
    return center * scale, scale


def normalize_back(grad, normal, scale):
    return scale * (
        grad
        - jnp.mean(grad, axis=-1, keepdims=True)
        - normal * jnp.mean(grad * normal, axis=-1, keepdims=True)
    )


def gelu_exact(values):
    return jax.nn.gelu(values, approximate=False)


def body(
    layer_input,
    cotangent,
    lengths,
    query_weight,
    query_bias,
    key_weight,
    value_weight,
    value_bias,
    output_weight,
    output_bias,
    attn_gain,
    attn_shift,
    expand_weight,
    expand_bias,
    reduce_weight,
    reduce_bias,
    final_gain,
    final_shift,
):
    place = Place()
    core = place.core
    chips = place.count // 2
    inputs = layer_input[0]
    rows, width = inputs.shape
    half = width // 2
    own = query_weight.shape[0]
    units = reduce_weight.shape[0]
    hidden_units = units * chips
    length = lengths[:1]
    middle_count = place.middle

    vectors = [query_bias, value_bias, output_bias, attn_gain, attn_shift, expand_bias, reduce_bias, final_gain, final_shift]
    sizes = [v.shape[0] for v in vectors]
    vector_row = jnp.concatenate(vectors)
    vector_row = jnp.pad(vector_row, (0, half - vector_row.shape[0]))[None]

    def column_halves(weight):
        return weight[:, :half], weight[:, half:]

    def pick(pair, which):
        return jnp.where(which == 0, pair[0], pair[1])

    expand4 = expand_weight.reshape(own, chips, 2, units)
    expand_pair = (
        expand4[:, :, 0, :].reshape(own, hidden_units),
        expand4[:, :, 1, :].reshape(own, hidden_units),
    )

    def packed(which):
        flat = [pick(column_halves(w), which) for w in (query_weight, key_weight, value_weight)]
        return jnp.concatenate(flat + [jnp.pad(vector_row, ((0, 7), (0, 0)))], axis=0)

    def packed_late(which):
        out_part = pick(column_halves(output_weight), which)
        wide = pick(expand_pair, which)
        pieces = [wide[:, i * half : (i + 1) * half] for i in range(hidden_units // half)]
        return jnp.concatenate([out_part] + pieces, axis=0)

    early_mine, early_other = packed(core), place.swap(packed(1 - core), 0)
    late_mine, late_other = packed_late(core), place.swap(packed_late(1 - core), 0)
    early = place.join(early_mine, early_other, 0, 0)
    late = place.join(late_mine, late_other, 0, 0)

    near = place.gather_middle(inputs)
    both = place.join(near, place.swap(near, 1), 1, 1)
    sequence = place.join(both, place.swap(both, 0), 0, 2).reshape(-1, width)
    tokens = sequence.shape[0]

    early_all = place.gather_chips(early).reshape(chips, 2, -1, half)
    late_all = place.gather_chips(late).reshape(chips, 2, -1, half)
    reduce_all = place.gather_chips(reduce_weight).reshape(hidden_units, width)

    def early_weight(i):
        return early_all[:, :, i * own : (i + 1) * own].reshape(width, half)

    def late_weight(i):
        return late_all[:, :, i * own : (i + 1) * own].reshape(width, half)

    query_half, key_half, value_half = (early_weight(i) for i in range(3))
    vector_all = early_all[:, :, 3 * own].reshape(2 * chips, half)
    split = []
    at = 0
    for size in sizes:
        split.append(vector_all[:, at : at + size].astype(F32))
        at += size
    query_offset, value_offset, output_offset, gain_one, shift_one, expand_offset, reduce_offset, gain_two, shift_two = split
    expand_half_offset = take(expand_offset.reshape(chips, 2, units), core, 1).reshape(-1)
    query_offset, value_offset, output_offset, gain_one, shift_one, reduce_offset, gain_two, shift_two = (
        v.reshape(width)
        for v in (query_offset, value_offset, output_offset, gain_one, shift_one, reduce_offset, gain_two, shift_two)
    )
    query_half_offset = lax.dynamic_slice(query_offset, (core * half,), (half,))
    value_half_offset = lax.dynamic_slice(value_offset, (core * half,), (half,))

    chip_rows = 2 * rows
    chip_start = (lax.axis_index("ctx") // 2) * chip_rows
    chip_inputs = lax.dynamic_slice(sequence, (chip_start, 0), (chip_rows, width))
    query = (dot(chip_inputs, query_half) + query_half_offset).astype(BF16)
    key = dot(sequence, key_half).astype(BF16)
    value = (dot(sequence, value_half) + value_half_offset).astype(BF16)
    attended, logs = attend(length, query, key, value)
    attended_low = attended.astype(BF16)

    def to_tokens(array):
        pair = array.reshape(2, rows, half)
        other = place.swap(take(pair, 1 - core), 0)
        return place.join(take(pair, core), other, 0, 1).reshape(rows, width)

    def to_heads(array):
        pair = array.reshape(rows, 2, half)
        other = place.swap(take(pair, 1 - core, 1), 0)
        return place.join(take(pair, core, 1), other, 0, 0).reshape(chip_rows, half)

    def to_chip(array):
        return place.join(array, place.swap(array, 0), 0, 0).reshape(chip_rows, array.shape[1])

    def core_sum(array):
        pair = array.reshape(2, rows, array.shape[1])
        return take(pair, core) + place.swap(take(pair, 1 - core), 0)

    attended_own = to_tokens(attended_low)
    output_half = late_weight(0)
    output_matrix = place.join(output_half, place.swap(output_half, 0), 0, 1).reshape(width, width)

    hidden = inputs.astype(F32) + dot(attended_own, output_matrix) + output_offset
    normal_one, scale_one = normalize(hidden)
    middle = normal_one * gain_one + shift_one
    middle_low = middle.astype(BF16)

    expand_matrix = jnp.concatenate([late_weight(1 + i) for i in range(hidden_units // half)], axis=1)
    middle_chip = to_chip(middle_low)
    expanded = dot(middle_chip, expand_matrix) + expand_half_offset
    active = gelu_exact(expanded).astype(BF16)
    combined = middle + core_sum(dot(active, reduce_all)) + reduce_offset
    normal_two, scale_two = normalize(combined)
    layer_output = normal_two * gain_two + shift_two

    own_rows = lax.axis_index("ctx") * rows + jnp.arange(rows, dtype=jnp.int32)
    upstream = cotangent[0].astype(F32) * (own_rows < length[0]).astype(F32)[:, None]
    grad_gain_two = jnp.sum(upstream * normal_two, axis=0)
    grad_shift_two = jnp.sum(upstream, axis=0)
    grad_combined = normalize_back(upstream * gain_two, normal_two, scale_two)
    combined_low = grad_combined.astype(BF16)
    combined_chip = to_chip(combined_low)
    grad_reduce = contract_rows(active, combined_chip)
    grad_reduce_bias = jnp.sum(grad_combined, axis=0)
    grad_active = times_transpose(combined_chip, reduce_all).astype(BF16)
    unused, gelu_back = jax.vjp(gelu_exact, expanded)
    grad_expanded = gelu_back(grad_active.astype(F32))[0].astype(BF16)
    grad_expand = contract_rows(middle_chip, grad_expanded)
    grad_expand_bias = jnp.sum(grad_expanded.astype(F32), axis=0)
    grad_middle = grad_combined + core_sum(times_transpose(grad_expanded, expand_matrix))

    reduce_out = place.scatter_chips(grad_reduce.reshape(2, middle_count, 2, units, width))
    expand_sum = place.scatter_chips(
        grad_expand.reshape(2, middle_count, 2, 2, own, hidden_units)
    )
    expand_swap = place.swap(take(expand_sum, 1 - core), 0)
    expand_out = place.join(
        take(expand_sum, core).reshape(own, chips, units), expand_swap.reshape(own, chips, units), 0, 2
    ).reshape(own, 2 * hidden_units)

    grad_gain_one = jnp.sum(grad_middle * normal_one, axis=0)
    grad_shift_one = jnp.sum(grad_middle, axis=0)
    grad_hidden = normalize_back(grad_middle * gain_one, normal_one, scale_one)
    hidden_low = grad_hidden.astype(BF16)
    grad_output_bias = jnp.sum(grad_hidden, axis=0)
    grad_output = contract_rows(attended_own, hidden_low).reshape(width, 2, half)
    grad_output_half = take(grad_output, core, 1) + place.swap(
        take(grad_output, 1 - core, 1).astype(BF16), 0
    ).astype(F32)
    grad_attended = times_transpose(hidden_low, output_matrix).astype(BF16)

    grad_heads = to_heads(grad_attended)
    grad_query, key_part, value_part = attend_back(length, query, key, value, grad_heads, attended, logs)
    input_part = times_transpose(key_part, key_half) + times_transpose(value_part, value_half)
    input_pair = input_part.reshape(middle_count, 2, 2, rows, width)
    input_core = take(input_pair, core, 2) + place.swap(
        take(input_pair, 1 - core, 2).astype(BF16), 0
    ).astype(F32)
    input_y = take(input_core, place.bit(1), 1) + place.swap(
        take(input_core, 1 - place.bit(1), 1).astype(BF16), 1
    ).astype(F32)
    input_sum = place.scatter_middle(input_y)
    query_sum = core_sum(times_transpose(grad_query, query_half))
    input_grad = grad_hidden + input_sum + query_sum

    grad_query_w = contract_rows(chip_inputs, grad_query)
    grad_key_w = contract_rows(sequence, key_part)
    grad_value_w = contract_rows(sequence, value_part)
    grad_query_b = jnp.sum(grad_query.astype(F32), axis=0)
    grad_value_b = jnp.sum(value_part.astype(F32), axis=0)

    def spread(vector, which):
        zero = jnp.zeros_like(vector)
        return jnp.where(which == 0, jnp.concatenate([vector, zero]), jnp.concatenate([zero, vector]))

    expand_rows = grad_expand_bias.reshape(chips, 1, units)
    zero_rows = jnp.zeros_like(expand_rows)
    expand_rows = jnp.where(
        core == 0,
        jnp.concatenate([expand_rows, zero_rows], 1),
        jnp.concatenate([zero_rows, expand_rows], 1),
    )
    grads = [
        spread(grad_query_b, core).reshape(chips, 2, own),
        spread(grad_value_b, core).reshape(chips, 2, own),
        grad_output_bias.reshape(chips, 2, own),
        grad_gain_one.reshape(chips, 2, own),
        grad_shift_one.reshape(chips, 2, own),
        expand_rows,
        grad_reduce_bias.reshape(chips, 2, own),
        grad_gain_two.reshape(chips, 2, own),
        grad_shift_two.reshape(chips, 2, own),
    ]
    grads = jnp.concatenate(grads, axis=2)
    filled = grads.shape[2]
    grads = jnp.pad(grads, ((0, 0), (0, 0), (0, half - filled)))
    vector_sum = take(grads, core, 1) + place.swap(take(grads, 1 - core, 1), 0)
    vector_rows = jnp.pad(vector_sum[:, None], ((0, 0), (0, 7), (0, 0)))

    parts = [
        g.reshape(chips, 2 * own, half)
        for g in (grad_query_w, grad_key_w, grad_value_w, grad_output_half)
    ]
    late_grads = jnp.concatenate(parts + [vector_rows], axis=1)
    late_sum = place.scatter_chips(
        late_grads.reshape((2, middle_count, 2) + late_grads.shape[1:])
    )
    weights_sum = late_sum[: 8 * own].reshape(4, 2, own, half)
    other = place.swap(take(weights_sum, 1 - core, 1), 0)
    weights_out = place.join(take(weights_sum, core, 1), other, 0, 2).reshape(4, own, width)
    vector_out = late_sum[8 * own]
    vectors_out = []
    at = 0
    for size in sizes:
        vectors_out.append(vector_out[at : at + size])
        at += size
    (
        query_b_out,
        value_b_out,
        output_b_out,
        gain_one_out,
        shift_one_out,
        expand_b_out,
        reduce_b_out,
        gain_two_out,
        shift_two_out,
    ) = vectors_out
    return (
        layer_output.astype(BF16)[None],
        input_grad[None],
        weights_out[0],
        query_b_out,
        weights_out[1],
        weights_out[2],
        value_b_out,
        weights_out[3],
        output_b_out,
        gain_one_out,
        shift_one_out,
        expand_out,
        expand_b_out,
        reduce_out,
        reduce_b_out,
        gain_two_out,
        shift_two_out,
    )


def solution(mesh):
    tokens = P("seq", "ctx", None)
    matrix = P(("seq", "ctx"), None)
    vector = P(("seq", "ctx"))
    placed = (
        tokens,
        tokens,
        P("seq"),
        matrix,
        vector,
        matrix,
        matrix,
        vector,
        matrix,
        vector,
        vector,
        vector,
        matrix,
        vector,
        matrix,
        vector,
        vector,
        vector,
    )
    return jax.shard_map(
        body,
        mesh=mesh,
        in_specs=placed,
        out_specs=(
            tokens,
            tokens,
            matrix,
            vector,
            matrix,
            matrix,
            vector,
            matrix,
            vector,
            vector,
            vector,
            matrix,
            vector,
            matrix,
            vector,
            vector,
            vector,
        ),
        check_vma=False,
    )
```

```python
import functools

import jax
import jax.numpy as jnp
import numpy as np
from jax import lax
from jax.experimental import pallas as pl
from jax.experimental.pallas import tpu as pltpu
from jax.sharding import PartitionSpec as P

HEADS = 12
HEAD_DIM = 64
EPSILON = 1e-12
MASKED = -1000000000.0
EVERY = ("seq", "ctx")
F32 = jnp.float32
BF16 = jnp.bfloat16
VMEM = pl.BlockSpec(memory_space=pltpu.VMEM)
SMEM = pl.BlockSpec(memory_space=pltpu.SMEM)
QUERY_B, VALUE_B, OUTPUT_B, GAIN_1, SHIFT_1, REDUCE_B, GAIN_2, SHIFT_2, EXPAND_B = range(9)
VECTOR_ROWS = 16
HELD_BYTES = 16 << 20


def dot(left, right):
    return jnp.dot(left, right, preferred_element_type=F32)


def contract_rows(left, right):
    return lax.dot_general(left, right, (((0,), (0,)), ((), ())), preferred_element_type=F32)


def times_transpose(left, right):
    return lax.dot_general(left, right, (((1,), (1,)), ((), ())), preferred_element_type=F32)


def shaped(shape, dtype):
    return jax.ShapeDtypeStruct(tuple(shape), dtype)


def after(array, *earlier):
    return lax.optimization_barrier((array, *earlier))[0]


def call(kernel, name, outs, *args, scalars=0, flops=0, moved=0, scratch=(), room=16, held=True):
    many = isinstance(outs, (tuple, list))
    flat = tuple(outs) if many else (outs,)
    size = sum(a.size * a.dtype.itemsize for a in (*args, *flat))
    if held and size < HELD_BYTES:
        args = args[:scalars] + tuple(pltpu.with_memory_space_constraint(a, pltpu.VMEM) for a in args[scalars:])
        flat = tuple(pltpu.VMEM(o.shape, o.dtype) for o in flat)
    return pl.pallas_call(
        kernel,
        out_shape=flat if many else flat[0],
        in_specs=[SMEM] * scalars + [VMEM] * (len(args) - scalars),
        out_specs=tuple(VMEM for _ in flat) if many else VMEM,
        scratch_shapes=list(scratch),
        cost_estimate=pl.CostEstimate(flops=int(flops), bytes_accessed=int(moved), transcendentals=0),
        compiler_params=pltpu.CompilerParams(vmem_limit_bytes=room << 20 if size < HELD_BYTES else None),
        name=name,
    )(*args)


def limit(tokens, mebibytes):
    return pltpu.CompilerParams(vmem_limit_bytes=mebibytes << 20 if tokens <= 4096 else None)


class Place:
    def __init__(self):
        self.ctx = lax.axis_size("ctx")
        self.count = lax.axis_size("seq") * self.ctx
        self.bits = self.count.bit_length() - 1
        self.context = lax.axis_index("ctx")
        self.number = lax.axis_index("seq") * self.ctx + self.context
        self.core = self.number & 1
        top = self.bits - 1
        middle = list(range(2, top))
        self.weight_stages = list(zip(middle[::-1], middle)) + [(1, top), (top, 1)]
        self.token_stages = [(1, 1)] + list(zip(middle[::-1], middle))

    def swap(self, array, even, odd=None):
        odd = even if odd is None else odd
        pairs = [(i, i ^ (1 << (odd if i & 1 else even))) for i in range(self.count)]
        return lax.ppermute(array, EVERY, pairs)

    def others(self, stages, core):
        masks = [0]
        for stage in stages:
            masks = masks + [m ^ (1 << stage[core]) for m in masks]
        return np.array(masks, np.int32)

    def gather(self, blocks, stages, stop=0):
        other = None
        for at, stage in enumerate(stages):
            if at:
                blocks = jnp.concatenate([blocks, other])
            other = self.swap(blocks, *stage)
        return blocks, other

    def scatter(self, mine, theirs, stages):
        for at, stage in enumerate(stages[::-1]):
            if at:
                half = mine.shape[0] // 2
                mine, theirs = mine[:half], mine[half:]
            got = self.swap(theirs, *stage)
            mine = (mine.astype(F32) + got.astype(F32)).astype(F32 if at == len(stages) - 1 else BF16)
        return mine[0]


def pack_vectors_kernel(number_ref, *refs):
    *in_refs, expand_ref, out_ref, rows_ref = refs
    own, units, width = in_refs[0].shape[1], expand_ref.shape[1], out_ref.shape[1]
    number = number_ref[0]
    rows_ref[...] = jnp.zeros_like(rows_ref)
    for i, ref in enumerate(in_refs):
        rows_ref[i : i + 1, :own] = ref[...].astype(F32)
    rows_ref[EXPAND_B : EXPAND_B + 1, :units] = expand_ref[...].astype(F32)
    first = pltpu.roll(rows_ref[:8, :], number * own, 1)
    offset = (number // 2) * units
    second = pltpu.roll(rows_ref[8:, :], offset % width, 1)
    here = lax.broadcasted_iota(jnp.int32, second.shape, 0) == offset // width
    second = jnp.where(here, jnp.broadcast_to(second[:1], second.shape), 0.0)
    out_ref[...] = jnp.concatenate([first, second], 0).astype(BF16)


def unpack_vectors_kernel(number_ref, sums_ref, *out_refs):
    own, units, width = out_refs[0].shape[1], out_refs[-1].shape[1], sums_ref.shape[1]
    number = number_ref[0]
    first = pltpu.roll(sums_ref[:8, :], width - number * own, 1)
    for i, ref in enumerate(out_refs[:-1]):
        ref[...] = first[i : i + 1, :own]
    offset = (number // 2) * units
    here = lax.broadcasted_iota(jnp.int32, (VECTOR_ROWS - 8, width), 0) == offset // width
    row = jnp.sum(jnp.where(here, sums_ref[8:, :], 0.0), axis=0, keepdims=True)
    row = pltpu.roll(jnp.broadcast_to(row, (8, width)), width - offset % width, 1)
    out_refs[-1][...] = row[:1, :units]


def place_attention_kernel(table_ref, core_ref, mine_ref, other_ref, vector_ref, kv_ref, q_ref, o_ref, bias_ref):
    half = kv_ref.shape[0] // 2
    rows, side = q_ref.shape[1], q_ref.shape[2]
    tile = mine_ref.shape[1]
    tiles = rows // tile

    def body(j, carry):
        for ref, at in ((mine_ref, j), (other_ref, j + half)):
            chip = table_ref[at]
            for i in range(tiles):
                to = slice(i * tile, (i + 1) * tile)
                kv_ref[chip, to] = ref[j * (2 * tiles) + i]
                q_ref[chip, to] = ref[j * (2 * tiles) + tiles + i, :, :side]
                o_ref[chip, to] = ref[j * (2 * tiles) + tiles + i, :, side:]
        return carry

    lax.fori_loop(0, half, body, 0)
    values = vector_ref[...].astype(F32)
    values = jnp.where(core_ref[0] == 0, values[:8, :side], values[:8, side:])
    bias_ref[:, :side] = jnp.zeros((8, side), F32)
    bias_ref[:, side : 2 * side] = jnp.broadcast_to(values[VALUE_B : VALUE_B + 1], (8, side))
    bias_ref[:, 2 * side :] = jnp.broadcast_to(values[QUERY_B : QUERY_B + 1], (8, side))


def place_expand_kernel(table_ref, mine_ref, other_ref, expand_ref):
    half = mine_ref.shape[0]
    rows, width = expand_ref.shape[1], mine_ref.shape[2]

    def body(j, carry):
        for ref, at in ((mine_ref, j), (other_ref, j + half)):
            chip = table_ref[at]
            for i in range(expand_ref.shape[2] // width):
                expand_ref[chip, :, i * width : (i + 1) * width] = ref[j, i * rows : (i + 1) * rows]
        return carry

    lax.fori_loop(0, half, body, 0)


def place_reduce_kernel(table_ref, mine_ref, other_ref, reduce_ref):
    half = mine_ref.shape[0]

    def body(j, carry):
        reduce_ref[table_ref[j]] = mine_ref[j]
        reduce_ref[table_ref[j + half]] = other_ref[j]
        return carry

    lax.fori_loop(0, half, body, 0)


def split_expand_kernel(table_ref, expand_ref, mine_ref, other_ref):
    half = mine_ref.shape[0]
    rows, width = expand_ref.shape[1], mine_ref.shape[2]

    def body(j, carry):
        for ref, at in ((mine_ref, j), (other_ref, j + half)):
            chip = table_ref[at]
            for i in range(expand_ref.shape[2] // width):
                ref[j, i * rows : (i + 1) * rows] = expand_ref[chip, :, i * width : (i + 1) * width]
        return carry

    lax.fori_loop(0, half, body, 0)


def split_reduce_kernel(table_ref, reduce_ref, mine_ref, other_ref):
    half = mine_ref.shape[0]

    def body(j, carry):
        mine_ref[j] = reduce_ref[table_ref[j]]
        other_ref[j] = reduce_ref[table_ref[j + half]]
        return carry

    lax.fori_loop(0, half, body, 0)


def split_attention_kernel(table_ref, kv_ref, q_ref, o_ref, mine_ref, other_ref):
    half = mine_ref.shape[0]
    rows, side = q_ref.shape[1], q_ref.shape[2]

    def body(j, carry):
        for ref, at in ((mine_ref, j), (other_ref, j + half)):
            chip = table_ref[at]
            ref[j, :rows] = kv_ref[chip]
            ref[j, rows:, :side] = q_ref[chip]
            ref[j, rows:, side:] = o_ref[chip]
        return carry

    lax.fori_loop(0, half, body, 0)


def fold_kernel(keep_ref, got_ref, *out_refs):
    if len(out_refs) == 1:
        out_refs[0][...] = keep_ref[...].astype(F32) + got_ref[...].astype(F32)
        return
    half = out_refs[0].shape[0]
    for i, ref in enumerate(out_refs):
        at = slice(i * half, (i + 1) * half)
        ref[...] = (keep_ref[at].astype(F32) + got_ref[at].astype(F32)).astype(BF16)


def fold(keep, got):
    blocks = keep.shape[0]
    out = shaped(keep.shape, F32) if blocks == 1 else (shaped((blocks // 2,) + keep.shape[1:], BF16),) * 2
    out = call(fold_kernel, "fold", out, keep, got, moved=2 * keep.size)
    return out[0] if blocks == 1 else out


def fold_vectors_kernel(keep_ref, got_ref, vector_ref, *out_refs):
    rows = keep_ref.shape[0]
    vectors = vector_ref[...] + got_ref[rows:, :].astype(F32)
    out_refs[-1][...] = vectors
    if len(out_refs) == 2:
        out_refs[0][...] = keep_ref[...].astype(F32) + got_ref[:rows, :].astype(F32)
        return
    half = rows // 2
    total = keep_ref[...].astype(F32) + got_ref[:rows, :].astype(F32)
    out_refs[0][...] = total[:half].astype(BF16)
    out_refs[1][:half, :] = total[half:].astype(BF16)
    out_refs[1][half:, :] = vectors.astype(BF16)


def fold_vectors(keep, got, vectors, last):
    rows, width = keep.shape
    if last:
        out = (shaped((rows, width), F32), shaped(vectors.shape, F32))
    else:
        out = (
            shaped((rows // 2, width), BF16),
            shaped((rows // 2 + VECTOR_ROWS, width), BF16),
            shaped(vectors.shape, F32),
        )
    return call(fold_vectors_kernel, "fold_vectors", out, keep, got, vectors, moved=2 * keep.size)


def project_kernel(mine_ref, other_ref, weight_ref, bias_ref, out_ref):
    width = weight_ref.shape[1]
    bias = bias_ref[:1, :width]

    @pl.when(pl.program_id(0) == 0)
    def _():
        out_ref[...] = (dot(mine_ref[...], weight_ref[...]) + bias).astype(BF16)

    @pl.when(pl.program_id(0) == 1)
    def _():
        out_ref[...] = (dot(other_ref[...], weight_ref[...]) + bias).astype(BF16)


def project(mine, other, weight, bias):
    rows, width = mine.shape
    step = min(rows, 512)
    steps = rows // step
    return pl.pallas_call(
        project_kernel,
        out_shape=shaped((2 * rows, width), BF16),
        grid=(2, steps),
        in_specs=[
            pl.BlockSpec((step, width), lambda i, j: (jnp.where(i == 0, j, steps - 1), 0)),
            pl.BlockSpec((step, width), lambda i, j: (jnp.where(i == 0, 0, j), 0)),
            pl.BlockSpec(weight.shape, lambda i, j: (0, 0)),
            pl.BlockSpec(bias.shape, lambda i, j: (0, 0)),
        ],
        out_specs=pl.BlockSpec((step, width), lambda i, j: (i * steps + j, 0)),
        cost_estimate=pl.CostEstimate(
            flops=4 * rows * width * width, bytes_accessed=8 * rows * width, transcendentals=0
        ),
        compiler_params=limit(2 * rows, 20),
        name="project",
    )(mine, other, weight, bias)


def attend_kernel(q_ref, k_ref, v_ref, mask_ref, out_ref, logs_ref):
    mask = mask_ref[:, :1].astype(F32)
    outs = []
    for half in range(2):
        at = slice(half * HEAD_DIM, (half + 1) * HEAD_DIM)
        scores = times_transpose(k_ref[:, at], q_ref[:, at]) * 0.125 + mask
        top = jnp.max(scores, axis=0, keepdims=True)
        weights = jnp.exp(scores - top)
        total = jnp.sum(weights, axis=0, keepdims=True)
        outs.append(contract_rows(v_ref[:, at], weights.astype(BF16)) / total)
        logs_ref[0, half : half + 1, :] = top + jnp.log(total)
    out_ref[...] = jnp.transpose(jnp.concatenate(outs, 0))


def attend(query, keys, mask):
    rows, width = query.shape
    tokens = keys.shape[0]
    step = rows if tokens <= 4096 else 128
    pair = 2 * HEAD_DIM
    pairs = width // pair
    spec_q = pl.BlockSpec((step, pair), lambda h, i: (i, h))
    flops = 16 * rows * tokens * width
    return pl.pallas_call(
        attend_kernel,
        out_shape=(shaped((rows, width), F32), shaped((pairs, 8, rows), F32)),
        grid=(pairs, rows // step),
        in_specs=[
            spec_q,
            pl.BlockSpec((tokens, pair), lambda h, i: (0, h)),
            pl.BlockSpec((tokens, pair), lambda h, i: (0, h + pairs)),
            pl.BlockSpec((tokens, 128), lambda h, i: (0, 0)),
        ],
        out_specs=[spec_q, pl.BlockSpec((1, 8, step), lambda h, i: (h, 0, i))],
        cost_estimate=pl.CostEstimate(flops=flops, bytes_accessed=4 * tokens * width, transcendentals=0),
        compiler_params=limit(tokens, 28),
        name="attend",
    )(query, keys, keys, mask)


def attend_back_kernel(
    q_ref, k_ref, v_ref, g_ref, o_ref, logs_ref, mask_ref, dq_ref, dk_ref, dv_ref, bias_ref, dk_sum, dv_sum
):
    step = pl.program_id(0)
    mask = mask_ref[:, :1].astype(F32)

    @pl.when(step == 0)
    def _():
        dk_sum[...] = jnp.zeros_like(dk_sum)
        dv_sum[...] = jnp.zeros_like(dv_sum)

    products = jnp.transpose(g_ref[...].astype(F32) * o_ref[...])
    grads = []
    for half in range(2):
        at = slice(half * HEAD_DIM, (half + 1) * HEAD_DIM)
        query, key, value, grad = q_ref[:, at], k_ref[:, at], v_ref[:, at], g_ref[:, at]
        scores = times_transpose(key, query) * 0.125 + mask
        probs = jnp.exp(scores - logs_ref[0, half : half + 1, :])
        dots = jnp.sum(products[at], axis=0, keepdims=True)
        grad_scores = (probs * (times_transpose(value, grad) - dots)).astype(BF16)
        grads.append(contract_rows(key, grad_scores))
        dk_sum[:, at] += dot(grad_scores, query)
        dv_sum[:, at] += dot(probs.astype(BF16), grad)
    dq_ref[...] = jnp.transpose(jnp.concatenate(grads, 0) * 0.125).astype(BF16)

    @pl.when(step == pl.num_programs(0) - 1)
    def _():
        dk_ref[...] = (dk_sum[...] * 0.125).astype(BF16)
        dv_ref[...] = dv_sum[...].astype(BF16)
        bias_ref[...] = jnp.broadcast_to(columns(dv_sum[...]), bias_ref.shape)


def attend_back(which, query, keys, grad, attended, logs, mask):
    rows, width = query.shape
    tokens = keys.shape[0]
    step = rows if tokens <= 4096 else 128
    pair = 2 * HEAD_DIM
    pairs = width // pair
    single = {"pipeline_mode": pl.Buffered(1)} if tokens > 4096 else {}
    spec_q = pl.BlockSpec((step, pair), lambda i: (i, which))
    spec_dq = pl.BlockSpec((step, pair), lambda i: (i, 0))
    spec_k = pl.BlockSpec((tokens, pair), lambda i: (0, which), **single)
    spec_v = pl.BlockSpec((tokens, pair), lambda i: (0, which + pairs), **single)
    spec_dk = pl.BlockSpec((tokens, pair), lambda i: (0, 0))
    flops = 40 * rows * tokens * pair
    return pl.pallas_call(
        attend_back_kernel,
        out_shape=(
            shaped((rows, pair), BF16),
            shaped((tokens, pair), BF16),
            shaped((tokens, pair), BF16),
            shaped((8, pair), F32),
        ),
        grid=(rows // step,),
        in_specs=[
            spec_q,
            spec_k,
            spec_v,
            spec_q,
            spec_q,
            pl.BlockSpec((1, 8, step), lambda i: (which, 0, i)),
            pl.BlockSpec((tokens, 128), lambda i: (0, 0), **single),
        ],
        out_specs=[spec_dq, spec_dk, spec_dk, pl.BlockSpec((8, pair), lambda i: (0, 0))],
        scratch_shapes=[pltpu.VMEM((tokens, pair), F32), pltpu.VMEM((tokens, pair), F32)],
        cost_estimate=pl.CostEstimate(flops=flops, bytes_accessed=8 * tokens * pair, transcendentals=0),
        compiler_params=limit(tokens, 28),
        name="attend_back",
    )(query, keys, keys, grad, attended, logs, mask)


def keys_inputs_kernel(*refs):
    *part_refs, weight_ref, out_ref = refs
    total = None
    for i, ref in enumerate(part_refs):
        width = ref.shape[1]
        if i % 2:
            continue
        both = jnp.concatenate([ref[...], part_refs[i + 1][...]], axis=1)
        term = times_transpose(both, weight_ref[:, i * width : (i + 2) * width])
        total = term if total is None else total + term
    out_ref[...] = total.astype(BF16)


def keys_inputs(which, parts, weight):
    tokens, pair = parts[0].shape
    tokens //= 2
    width = weight.shape[0]
    step = min(tokens, 512)
    spec = pl.BlockSpec((step, pair), lambda i: (i + which * (tokens // step), 0))
    return pl.pallas_call(
        keys_inputs_kernel,
        out_shape=shaped((tokens, width), BF16),
        grid=(tokens // step,),
        in_specs=[spec] * len(parts) + [pl.BlockSpec(weight.shape, lambda i: (0, 0))],
        out_specs=pl.BlockSpec((step, width), lambda i: (i, 0)),
        cost_estimate=pl.CostEstimate(
            flops=2 * tokens * width * width, bytes_accessed=5 * tokens * width, transcendentals=0
        ),
        compiler_params=limit(tokens, 20),
        name="keys_inputs",
    )(*parts, weight)


def keys_weights_kernel(table_ref, mine_ref, other_ref, q_ref, o_ref, *refs):
    *part_refs, keep_ref, send_ref, sum_ref, held_ref = refs
    first = (pl.program_id(0) == 0) & (pl.program_id(1) == 0)
    last = (pl.program_id(0) == 1) & (pl.program_id(1) == pl.num_programs(1) - 1)
    both = jnp.concatenate([ref[...] for ref in part_refs], axis=1)
    chips, rows, width = held_ref.shape
    half, side = chips // 2, width // 2

    @pl.when(first)
    def _():
        sum_ref[...] = contract_rows(mine_ref[...], both)

    @pl.when((pl.program_id(0) == 0) & (pl.program_id(1) > 0))
    def _():
        sum_ref[...] += contract_rows(mine_ref[...], both)

    @pl.when(pl.program_id(0) == 1)
    def _():
        sum_ref[...] += contract_rows(other_ref[...], both)

    @pl.when(last)
    def _():
        held_ref[...] = sum_ref[...].astype(BF16).reshape(held_ref.shape)

        def body(j, carry):
            for ref, at in ((keep_ref, j), (send_ref, j + half)):
                chip = table_ref[at]
                ref[j, :rows] = held_ref[chip]
                ref[j, rows:, :side] = q_ref[chip]
                ref[j, rows:, side:] = o_ref[chip]
            return carry

        lax.fori_loop(0, half, body, 0)


def flat_keys_weights_kernel(mine_ref, other_ref, *refs):
    *part_refs, grad_ref, sum_ref = refs
    first = (pl.program_id(0) == 0) & (pl.program_id(1) == 0)
    last = (pl.program_id(0) == 1) & (pl.program_id(1) == pl.num_programs(1) - 1)
    both = jnp.concatenate([ref[...] for ref in part_refs], axis=1)

    @pl.when(first)
    def _():
        sum_ref[...] = jnp.zeros_like(sum_ref)

    @pl.when(pl.program_id(0) == 0)
    def _():
        sum_ref[...] += contract_rows(mine_ref[...], both)

    @pl.when(pl.program_id(0) == 1)
    def _():
        sum_ref[...] += contract_rows(other_ref[...], both)

    @pl.when(last)
    def _():
        grad_ref[...] = sum_ref[...].astype(BF16)


def keys_weights(table, mine, other, grad_q, grad_o, parts):
    rows, width = mine.shape
    pair = parts[0].shape[1]
    chips, own = grad_q.shape[:2]
    step = min(rows, 512)
    steps = rows // step
    fused = own % 16 == 0
    block = shaped((chips // 2, 2 * own, width), BF16)
    tokens = [
        pl.BlockSpec((step, width), lambda i, j, *t: (jnp.where(i == 0, j, steps - 1), 0)),
        pl.BlockSpec((step, width), lambda i, j, *t: (jnp.where(i == 0, 0, j), 0)),
    ]
    spec = pl.BlockSpec((step, pair), lambda i, j, *t: (i * steps + j, 0))
    whole = pl.BlockSpec((chips, own, width // 2), lambda i, j, *t: (0, 0, 0))
    blocks = pl.BlockSpec(block.shape, lambda i, j, *t: (0, 0, 0))
    cost = pl.CostEstimate(flops=4 * rows * width * width, bytes_accessed=8 * rows * width, transcendentals=0)
    if fused:
        return pl.pallas_call(
            keys_weights_kernel,
            out_shape=(block, block),
            grid_spec=pltpu.PrefetchScalarGridSpec(
                num_scalar_prefetch=1,
                grid=(2, steps),
                in_specs=tokens + [whole, whole] + [spec] * len(parts),
                out_specs=[blocks, blocks],
                scratch_shapes=[pltpu.VMEM((width, width), F32), pltpu.VMEM((chips, own, width), BF16)],
            ),
            cost_estimate=cost,
            compiler_params=limit(2 * rows, 24),
            name="keys_weights",
        )(table, mine, other, grad_q, grad_o, *parts)
    grad = pl.pallas_call(
        flat_keys_weights_kernel,
        out_shape=shaped((width, width), BF16),
        grid=(2, steps),
        in_specs=tokens + [spec] * len(parts),
        out_specs=pl.BlockSpec((width, width), lambda i, j: (0, 0)),
        scratch_shapes=[pltpu.VMEM((width, width), F32)],
        cost_estimate=cost,
        name="keys_weights",
    )(mine, other, *parts)
    return call(
        split_attention_kernel,
        "split_attention",
        (block, block),
        table,
        grad.reshape(chips, own, width),
        grad_q,
        grad_o,
        scalars=1,
        moved=8 * width * width,
    )


def normalize(values):
    center = values - jnp.mean(values, axis=-1, keepdims=True)
    scale = lax.rsqrt(jnp.mean(center * center, axis=-1, keepdims=True) + EPSILON)
    return center * scale, scale


def normalize_back(grad, normal, scale):
    return scale * (
        grad
        - jnp.mean(grad, axis=-1, keepdims=True)
        - normal * jnp.mean(grad * normal, axis=-1, keepdims=True)
    )


def row(ref, which):
    return ref[which : which + 1, :].astype(F32)


def columns(values):
    return jnp.sum(values, axis=0, keepdims=True)


def output_kernel(
    core_ref, inputs_ref, mine_ref, other_ref, near_ref, far_ref, vector_ref, normal_ref, scale_ref, low_ref
):
    side = mine_ref.shape[1]
    core = core_ref[0]
    here, there = pl.ds(core * side, side), pl.ds((1 - core) * side, side)

    def product(ref):
        return dot(mine_ref[...], ref[here, :]) + dot(other_ref[...], ref[there, :])

    near, far = product(near_ref), product(far_ref)
    even = core == 0
    hidden = jnp.concatenate([jnp.where(even, near, far), jnp.where(even, far, near)], axis=1)
    hidden = inputs_ref[...].astype(F32) + hidden + row(vector_ref, OUTPUT_B)
    normal, scale = normalize(hidden)
    normal_ref[...] = normal
    scale_ref[...] = jnp.broadcast_to(scale, scale_ref.shape)
    low_ref[...] = (normal * row(vector_ref, GAIN_1) + row(vector_ref, SHIFT_1)).astype(BF16)


def hidden_kernel(mine_ref, other_ref, expand_ref, reduce_ref, bias_ref, active_ref, slope_ref, near_ref, far_ref):
    rows = mine_ref.shape[0]
    width = mine_ref.shape[1]
    both = jnp.concatenate([mine_ref[...], other_ref[...]], axis=0)
    total = None
    for i in range(expand_ref.shape[1] // width):
        at = slice(i * width, (i + 1) * width)
        value = dot(both, expand_ref[:, at]) + row(bias_ref, EXPAND_B + 0 + i)
        normal = 0.5 + 0.5 * lax.erf(value * np.float32(0.7071067811865476))
        active = (value * normal).astype(BF16)
        active_ref[:, at] = active
        density = jnp.exp(value * value * -0.5) * np.float32(0.3989422804014327)
        slope_ref[:, at] = normal + value * density
        term = dot(active, reduce_ref[at, :])
        total = term if total is None else total + term
    near_ref[...] = total[:rows]
    far_ref[...] = total[rows:]


def final_kernel(
    start_ref, normal_one_ref, near_ref, far_ref, cotangent_ref, vector_ref, out_ref, grad_ref, low_ref, sums_ref
):
    middle = normal_one_ref[...] * row(vector_ref, GAIN_1) + row(vector_ref, SHIFT_1)
    combined = middle + near_ref[...] + far_ref[...] + row(vector_ref, REDUCE_B)
    normal, scale = normalize(combined)
    gain = row(vector_ref, GAIN_2)
    out_ref[...] = (normal * gain + row(vector_ref, SHIFT_2)).astype(BF16)
    place = start_ref[0] + lax.broadcasted_iota(jnp.int32, combined.shape, 0)
    upstream = jnp.where(place < start_ref[1], cotangent_ref[...].astype(F32), 0.0)
    grad = normalize_back(upstream * gain, normal, scale)
    grad_ref[...] = grad
    low_ref[...] = grad.astype(BF16)
    sums_ref[...] = jnp.zeros_like(sums_ref)
    sums_ref[REDUCE_B : REDUCE_B + 1, :] = columns(grad)
    sums_ref[GAIN_2 : GAIN_2 + 1, :] = columns(upstream * normal)
    sums_ref[SHIFT_2 : SHIFT_2 + 1, :] = columns(upstream)


def hidden_back_kernel(mine_ref, other_ref, expand_ref, reduce_ref, slope_ref, low_ref, near_ref, far_ref, sums_ref):
    rows, width = mine_ref.shape
    both = jnp.concatenate([mine_ref[...], other_ref[...]], axis=0)
    total = None
    sums_ref[...] = jnp.zeros_like(sums_ref)
    for i in range(expand_ref.shape[1] // width):
        at = slice(i * width, (i + 1) * width)
        active = times_transpose(both, reduce_ref[at, :]).astype(BF16)
        grad = (active.astype(F32) * slope_ref[:, at]).astype(BF16)
        low_ref[:, at] = grad
        sums_ref[i : i + 1, :] = columns(grad.astype(F32))
        term = times_transpose(grad, expand_ref[:, at])
        total = term if total is None else total + term
    near_ref[...] = total[:rows]
    far_ref[...] = total[rows:]


def reduce_grads_kernel(table_ref, low_mine_ref, low_other_ref, active_ref, *refs):
    width = low_mine_ref.shape[1]
    low = jnp.concatenate([low_mine_ref[...], low_other_ref[...]], axis=0)
    held = refs[-1]
    chips, rows = held.shape[0], held.shape[1]
    for i in range(active_ref.shape[1] // width):
        part = contract_rows(active_ref[:, i * width : (i + 1) * width], low).astype(BF16)
        if len(refs) == 3:
            held[i * width // rows : (i + 1) * width // rows] = part.reshape(width // rows, rows, width)
        else:
            held[i * width : (i + 1) * width, :] = part
    if len(refs) == 3:
        split_reduce_kernel(table_ref, held, refs[0], refs[1])


def expand_grads_kernel(table_ref, mid_mine_ref, mid_other_ref, low_ref, *refs):
    width = mid_mine_ref.shape[1]
    mid = jnp.concatenate([mid_mine_ref[...], mid_other_ref[...]], axis=0)
    held = refs[-1]
    chips, rows = held.shape[0], held.shape[1]
    for i in range(low_ref.shape[1] // width):
        at = slice(i * width, (i + 1) * width)
        part = contract_rows(mid, low_ref[:, at]).astype(BF16)
        if len(refs) == 3:
            held[:, :, at] = part.reshape(width // rows, rows, width)
        else:
            held[:, at] = part
    if len(refs) == 3:
        split_expand_kernel(table_ref, held, refs[0], refs[1])


def output_back_kernel(
    core_ref, normal_ref, scale_ref, grad_ref, near_sum_ref, far_sum_ref, near_ref, far_ref, vector_ref,
    hidden_ref, low_ref, mine_ref, other_ref, sums_ref,
):
    side = near_ref.shape[1]
    core = core_ref[0]
    even = core == 0
    normal = normal_ref[...]
    grad_middle = grad_ref[...] + near_sum_ref[...] + far_sum_ref[...]
    grad = normalize_back(grad_middle * row(vector_ref, GAIN_1), normal, scale_ref[:, :1])
    hidden_ref[...] = grad
    low = grad.astype(BF16)
    low_ref[...] = low
    low_near = jnp.where(even, low[:, :side], low[:, side:])
    low_far = jnp.where(even, low[:, side:], low[:, :side])
    here, there = pl.ds(core * side, side), pl.ds((1 - core) * side, side)

    def product(rows):
        return times_transpose(low_near, near_ref[rows, :]) + times_transpose(low_far, far_ref[rows, :])

    mine_ref[...] = product(here).astype(BF16)
    other_ref[...] = product(there).astype(BF16)
    sums_ref[...] = jnp.zeros_like(sums_ref)
    sums_ref[OUTPUT_B : OUTPUT_B + 1, :] = columns(grad)
    sums_ref[GAIN_1 : GAIN_1 + 1, :] = columns(grad_middle * normal)
    sums_ref[SHIFT_1 : SHIFT_1 + 1, :] = columns(grad_middle)


def output_grads_kernel(core_ref, mine_ref, other_ref, low_ref, near_ref, far_ref):
    side = mine_ref.shape[1]
    core = core_ref[0]
    even = core == 0
    here, there = pl.ds(core * side, side), pl.ds((1 - core) * side, side)
    for rows, ref in ((here, mine_ref), (there, other_ref)):
        product = contract_rows(ref[...], low_ref[...])
        near_ref[rows, :] = jnp.where(even, product[:, :side], product[:, side:])
        far_ref[rows, :] = jnp.where(even, product[:, side:], product[:, :side]).astype(BF16)


def query_back_kernel(mine_ref, other_ref, weight_ref, *refs):
    *dq_refs, near_ref, far_ref, grad_ref, sums_ref = refs
    rows = mine_ref.shape[0]
    grads = jnp.concatenate([ref[...] for ref in dq_refs], axis=1)
    product = times_transpose(grads, weight_ref[...])
    near_ref[...] = product[:rows]
    far_ref[...] = product[rows:]
    both = jnp.concatenate([mine_ref[...], other_ref[...]], axis=0)
    grad_ref[...] = contract_rows(both, grads).astype(BF16)
    sums_ref[...] = jnp.broadcast_to(columns(grads.astype(F32)), sums_ref.shape)


def body(
    layer_input,
    cotangent,
    lengths,
    query_weight,
    query_bias,
    key_weight,
    value_weight,
    value_bias,
    output_weight,
    output_bias,
    attn_gain,
    attn_shift,
    expand_weight,
    expand_bias,
    reduce_weight,
    reduce_bias,
    final_gain,
    final_shift,
):
    place = Place()
    core = place.core
    core_s = core.reshape(1)
    number_s = place.number.reshape(1)
    chips = place.count // 2
    inputs = layer_input[0]
    rows, width = inputs.shape
    side = width // 2
    own = query_weight.shape[0]
    units = reduce_weight.shape[0]
    hidden_units = units * chips
    times = hidden_units // width
    length = lengths[0]
    even = core == 0

    masks = [place.others(place.weight_stages, k) for k in range(2)]
    table = (place.number ^ jnp.where(even, masks[0], masks[1])) // 2
    token_masks = [place.others(place.token_stages, k) for k in range(2)]
    near_ctx = place.context ^ jnp.where(even, token_masks[0], token_masks[1])
    far_ctx = (place.context ^ 1) ^ jnp.where(even, token_masks[1], token_masks[0])
    blocks = jnp.concatenate([near_ctx, far_ctx])
    positions = (blocks[:, None] * rows + jnp.arange(rows, dtype=jnp.int32)).reshape(-1, 1)
    mask = jnp.broadcast_to(jnp.where(positions < length, 0.0, MASKED).astype(BF16), (positions.shape[0], 128))

    def halves(weight, which):
        return jnp.where(which == 0, weight[:, :side], weight[:, side:])

    def attention_part(which):
        k, v, q, o = (halves(w, which) for w in (key_weight, value_weight, query_weight, output_weight))
        return jnp.stack([jnp.concatenate([k, v], 1), jnp.concatenate([q, o], 1)])

    expand4 = expand_weight.reshape(own, chips, 2, units)

    def expand_part(which):
        part = jnp.where(which == 0, expand4[:, :, 0], expand4[:, :, 1]).reshape(own, hidden_units)
        return jnp.stack([part[:, i * width : (i + 1) * width] for i in range(times)])

    def joined(mine, other):
        return jnp.where(
            even, jnp.concatenate([mine, other], 1), jnp.concatenate([other, mine], 1)
        ).reshape(-1, width)

    vector_list = [query_bias, value_bias, output_bias, attn_gain, attn_shift, reduce_bias, final_gain, final_shift]
    vectors = call(
        pack_vectors_kernel,
        "pack_vectors",
        shaped((VECTOR_ROWS, width), BF16),
        number_s,
        *[v.reshape(1, own) for v in vector_list],
        expand_bias.reshape(1, units),
        scalars=1,
        held=False,
        scratch=[pltpu.VMEM((VECTOR_ROWS, width), F32)],
    )
    vector_swap = place.swap(vectors, 0)
    vectors = vectors + jnp.where(jnp.arange(VECTOR_ROWS)[:, None] < 8, vector_swap, 0)

    stages = place.weight_stages
    token_stages = place.token_stages

    def swap(stage, array, *earlier):
        return place.swap(after(array, *earlier) if earlier else array, *stage)

    def grow(held, got):
        return jnp.concatenate([held, got])

    other_inputs = place.swap(inputs, 0)
    b_held = joined(attention_part(core), place.swap(attention_part(1 - core), 0))
    a_held = joined(expand_part(core), place.swap(expand_part(1 - core), 0))[None]
    d_held = reduce_weight[None]
    x_held = inputs[None]
    block_rows = b_held.shape[0]
    last = len(stages) - 1
    b_gots, x_gots, a_gots, d_gots = [], [], [], []
    for at in range(last + 1):
        b_gots.append(swap(stages[at], jnp.concatenate([b_held, vectors])))
        vectors = vectors + b_gots[-1][-VECTOR_ROWS:]
        if at < len(token_stages):
            if at:
                x_held = grow(x_held, x_gots[-1])
            x_gots.append(swap(token_stages[at], x_held, *b_gots[at - 1 : at] if at else ()))
        if at < last:
            b_held = grow(b_held, b_gots[-1][:-VECTOR_ROWS])
    for at in range(last - 1):
        if at:
            a_held = grow(a_held, after(a_gots[-1], b_gots[at]))
            d_held = grow(d_held, after(d_gots[-1], a_gots[-1], b_gots[at + 1]))
        a_gots.append(swap(stages[at], a_held, *b_gots[at : at + 1] if at else ()))
        d_gots.append(swap(stages[at], d_held, a_gots[-1]))
    a_held = grow(a_held, after(a_gots[-1], b_gots[last - 1]))
    a_gots.append(swap(stages[last - 1], a_held))

    aligned = (2 * own) % 16 == 0
    tile = 16 if aligned else 2 * own

    def tiles(array):
        array = array if aligned else array[: array.shape[0] // block_rows * block_rows]
        return array.reshape(-1, tile, width)

    weights_kv, weights_q, output_near, bias = call(
        place_attention_kernel,
        "place_attention",
        (
            shaped((chips, 2 * own, width), BF16),
            shaped((chips, 2 * own, side), BF16),
            shaped((chips, 2 * own, side), BF16),
            shaped((8, 3 * side), F32),
        ),
        table,
        core_s,
        tiles(b_held),
        tiles(b_gots[-1]),
        vectors,
        scalars=2,
        moved=8 * width * width,
    )
    weights_kv = weights_kv.reshape(width, width)
    weights_q = weights_q.reshape(width, side)
    output_near = output_near.reshape(width, side)
    sequence_near = grow(x_held, x_gots[-1]).reshape(-1, width)
    sequence_far = place.swap(sequence_near, 0)
    keys = project(sequence_near, sequence_far, weights_kv, bias)
    a_held = grow(a_held, after(a_gots[-1], weights_kv))
    a_gots.append(swap(stages[last], a_held))
    d_held = grow(d_held, after(d_gots[-1], weights_kv))
    d_gots.append(swap(stages[last - 1], d_held))
    d_held = grow(d_held, after(d_gots[-1], keys))
    d_got = swap(stages[last], d_held)
    query = jnp.concatenate([inputs, other_inputs])
    query = (dot(query, weights_q) + bias[:1, 2 * side :]).astype(BF16)
    attended, logs = attend(query, keys, mask)
    output_far = place.swap(output_near, 0)
    expand_matrix = call(
        place_expand_kernel,
        "place_expand",
        shaped((chips, 2 * own, hidden_units), BF16),
        table,
        a_held,
        a_gots[-1],
        scalars=1,
        moved=4 * hidden_units * width,
    ).reshape(width, hidden_units)
    reduce_matrix = call(
        place_reduce_kernel,
        "place_reduce",
        shaped((chips, units, width), BF16),
        table,
        d_held,
        d_got,
        scalars=1,
        moved=4 * hidden_units * width,
    ).reshape(hidden_units, width)
    attended_low = attended.astype(BF16)
    attended_mine = attended_low[:rows]
    attended_other = place.swap(attended_low[rows:], 0)

    normal_one, scale_one, middle_low = call(
        output_kernel,
        "output",
        (shaped((rows, width), F32), shaped((rows, 128), F32), shaped((rows, width), BF16)),
        core_s,
        after(inputs, expand_matrix),
        attended_mine,
        attended_other,
        output_near,
        output_far,
        vectors,
        scalars=1,
        flops=2 * rows * width * width,
        moved=4 * width * width,
    )

    middle_other = place.swap(middle_low, 0)
    active, slope, near, far = call(
        hidden_kernel,
        "hidden",
        (
            shaped((2 * rows, hidden_units), BF16),
            shaped((2 * rows, hidden_units), F32),
            shaped((rows, width), F32),
            shaped((rows, width), F32),
        ),
        middle_low,
        middle_other,
        expand_matrix,
        reduce_matrix,
        vectors,
        flops=8 * rows * width * hidden_units,
        moved=4 * width * hidden_units,
    )
    far = place.swap(far, 0)
    start_s = jnp.stack([place.context * rows, length])
    layer_output, grad_combined, combined_low, sums_two = call(
        final_kernel,
        "final",
        (
            shaped((rows, width), BF16),
            shaped((rows, width), F32),
            shaped((rows, width), BF16),
            shaped((8, width), F32),
        ),
        start_s,
        normal_one,
        near,
        far,
        cotangent[0],
        vectors,
        scalars=1,
        moved=12 * rows * width,
    )
    combined_other = place.swap(combined_low, 0)
    grad_expanded, near, far, sums_expand = call(
        hidden_back_kernel,
        "hidden_back",
        (
            shaped((2 * rows, hidden_units), BF16),
            shaped((rows, width), F32),
            shaped((rows, width), F32),
            shaped((8, width), F32),
        ),
        combined_low,
        combined_other,
        expand_matrix,
        reduce_matrix,
        slope,
        flops=8 * rows * width * hidden_units,
        moved=4 * width * hidden_units,
    )
    far = place.swap(far, 0)
    def weight_grads(kernel, split, name, shape, blocks, *args):
        out = (shaped((chips // 2,) + blocks, BF16),) * 2
        cost = dict(flops=4 * rows * width * hidden_units, moved=6 * width * hidden_units)
        if (2 * own) % 16 == 0:
            rows_each = shape[0] // chips
            scratch = [pltpu.VMEM((chips, rows_each, shape[1]), BF16)]
            return call(kernel, name, out, table, *args, scalars=1, scratch=scratch, **cost)
        flat = call(kernel, name, shaped(shape, BF16), table, *args, scalars=1, **cost)
        return call(split, name + "_split", out, table, flat.reshape(chips, -1, shape[1]), scalars=1, **cost)

    reduce_keep, reduce_send = weight_grads(
        reduce_grads_kernel,
        split_reduce_kernel,
        "reduce_grads",
        (hidden_units, width),
        (units, width),
        combined_low,
        combined_other,
        active,
    )
    expand_keep, expand_send = weight_grads(
        expand_grads_kernel,
        split_expand_kernel,
        "expand_grads",
        (width, hidden_units),
        (times * 2 * own, width),
        middle_low,
        middle_other,
        grad_expanded,
    )

    grad_hidden, hidden_low, grad_mine, grad_other, sums_one = call(
        output_back_kernel,
        "output_back",
        (
            shaped((rows, width), F32),
            shaped((rows, width), BF16),
            shaped((rows, side), BF16),
            shaped((rows, side), BF16),
            shaped((8, width), F32),
        ),
        core_s,
        normal_one,
        scale_one,
        grad_combined,
        near,
        far,
        output_near,
        output_far,
        vectors,
        scalars=1,
        flops=2 * rows * width * width,
        moved=4 * width * width,
    )
    grad_heads = jnp.concatenate([grad_mine, place.swap(grad_other, 0)])
    output_near_grad, output_far_grad = call(
        output_grads_kernel,
        "output_grads",
        (shaped((width, side), F32), shaped((width, side), BF16)),
        core_s,
        attended_mine,
        attended_other,
        hidden_low,
        scalars=1,
        flops=2 * rows * width * width,
        moved=4 * width * width,
    )
    grad_output = (output_near_grad + place.swap(output_far_grad, 0).astype(F32)).astype(BF16)

    back = place.weight_stages[::-1]

    def own_half(array, axis):
        first, second = lax.index_in_dim(array, 0, axis, False), lax.index_in_dim(array, 1, axis, False)
        return jnp.where(even, first, second), jnp.where(even, second, first)

    d_keep, d_send = reduce_keep, reduce_send
    a_keep, a_send = expand_keep, expand_send
    done = len(back) - 1
    d_at = a_at = 0

    def d_start():
        return swap(back[d_at], d_send)

    def a_start():
        return swap(back[a_at], a_send)

    def d_end(got, *earlier):
        nonlocal d_keep, d_send, d_at
        out = fold(d_keep, after(got, *earlier) if earlier else got)
        d_keep, d_send = (out, None) if d_at == done else out
        d_at += 1
        return d_start() if d_at <= done else None

    def a_end(got, *earlier):
        nonlocal a_keep, a_send, a_at
        out = fold(a_keep, after(got, *earlier) if earlier else got)
        a_keep, a_send = (out, None) if a_at == done else out
        a_at += 1
        return a_start() if a_at <= done else None

    d_got, a_got = d_start(), a_start()
    first_got = d_got
    parts = []
    pairs = side // (2 * HEAD_DIM)
    for which in range(pairs):
        pinned = after(query, first_got) if which else query
        parts.append(attend_back(which, pinned, keys, grad_heads, attended, logs, mask))
    d_got = d_end(d_got)
    grad_query, grad_keys, grad_values, value_bias_sums = zip(*parts)
    parts = grad_keys + grad_values
    far_part = keys_inputs(1, parts, weights_kv)
    far_got = place.swap(far_part, 0)
    near_part = keys_inputs(0, parts, weights_kv)
    tokens = sequence_near.shape[0]
    blocks_shape = (tokens // rows, rows, width)
    x_keep, x_send = fold(near_part.reshape(blocks_shape), far_got.reshape(blocks_shape))
    first_got = a_got
    a_got = a_end(a_got, far_part)
    near, far, grad_query_w, query_bias_sum = call(
        query_back_kernel,
        "query_back",
        (
            shaped((rows, width), F32),
            shaped((rows, width), F32),
            shaped((width, side), BF16),
            shaped((8, side), F32),
        ),
        inputs,
        other_inputs,
        weights_q,
        *grad_query,
        flops=8 * rows * width * side,
        moved=6 * width * width,
    )
    query_part = grad_hidden + near + place.swap(far, 0)

    mine_rows = jnp.stack([query_bias_sum[0], jnp.concatenate([v[0] for v in value_bias_sums])])
    zero = jnp.zeros_like(mine_rows)
    mine_rows = jnp.where(even, jnp.concatenate([mine_rows, zero], 1), jnp.concatenate([zero, mine_rows], 1))
    vector_sums = jnp.concatenate([mine_rows, (sums_one + sums_two)[2:], sums_expand])
    vector_swap = place.swap(vector_sums, 0)
    vector_sums = vector_sums + jnp.where(jnp.arange(VECTOR_ROWS)[:, None] < 8, vector_swap, 0)

    keep, send = keys_weights(
        table,
        after(sequence_near, first_got, x_send),
        sequence_far,
        grad_query_w.reshape(chips, 2 * own, side),
        grad_output.reshape(chips, 2 * own, side),
        parts,
    )
    keep = keep.reshape(-1, width)
    send = jnp.concatenate([send.reshape(-1, width), vector_sums.astype(BF16)])
    token_back = token_stages[::-1]
    x_count, count = len(token_back), len(back)
    d_got = d_end(d_got, keep)
    a_got = a_end(a_got, keep)
    for at in range(count):
        x_got = ()
        if at < x_count:
            x_got = (swap(token_back[at], x_send),)
            x_keep = fold(x_keep, x_got[0])
            if at + 1 < x_count:
                x_keep, x_send = x_keep
        b_got = swap(back[at], send)
        if d_at <= done:
            d_got = d_end(d_got, *x_got)
        if a_at <= done:
            a_got = a_end(a_got, *x_got, b_got)
        if at + 1 < count:
            keep, send, vector_sums = fold_vectors(keep, b_got, vector_sums, False)
        else:
            keep, vector_sums = fold_vectors(keep, b_got, vector_sums, True)
    reduce_out = d_keep
    expand_sum = a_keep.reshape(times, 2, own, width)
    input_grad = query_part + x_keep

    expand_mine, expand_other = own_half(expand_sum, 1)
    expand_other = place.swap(expand_other, 0)

    def unit_order(array):
        return jnp.concatenate([array[i] for i in range(times)], 1).reshape(own, chips, units)

    expand_mine, expand_other = unit_order(expand_mine), unit_order(expand_other)
    expand_out = jnp.stack(
        [jnp.where(even, expand_mine, expand_other), jnp.where(even, expand_other, expand_mine)], 2
    ).reshape(own, 2 * hidden_units)

    pieces = keep.reshape(2, 2, own, width)
    pieces_mine, pieces_other = own_half(pieces, 1)
    pieces_other = place.swap(pieces_other, 0)

    def weight_out(pair, second):
        at = slice(side, None) if second else slice(0, side)
        a, b = pieces_mine[pair, :, at], pieces_other[pair, :, at]
        return jnp.concatenate([jnp.where(even, a, b), jnp.where(even, b, a)], 1)

    outs = call(
        unpack_vectors_kernel,
        "unpack_vectors",
        [shaped((1, own), F32)] * 8 + [shaped((1, units), F32)],
        number_s,
        vector_sums,
        scalars=1,
        held=False,
    )
    outs = [v.reshape(-1) for v in outs]
    return (
        layer_output[None],
        input_grad[None],
        weight_out(1, False),
        outs[QUERY_B],
        weight_out(0, False),
        weight_out(0, True),
        outs[VALUE_B],
        weight_out(1, True),
        outs[OUTPUT_B],
        outs[GAIN_1],
        outs[SHIFT_1],
        expand_out,
        outs[EXPAND_B],
        reduce_out,
        outs[REDUCE_B],
        outs[GAIN_2],
        outs[SHIFT_2],
    )


def solution(mesh):
    tokens = P("seq", "ctx", None)
    matrix = P(("seq", "ctx"), None)
    vector = P(("seq", "ctx"))
    weights = (
        matrix,
        vector,
        matrix,
        matrix,
        vector,
        matrix,
        vector,
        vector,
        vector,
        matrix,
        vector,
        matrix,
        vector,
        vector,
        vector,
    )
    return jax.shard_map(
        body,
        mesh=mesh,
        in_specs=(tokens, tokens, P("seq")) + weights,
        out_specs=(tokens, tokens) + weights,
        check_vma=False,
    )
```

```python
import functools

import jax
import jax.numpy as jnp
import numpy as np
from jax import lax
from jax.experimental import pallas as pl
from jax.experimental.pallas import tpu as pltpu
from jax.sharding import PartitionSpec as P

HEADS = 12
HEAD_DIM = 64
EPSILON = 1e-12
MASKED = -1000000000.0
EVERY = ("seq", "ctx")
F32 = jnp.float32
BF16 = jnp.bfloat16
VMEM = pl.BlockSpec(memory_space=pltpu.VMEM)
SMEM = pl.BlockSpec(memory_space=pltpu.SMEM)
QUERY_B, VALUE_B, OUTPUT_B, GAIN_1, SHIFT_1, REDUCE_B, GAIN_2, SHIFT_2, EXPAND_B = range(9)
VECTOR_ROWS = 16
SMALL_BYTES = 16 << 20
COST = pl.CostEstimate(flops=1000, bytes_accessed=1000, transcendentals=0)
FORWARD = ('XBADbxad|BAba|BADXbadx|BDXbd|', 'xAD', '', 'ad|')
BACKWARD = ('', '', 'a|A', 'da|DX', 'BA|dab|DABx|aXdbBDxd|Xb|Bx|b')
TOKEN_NEAR = 0
TOKEN_TURN = 'yba'
WEIGHT_TURNS = {'D': (1, 0, 3, 2), 'A': (3, 2, 1, 0), 'B': (3, 2, 1, 0)}
WAITS = (False, False, False, False, False, False)
FIRST_WAITS = False
INPUTS_FIRST = False
STRICT = (True, False)


def dot(left, right):
    return jnp.dot(left, right, preferred_element_type=F32)


def contract_rows(left, right):
    return lax.dot_general(left, right, (((0,), (0,)), ((), ())), preferred_element_type=F32)


def times_transpose(left, right):
    return lax.dot_general(left, right, (((1,), (1,)), ((), ())), preferred_element_type=F32)


def shaped(shape, dtype):
    return jax.ShapeDtypeStruct(tuple(shape), dtype)


def after(array, *earlier):
    return lax.optimization_barrier((array, *earlier))[0]


def in_hbm(array):
    return pltpu.with_memory_space_constraint(array, pltpu.HBM)


class Far:
    def __init__(self, array):
        self.array = array


def fetching(kernel, scalars, far, count, *refs):
    inputs, rest = list(refs[:count]), refs[count : len(refs) - len(far) - 1]
    held, sems = refs[len(refs) - len(far) - 1 : -1], refs[-1]
    copies = [pltpu.make_async_copy(inputs[at], room, sems.at[i]) for i, (at, room) in enumerate(zip(far, held))]
    for copy in copies:
        copy.start()
    for copy in copies:
        copy.wait()
    for at, room in zip(far, held):
        inputs[at] = room
    kernel(*inputs, *rest)


def call(kernel, name, outs, *args, scalars=0, scratch=(), room=16, stored=()):
    many = isinstance(outs, (tuple, list))
    far = [i for i, a in enumerate(args) if isinstance(a, Far)]
    args = [a.array if isinstance(a, Far) else a for a in args]
    flat = tuple(outs) if many else (outs,)
    small = sum(a.size * a.dtype.itemsize for a in (*args, *flat)) < SMALL_BYTES
    specs = [SMEM] * scalars + [VMEM] * (len(args) - scalars)
    scratch = list(scratch)
    if far and small:
        kernel = functools.partial(fetching, kernel, scalars, far, len(args))
        for at in far:
            specs[at] = pl.BlockSpec(memory_space=pltpu.HBM)
            args[at] = pltpu.with_memory_space_constraint(args[at], pltpu.HBM)
            scratch.append(pltpu.VMEM(args[at].shape, args[at].dtype))
        scratch.append(pltpu.SemaphoreType.DMA((len(far),)))
    out_specs = [VMEM] * len(flat)
    for at in stored:
        out_specs[at] = pl.BlockSpec(memory_space=pltpu.HBM)
        flat = flat[:at] + (pltpu.HBM(flat[at].shape, flat[at].dtype),) + flat[at + 1 :]
    return pl.pallas_call(
        kernel,
        out_shape=flat if many else flat[0],
        in_specs=specs,
        out_specs=tuple(out_specs) if many else out_specs[0],
        scratch_shapes=scratch,
        cost_estimate=COST,
        compiler_params=pltpu.CompilerParams(vmem_limit_bytes=room << 20 if small else None),
        name=name,
    )(*args)


def limit(tokens, mebibytes):
    return pltpu.CompilerParams(vmem_limit_bytes=mebibytes << 20 if tokens <= 4096 else None)


class Place:
    def __init__(self):
        self.ctx = lax.axis_size("ctx")
        self.count = lax.axis_size("seq") * self.ctx
        self.bits = self.count.bit_length() - 1
        self.context = lax.axis_index("ctx")
        self.number = lax.axis_index("seq") * self.ctx + self.context
        self.core = self.number & 1
        top = self.bits - 1
        middle = list(range(2, top))
        self.weight_stages = list(zip(middle[::-1], middle)) + [(1, top), (top, 1)]
        self.token_stages = list(zip(middle[::-1], middle))
        self.token_stages.insert(min(TOKEN_NEAR, len(middle)), (1, 1))

    def swap(self, array, even, odd=None):
        odd = even if odd is None else odd
        pairs = [(i, i ^ (1 << (odd if i & 1 else even))) for i in range(self.count)]
        return lax.ppermute(array, EVERY, pairs)

    def others(self, stages, core):
        masks = [0]
        for stage in stages:
            masks = masks + [m ^ (1 << stage[core]) for m in masks]
        return np.array(masks, np.int32)


class Order:
    def __init__(self, place, strict):
        self.place = place
        self.strict = strict
        self.last = ()
        self.ended = ()

    def close(self):
        if self.ended:
            self.last, self.ended = self.ended, ()

    def wait(self, array):
        return after(array, *self.last) if self.last else array

    def start(self, array, stage):
        return self.place.swap(self.wait(array), *stage)

    def done(self, got):
        used = self.wait(got) if self.strict else got
        self.ended += (got,)
        return used

    def ran(self, out):
        self.ended += (out,)
        return out


class Gather:
    def __init__(self, order, blocks, stages, vectors=None):
        self.order, self.held, self.stages, self.vectors = order, blocks, list(stages), vectors
        self.got = None

    def start(self):
        sent = self.held if self.vectors is None else jnp.concatenate([self.held, self.vectors])
        self.got = self.order.start(sent, self.stages.pop(0))

    def done(self):
        self.got = self.order.done(self.got)
        got = self.got
        if self.vectors is not None:
            self.vectors = self.vectors + got[-VECTOR_ROWS:]
            got = got[:-VECTOR_ROWS]
        if self.stages:
            self.held = jnp.concatenate([self.held, got])


class Scatter:
    def __init__(self, order, keep, send, stages, vectors=None, turn=None):
        self.order, self.keep, self.send, self.vectors = order, keep, send, vectors
        turn = list(range(len(stages)))[::-1] if turn is None else list(turn)
        self.stages = [stages[i] for i in turn]
        left = sorted(turn)
        self.bits = []
        for i in turn:
            self.bits.append(left.index(i))
            left.remove(i)
        self.bits.pop(0)

    def start(self):
        self.got = self.order.start(self.send, self.stages.pop(0))

    def done(self, *earlier):
        got = self.order.done(self.got)
        got = after(got, *earlier) if earlier else got
        last = not self.stages
        if self.vectors is None:
            out = fold(self.keep, got, None if last else self.bits.pop(0))
            self.keep, self.send = (out, None) if last else out
        elif last:
            self.keep, self.vectors = fold_vectors(self.keep, got, self.vectors, None)
        else:
            bit = (self.bits.pop(0), 2 << len(self.bits))
            self.keep, self.send, self.vectors = fold_vectors(self.keep, got, self.vectors, bit)


def play(events, chains):
    for event in events:
        if event == "|":
            next(iter(chains.values())).order.close()
            continue
        chain = chains[event.upper()]
        if event.isupper():
            chain.start()
        else:
            chain.done()


def plain_events(chains):
    events = ""
    left = {name: len(chain.stages) for name, chain in chains.items()}
    while any(left.values()):
        names = [n for n in left if left[n]]
        events += "".join(names) + "".join(names).lower() + "|"
        for n in names:
            left[n] -= 1
    return events


def prepare_kernel(units, number_ref, *refs):
    count = EXPAND_B + 6
    in_refs, outs = refs[:count], refs[count : count + 5]
    rows_ref, split_ref = refs[count + 5 : count + 7]
    held_refs, sems = refs[count + 7 : -1], refs[-1]
    copies = [pltpu.make_async_copy(i, h, sems.at[at]) for at, (i, h) in enumerate(zip(in_refs, held_refs))]
    for copy in copies:
        copy.start()
    key_mine_ref, key_other_ref, expand_mine_ref, expand_other_ref, vectors_ref = outs
    number = number_ref[0]
    even = number % 2 == 0
    rows_ref[...] = jnp.zeros_like(rows_ref)
    for copy in copies:
        copy.wait()
    weights, expand_ref, vectors = held_refs[:4], held_refs[4], held_refs[5:]
    own, width = weights[0].shape
    side = width // 2
    for i, ref in enumerate(weights):
        first, second = ref[:, :side], ref[:, side:]
        at = slice(i % 2 * side, (i % 2 + 1) * side)
        key_mine_ref[i // 2, :, at] = jnp.where(even, first, second)
        key_other_ref[i // 2, :, at] = jnp.where(even, second, first)
    for i in range(expand_ref.shape[1] // units):
        at = i // 2 * units
        split_ref[i % 2, :, at : at + units] = expand_ref[:, i * units : (i + 1) * units].astype(F32)
    for i in range(expand_mine_ref.shape[0]):
        at = slice(i * width, (i + 1) * width)
        first, second = split_ref[0, :, at], split_ref[1, :, at]
        expand_mine_ref[i] = jnp.where(even, first, second).astype(BF16)
        expand_other_ref[i] = jnp.where(even, second, first).astype(BF16)
    for i, ref in enumerate(vectors[:-1]):
        rows_ref[i : i + 1, :own] = ref[...].astype(F32)
    rows_ref[EXPAND_B : EXPAND_B + 1, :units] = vectors[-1][...].astype(F32)
    first = pltpu.roll(rows_ref[:8, :], number * own, 1)
    offset = (number // 2) * units
    second = pltpu.roll(rows_ref[8:, :], offset % width, 1)
    here = lax.broadcasted_iota(jnp.int32, second.shape, 0) == offset // width
    second = jnp.where(here, jnp.broadcast_to(second[:1], second.shape), 0.0)
    vectors_ref[...] = jnp.concatenate([first, second], 0).astype(BF16)


def prepare(number, weights, expand, vectors):
    own, width = weights[0].shape
    units = vectors[-1].shape[0]
    arrays = [*weights, expand, *[v.reshape(1, -1) for v in vectors]]
    arrays = [pltpu.with_memory_space_constraint(v, pltpu.HBM) for v in arrays]
    times = expand.shape[1] // 2 // width
    halves = [shaped((2, own, width), BF16)] * 2 + [shaped((times, own, width), BF16)] * 2
    return pl.pallas_call(
        functools.partial(prepare_kernel, units),
        out_shape=(*halves, shaped((VECTOR_ROWS, width), BF16)),
        in_specs=[SMEM] + [pl.BlockSpec(memory_space=pltpu.HBM)] * len(arrays),
        out_specs=(VMEM,) * 5,
        scratch_shapes=[
            pltpu.VMEM((VECTOR_ROWS, width), F32),
            pltpu.VMEM((2, own, expand.shape[1] // 2), F32),
            *[pltpu.VMEM(v.shape, v.dtype) for v in arrays],
            pltpu.SemaphoreType.DMA((len(arrays),)),
        ],
        cost_estimate=COST,
        compiler_params=pltpu.CompilerParams(vmem_limit_bytes=8 << 20),
        name="prepare",
    )(number, *arrays)


def unpack_vectors(number_ref, sums_ref, out_refs):
    own, units, width = out_refs[0].shape[1], out_refs[-1].shape[1], sums_ref.shape[1]
    number = number_ref[0]
    first = pltpu.roll(sums_ref[:8, :], width - number * own, 1)
    for i, ref in enumerate(out_refs[:-1]):
        ref[...] = first[i : i + 1, :own]
    offset = (number // 2) * units
    here = lax.broadcasted_iota(jnp.int32, (VECTOR_ROWS - 8, width), 0) == offset // width
    row = jnp.sum(jnp.where(here, sums_ref[8:, :], 0.0), axis=0, keepdims=True)
    row = pltpu.roll(jnp.broadcast_to(row, (8, width)), width - offset % width, 1)
    out_refs[-1][...] = row[:1, :units]


def place_attention_kernel(table_ref, core_ref, mine_ref, other_ref, vector_ref, kv_ref, q_ref, o_ref, bias_ref):
    half = kv_ref.shape[0] // 2
    rows, side = q_ref.shape[1], q_ref.shape[2]
    tile = mine_ref.shape[1]
    tiles = rows // tile

    def body(j, carry):
        for ref, at in ((mine_ref, j), (other_ref, j + half)):
            chip = table_ref[at]
            for i in range(tiles):
                to = slice(i * tile, (i + 1) * tile)
                kv_ref[chip, to] = ref[j * (2 * tiles) + i]
                q_ref[chip, to] = ref[j * (2 * tiles) + tiles + i, :, :side]
                o_ref[chip, to] = ref[j * (2 * tiles) + tiles + i, :, side:]
        return carry

    lax.fori_loop(0, half, body, 0)
    values = vector_ref[...].astype(F32)
    values = jnp.where(core_ref[0] == 0, values[:8, :side], values[:8, side:])
    bias_ref[:, :side] = jnp.zeros((8, side), F32)
    bias_ref[:, side : 2 * side] = jnp.broadcast_to(values[VALUE_B : VALUE_B + 1], (8, side))
    bias_ref[:, 2 * side :] = jnp.broadcast_to(values[QUERY_B : QUERY_B + 1], (8, side))


def place_hidden_kernel(table_ref, mine_a_ref, other_a_ref, mine_d_ref, other_d_ref, expand_ref, reduce_ref):
    half = mine_a_ref.shape[0]
    rows, width = expand_ref.shape[1], mine_a_ref.shape[2]

    def body(j, carry):
        for a_ref, d_ref, at in ((mine_a_ref, mine_d_ref, j), (other_a_ref, other_d_ref, j + half)):
            chip = table_ref[at]
            for i in range(expand_ref.shape[2] // width):
                expand_ref[chip, :, i * width : (i + 1) * width] = a_ref[j, i * rows : (i + 1) * rows]
            reduce_ref[chip] = d_ref[j]
        return carry

    lax.fori_loop(0, half, body, 0)


def split_expand_kernel(table_ref, expand_ref, mine_ref, other_ref):
    half = mine_ref.shape[0]
    rows, width = expand_ref.shape[1], mine_ref.shape[2]

    def body(j, carry):
        for ref, at in ((mine_ref, j), (other_ref, j + half)):
            chip = table_ref[at]
            for i in range(expand_ref.shape[2] // width):
                ref[j, i * rows : (i + 1) * rows] = expand_ref[chip, :, i * width : (i + 1) * width]
        return carry

    lax.fori_loop(0, half, body, 0)


def split_reduce_kernel(table_ref, reduce_ref, mine_ref, other_ref):
    half = mine_ref.shape[0]

    def body(j, carry):
        mine_ref[j] = reduce_ref[table_ref[j]]
        other_ref[j] = reduce_ref[table_ref[j + half]]
        return carry

    lax.fori_loop(0, half, body, 0)


def split_attention_kernel(table_ref, kv_ref, q_ref, o_ref, mine_ref, other_ref):
    half = mine_ref.shape[0]
    rows, side = q_ref.shape[1], q_ref.shape[2]

    def body(j, carry):
        for ref, at in ((mine_ref, j), (other_ref, j + half)):
            chip = table_ref[at]
            ref[j, :rows] = kv_ref[chip]
            ref[j, rows:, :side] = q_ref[chip]
            ref[j, rows:, side:] = o_ref[chip]
        return carry

    lax.fori_loop(0, half, body, 0)


def fold_kernel(bit, keep_ref, got_ref, *out_refs):
    if len(out_refs) == 1:
        out_refs[0][...] = keep_ref[...].astype(F32) + got_ref[...].astype(F32)
        return
    low = 1 << bit
    for j in range(out_refs[0].shape[0]):
        block = j % low + j // low * 2 * low
        for i, ref in enumerate(out_refs):
            at = block + i * low
            ref[j] = (keep_ref[at].astype(F32) + got_ref[at].astype(F32)).astype(BF16)


def fold(keep, got, bit):
    blocks = keep.shape[0]
    out = shaped(keep.shape, F32) if blocks == 1 else (shaped((blocks // 2,) + keep.shape[1:], BF16),) * 2
    return call(functools.partial(fold_kernel, bit), "fold", out, keep, got)


def fold_vectors_kernel(bit, keep_ref, got_ref, vector_ref, *out_refs):
    rows = keep_ref.shape[0]
    vectors = vector_ref[...] + got_ref[rows:, :].astype(F32)
    out_refs[-1][...] = vectors
    if len(out_refs) == 2:
        out_refs[0][...] = keep_ref[...].astype(F32) + got_ref[:rows, :].astype(F32)
        return
    bit, blocks = bit
    size, low = rows // blocks, 1 << bit
    for j in range(blocks // 2):
        block = j % low + j // low * 2 * low
        for i in range(2):
            at = (block + i * low) * size
            total = keep_ref[at : at + size, :].astype(F32) + got_ref[at : at + size, :].astype(F32)
            out_refs[i][j * size : (j + 1) * size, :] = total.astype(BF16)
    out_refs[1][rows // 2 :, :] = vectors.astype(BF16)


def fold_vectors(keep, got, vectors, bit):
    rows, width = keep.shape
    if bit is None:
        out = (shaped((rows, width), F32), shaped(vectors.shape, F32))
    else:
        out = (
            shaped((rows // 2, width), BF16),
            shaped((rows // 2 + VECTOR_ROWS, width), BF16),
            shaped(vectors.shape, F32),
        )
    return call(functools.partial(fold_vectors_kernel, bit), "fold_vectors", out, keep, got, vectors)


def project_kernel(mine_ref, other_ref, weight_ref, bias_ref, out_ref):
    width = weight_ref.shape[1]
    bias = bias_ref[:1, :width]

    @pl.when(pl.program_id(0) == 0)
    def _():
        out_ref[...] = (dot(mine_ref[...], weight_ref[...]) + bias).astype(BF16)

    @pl.when(pl.program_id(0) == 1)
    def _():
        out_ref[...] = (dot(other_ref[...], weight_ref[...]) + bias).astype(BF16)


def project(mine, other, weight, bias):
    rows, width = mine.shape
    step = min(rows, 512)
    steps = rows // step
    return pl.pallas_call(
        project_kernel,
        out_shape=shaped((2 * rows, width), BF16),
        grid=(2, steps),
        in_specs=[
            pl.BlockSpec((step, width), lambda i, j: (jnp.where(i == 0, j, steps - 1), 0)),
            pl.BlockSpec((step, width), lambda i, j: (jnp.where(i == 0, 0, j), 0)),
            pl.BlockSpec(weight.shape, lambda i, j: (0, 0)),
            pl.BlockSpec(bias.shape, lambda i, j: (0, 0)),
        ],
        out_specs=pl.BlockSpec((step, width), lambda i, j: (i * steps + j, 0)),
        cost_estimate=COST,
        compiler_params=limit(2 * rows, 20),
        name="project",
    )(mine, other, weight, bias)


def head_scores(half, query, key, mask):
    column = lax.broadcasted_iota(jnp.int32, (1, 2 * HEAD_DIM), 1)
    here = (column < HEAD_DIM) if half == 0 else (column >= HEAD_DIM)
    one = (column == HEAD_DIM * (1 - half)).astype(F32).astype(BF16)
    return times_transpose(jnp.where(here, key, mask), jnp.where(here, query, one))


def scaled(query):
    return (query.astype(F32) * 0.125).astype(BF16)


def attend_kernel(q_ref, k_ref, v_ref, mask_ref, out_ref, logs_ref):
    query = scaled(q_ref[...])
    outs = []
    for half in range(2):
        at = slice(half * HEAD_DIM, (half + 1) * HEAD_DIM)
        scores = head_scores(half, query, k_ref[...], mask_ref[...])
        top = jnp.max(scores, axis=0, keepdims=True)
        weights = jnp.exp(scores - top)
        total = jnp.sum(weights, axis=0, keepdims=True)
        outs.append(contract_rows(v_ref[:, at], weights.astype(BF16)) / total)
        logs_ref[0, half : half + 1, :] = top + jnp.log(total)
    out_ref[...] = jnp.transpose(jnp.concatenate(outs, 0))


def attend(query, keys, mask):
    rows, width = query.shape
    tokens = keys.shape[0]
    step = rows if tokens <= 4096 else 128
    pair = 2 * HEAD_DIM
    pairs = width // pair
    spec_q = pl.BlockSpec((step, pair), lambda h, i: (i, h))
    flops = 16 * rows * tokens * width
    return pl.pallas_call(
        attend_kernel,
        out_shape=(shaped((rows, width), F32), shaped((pairs, 8, rows), F32)),
        grid=(pairs, rows // step),
        in_specs=[
            spec_q,
            pl.BlockSpec((tokens, pair), lambda h, i: (0, h)),
            pl.BlockSpec((tokens, pair), lambda h, i: (0, h + pairs)),
            pl.BlockSpec((tokens, 128), lambda h, i: (0, 0)),
        ],
        out_specs=[spec_q, pl.BlockSpec((1, 8, step), lambda h, i: (h, 0, i))],
        cost_estimate=COST,
        compiler_params=limit(tokens, 28),
        name="attend",
    )(query, keys, keys, mask)


def attend_back_kernel(
    q_ref, k_ref, v_ref, g_ref, o_ref, logs_ref, mask_ref, dq_ref, dk_ref, dv_ref, bias_ref, dk_sum, dv_sum
):
    step = pl.program_id(0)
    column = lax.broadcasted_iota(jnp.int32, (1, 2 * HEAD_DIM), 1)
    low_query, none = scaled(q_ref[...]), jnp.zeros((), BF16)

    @pl.when(step == 0)
    def _():
        dk_sum[...] = jnp.zeros_like(dk_sum)
        dv_sum[...] = jnp.zeros_like(dv_sum)

    products = jnp.transpose(g_ref[...].astype(F32) * o_ref[...])
    grads, dk, dv = [], None, None
    for half in range(2):
        at = slice(half * HEAD_DIM, (half + 1) * HEAD_DIM)
        here = (column < HEAD_DIM) if half == 0 else (column >= HEAD_DIM)
        grad = jnp.where(here, g_ref[...], none)
        scores = head_scores(half, low_query, k_ref[...], mask_ref[...])
        probs = jnp.exp(scores - logs_ref[0, half : half + 1, :])
        dots = jnp.sum(products[at], axis=0, keepdims=True)
        grad_scores = (probs * (times_transpose(v_ref[...], grad) - dots)).astype(BF16)
        grads.append(contract_rows(k_ref[...], grad_scores)[at])
        dk_part = dot(grad_scores, jnp.where(here, q_ref[...], none))
        dv_part = dot(probs.astype(BF16), grad)
        if dk_sum.shape[0] > 4096:
            dk_sum[...] += dk_part
            dv_sum[...] += dv_part
        else:
            dk, dv = (dk_part, dv_part) if half == 0 else (dk + dk_part, dv + dv_part)
    if dk is not None:
        dk_sum[...] += dk
        dv_sum[...] += dv
    dq_ref[...] = jnp.transpose(jnp.concatenate(grads, 0) * 0.125).astype(BF16)

    @pl.when(step == pl.num_programs(0) - 1)
    def _():
        dk_ref[...] = (dk_sum[...] * 0.125).astype(BF16)
        dv_ref[...] = dv_sum[...].astype(BF16)
        bias_ref[...] = jnp.broadcast_to(columns(dv_sum[...]), bias_ref.shape)


def attend_back(which, query, keys, grad, attended, logs, mask):
    rows, width = query.shape
    tokens = keys.shape[0]
    step = rows if tokens <= 4096 else 128
    pair = 2 * HEAD_DIM
    pairs = width // pair
    single = {"pipeline_mode": pl.Buffered(1)} if tokens > 4096 else {}
    spec_q = pl.BlockSpec((step, pair), lambda i: (i, which))
    spec_dq = pl.BlockSpec((step, pair), lambda i: (i, 0))
    spec_k = pl.BlockSpec((tokens, pair), lambda i: (0, which), **single)
    spec_v = pl.BlockSpec((tokens, pair), lambda i: (0, which + pairs), **single)
    spec_dk = pl.BlockSpec((tokens, pair), lambda i: (0, 0))
    flops = 40 * rows * tokens * pair
    return pl.pallas_call(
        attend_back_kernel,
        out_shape=(
            shaped((rows, pair), BF16),
            shaped((tokens, pair), BF16),
            shaped((tokens, pair), BF16),
            shaped((8, pair), F32),
        ),
        grid=(rows // step,),
        in_specs=[
            spec_q,
            spec_k,
            spec_v,
            spec_q,
            spec_q,
            pl.BlockSpec((1, 8, step), lambda i: (which, 0, i)),
            pl.BlockSpec((tokens, 128), lambda i: (0, 0), **single),
        ],
        out_specs=[spec_dq, spec_dk, spec_dk, pl.BlockSpec((8, pair), lambda i: (0, 0))],
        scratch_shapes=[pltpu.VMEM((tokens, pair), F32), pltpu.VMEM((tokens, pair), F32)],
        cost_estimate=COST,
        compiler_params=limit(tokens, 28),
        name="attend_back",
    )(query, keys, keys, grad, attended, logs, mask)


def keys_inputs_kernel(*refs):
    *part_refs, weight_ref, out_ref = refs
    total = None
    for i, ref in enumerate(part_refs):
        width = ref.shape[1]
        if i % 2:
            continue
        both = jnp.concatenate([ref[...], part_refs[i + 1][...]], axis=1)
        term = times_transpose(both, weight_ref[:, i * width : (i + 2) * width])
        total = term if total is None else total + term
    out_ref[...] = total.astype(BF16)


def keys_inputs(which, parts, weight):
    tokens, pair = parts[0].shape
    tokens //= 2
    width = weight.shape[0]
    step = min(tokens, 512)
    spec = pl.BlockSpec((step, pair), lambda i: (i + which * (tokens // step), 0))
    return pl.pallas_call(
        keys_inputs_kernel,
        out_shape=shaped((tokens, width), BF16),
        grid=(tokens // step,),
        in_specs=[spec] * len(parts) + [pl.BlockSpec(weight.shape, lambda i: (0, 0))],
        out_specs=pl.BlockSpec((step, width), lambda i: (i, 0)),
        cost_estimate=COST,
        compiler_params=limit(tokens, 20),
        name="keys_inputs",
    )(*parts, weight)


def keys_weights_kernel(table_ref, mine_ref, other_ref, q_ref, o_ref, *refs):
    *part_refs, keep_ref, send_ref, sum_ref, held_ref = refs
    first = (pl.program_id(0) == 0) & (pl.program_id(1) == 0)
    last = (pl.program_id(0) == 1) & (pl.program_id(1) == pl.num_programs(1) - 1)
    both = jnp.concatenate([ref[...] for ref in part_refs], axis=1)
    chips, rows, width = held_ref.shape
    half, side = chips // 2, width // 2

    @pl.when(first)
    def _():
        sum_ref[...] = contract_rows(mine_ref[...], both)

    @pl.when((pl.program_id(0) == 0) & (pl.program_id(1) > 0))
    def _():
        sum_ref[...] += contract_rows(mine_ref[...], both)

    @pl.when(pl.program_id(0) == 1)
    def _():
        sum_ref[...] += contract_rows(other_ref[...], both)

    @pl.when(last)
    def _():
        held_ref[...] = sum_ref[...].astype(BF16).reshape(held_ref.shape)

        def body(j, carry):
            for ref, at in ((keep_ref, j), (send_ref, j + half)):
                chip = table_ref[at]
                ref[j, :rows] = held_ref[chip]
                ref[j, rows:, :side] = q_ref[chip]
                ref[j, rows:, side:] = o_ref[chip]
            return carry

        lax.fori_loop(0, half, body, 0)


def flat_keys_weights_kernel(mine_ref, other_ref, *refs):
    *part_refs, grad_ref, sum_ref = refs
    first = (pl.program_id(0) == 0) & (pl.program_id(1) == 0)
    last = (pl.program_id(0) == 1) & (pl.program_id(1) == pl.num_programs(1) - 1)
    both = jnp.concatenate([ref[...] for ref in part_refs], axis=1)

    @pl.when(first)
    def _():
        sum_ref[...] = jnp.zeros_like(sum_ref)

    @pl.when(pl.program_id(0) == 0)
    def _():
        sum_ref[...] += contract_rows(mine_ref[...], both)

    @pl.when(pl.program_id(0) == 1)
    def _():
        sum_ref[...] += contract_rows(other_ref[...], both)

    @pl.when(last)
    def _():
        grad_ref[...] = sum_ref[...].astype(BF16)


def keys_weights(table, mine, other, grad_q, grad_o, parts):
    rows, width = mine.shape
    pair = parts[0].shape[1]
    chips, own = grad_q.shape[:2]
    step = min(rows, 512)
    steps = rows // step
    fused = own % 16 == 0
    block = shaped((chips // 2, 2 * own, width), BF16)
    tokens = [
        pl.BlockSpec((step, width), lambda i, j, *t: (jnp.where(i == 0, j, steps - 1), 0)),
        pl.BlockSpec((step, width), lambda i, j, *t: (jnp.where(i == 0, 0, j), 0)),
    ]
    spec = pl.BlockSpec((step, pair), lambda i, j, *t: (i * steps + j, 0))
    whole = pl.BlockSpec((chips, own, width // 2), lambda i, j, *t: (0, 0, 0))
    blocks = pl.BlockSpec(block.shape, lambda i, j, *t: (0, 0, 0))
    cost = COST
    if fused:
        return pl.pallas_call(
            keys_weights_kernel,
            out_shape=(block, block),
            grid_spec=pltpu.PrefetchScalarGridSpec(
                num_scalar_prefetch=1,
                grid=(2, steps),
                in_specs=tokens + [whole, whole] + [spec] * len(parts),
                out_specs=[blocks, blocks],
                scratch_shapes=[pltpu.VMEM((width, width), F32), pltpu.VMEM((chips, own, width), BF16)],
            ),
            cost_estimate=cost,
            compiler_params=limit(2 * rows, 24),
            name="keys_weights",
        )(table, mine, other, grad_q, grad_o, *parts)
    grad = pl.pallas_call(
        flat_keys_weights_kernel,
        out_shape=shaped((width, width), BF16),
        grid=(2, steps),
        in_specs=tokens + [spec] * len(parts),
        out_specs=pl.BlockSpec((width, width), lambda i, j: (0, 0)),
        scratch_shapes=[pltpu.VMEM((width, width), F32)],
        cost_estimate=cost,
        name="keys_weights",
    )(mine, other, *parts)
    return call(
        split_attention_kernel,
        "split_attention",
        (block, block),
        table,
        grad.reshape(chips, own, width),
        grad_q,
        grad_o,
        scalars=1,
    )


def normalize(values):
    center = values - jnp.mean(values, axis=-1, keepdims=True)
    scale = lax.rsqrt(jnp.mean(center * center, axis=-1, keepdims=True) + EPSILON)
    return center * scale, scale


def normalize_back(grad, normal, scale):
    return scale * (
        grad
        - jnp.mean(grad, axis=-1, keepdims=True)
        - normal * jnp.mean(grad * normal, axis=-1, keepdims=True)
    )


def row(ref, which):
    return ref[which : which + 1, :].astype(F32)


def columns(values):
    return jnp.sum(values, axis=0, keepdims=True)


def output_kernel(
    core_ref, inputs_ref, mine_ref, other_ref, near_ref, far_ref, vector_ref, normal_ref, scale_ref, low_ref
):
    side = mine_ref.shape[1]
    core = core_ref[0]
    here, there = pl.ds(core * side, side), pl.ds((1 - core) * side, side)

    def product(ref):
        return dot(mine_ref[...], ref[here, :]) + dot(other_ref[...], ref[there, :])

    near, far = product(near_ref), product(far_ref)
    even = core == 0
    hidden = jnp.concatenate([jnp.where(even, near, far), jnp.where(even, far, near)], axis=1)
    hidden = inputs_ref[...].astype(F32) + hidden + row(vector_ref, OUTPUT_B)
    normal, scale = normalize(hidden)
    normal_ref[...] = normal
    scale_ref[...] = jnp.broadcast_to(scale, scale_ref.shape)
    low_ref[...] = (normal * row(vector_ref, GAIN_1) + row(vector_ref, SHIFT_1)).astype(BF16)


def hidden_kernel(
    mine_ref, other_ref, normal_ref, expand_ref, reduce_ref, vector_ref, active_ref, slope_ref, base_ref, far_ref,
    active_held, slope_held, base_held, sems,
):
    rows = mine_ref.shape[0]
    width = mine_ref.shape[1]
    both = jnp.concatenate([mine_ref[...], other_ref[...]], axis=0)
    total, copies = None, []
    for i in range(expand_ref.shape[1] // width):
        at = slice(i * width, (i + 1) * width)
        value = dot(both, expand_ref[:, at]) + row(vector_ref, EXPAND_B + i)
        normal = 0.5 + 0.5 * lax.erf(value * np.float32(0.7071067811865476))
        active = (value * normal).astype(BF16)
        active_held[:, at] = active
        density = jnp.exp(value * value * -0.5) * np.float32(0.3989422804014327)
        slope_held[:, at] = (normal + value * density).astype(BF16)
        for j, (held, ref) in enumerate(((active_held, active_ref), (slope_held, slope_ref))):
            copies.append(pltpu.make_async_copy(held.at[:, at], ref.at[:, at], sems.at[2 * i + j]))
            copies[-1].start()
        term = dot(active, reduce_ref[at, :])
        total = term if total is None else total + term
    middle = normal_ref[...] * row(vector_ref, GAIN_1) + row(vector_ref, SHIFT_1)
    base_held[...] = middle + total[:rows] + row(vector_ref, REDUCE_B)
    copies.append(pltpu.make_async_copy(base_held, base_ref, sems.at[len(copies)]))
    copies[-1].start()
    far_ref[...] = total[rows:].astype(BF16)
    for copy in copies:
        copy.wait()


def final_kernel(
    start_ref, base_ref, far_ref, cotangent_ref, vector_ref, out_ref, grad_ref, low_ref, sums_ref
):
    combined = base_ref[...] + far_ref[...].astype(F32)
    normal, scale = normalize(combined)
    gain = row(vector_ref, GAIN_2)
    out_ref[...] = (normal * gain + row(vector_ref, SHIFT_2)).astype(BF16)
    place = start_ref[0] + lax.broadcasted_iota(jnp.int32, combined.shape, 0)
    upstream = jnp.where(place < start_ref[1], cotangent_ref[...].astype(F32), 0.0)
    grad = normalize_back(upstream * gain, normal, scale)
    grad_ref[...] = grad
    low_ref[...] = grad.astype(BF16)
    sums_ref[...] = jnp.zeros_like(sums_ref)
    sums_ref[REDUCE_B : REDUCE_B + 1, :] = columns(grad)
    sums_ref[GAIN_2 : GAIN_2 + 1, :] = columns(upstream * normal)
    sums_ref[SHIFT_2 : SHIFT_2 + 1, :] = columns(upstream)


def hidden_back_kernel(table_a_ref, table_d_ref, *refs):
    cl_mine_ref, cl_other_ref, *far = refs[:8]
    outs, held, sems = refs[8:15], refs[15:-1], refs[-1]
    copies = [pltpu.make_async_copy(i, h, sems.at[at]) for at, (i, h) in enumerate(zip(far, held))]
    copies[0].start()
    active_ref, slope_ref, reduce_ref, expand_ref, mid_mine_ref, mid_other_ref = held[:6]
    near_ref, far_ref, sums_ref, d_keep_ref, d_send_ref, a_keep_ref, a_send_ref = outs
    d_held_ref, a_held_ref, low_ref = held[6:]
    rows, width = cl_mine_ref.shape
    times = expand_ref.shape[1] // width
    both = jnp.concatenate([cl_mine_ref[...], cl_other_ref[...]], axis=0)
    sums_ref[...] = jnp.zeros_like(sums_ref)
    copies[0].wait()
    for copy in copies[1:]:
        copy.start()
    units = d_held_ref.shape[1]
    for i in range(times):
        part = contract_rows(active_ref[:, i * width : (i + 1) * width], both).astype(BF16)
        d_held_ref[i * width // units : (i + 1) * width // units] = part.reshape(width // units, units, width)
    split_reduce_kernel(table_d_ref, d_held_ref, d_keep_ref, d_send_ref)
    for copy in copies[1:3]:
        copy.wait()
    total = None
    for i in range(times):
        at = slice(i * width, (i + 1) * width)
        active = times_transpose(both, reduce_ref[at, :]).astype(BF16)
        grad = (active.astype(F32) * slope_ref[:, at].astype(F32)).astype(BF16)
        low_ref[:, at] = grad
        sums_ref[i : i + 1, :] = columns(grad.astype(F32))
    copies[3].wait()
    for i in range(times):
        at = slice(i * width, (i + 1) * width)
        term = times_transpose(low_ref[:, at], expand_ref[:, at])
        total = term if total is None else total + term
    near_ref[...] = total[:rows]
    far_ref[...] = total[rows:].astype(BF16)
    for copy in copies[4:]:
        copy.wait()
    mid = jnp.concatenate([mid_mine_ref[...], mid_other_ref[...]], axis=0)
    own = a_held_ref.shape[1]
    for i in range(times):
        at = slice(i * width, (i + 1) * width)
        a_held_ref[:, :, at] = contract_rows(mid, low_ref[:, at]).astype(BF16).reshape(width // own, own, width)
    split_expand_kernel(table_a_ref, a_held_ref, a_keep_ref, a_send_ref)


def hidden_back_plain_kernel(mine_ref, other_ref, expand_ref, reduce_ref, slope_ref, low_ref, near_ref, far_ref, sums_ref):
    rows, width = mine_ref.shape
    both = jnp.concatenate([mine_ref[...], other_ref[...]], axis=0)
    total = None
    sums_ref[...] = jnp.zeros_like(sums_ref)
    for i in range(expand_ref.shape[1] // width):
        at = slice(i * width, (i + 1) * width)
        active = times_transpose(both, reduce_ref[at, :]).astype(BF16)
        grad = (active.astype(F32) * slope_ref[:, at].astype(F32)).astype(BF16)
        low_ref[:, at] = grad
        sums_ref[i : i + 1, :] = columns(grad.astype(F32))
        term = times_transpose(grad, expand_ref[:, at])
        total = term if total is None else total + term
    near_ref[...] = total[:rows]
    far_ref[...] = total[rows:].astype(BF16)


def hidden_back(table_a, table_d, low, low_other, active, slope, reduce, expand, middle, middle_other, units):
    rows, width = low.shape
    hidden_units = reduce.shape[0]
    chips, own, times = hidden_units // units, width * units // hidden_units, hidden_units // width
    far = [active, slope, reduce, expand, middle, middle_other]
    far = [pltpu.with_memory_space_constraint(v, pltpu.HBM) for v in far]
    return pl.pallas_call(
        hidden_back_kernel,
        out_shape=(
            shaped((rows, width), F32),
            shaped((rows, width), BF16),
            shaped((8, width), F32),
            *(shaped((chips // 2, units, width), BF16),) * 2,
            *(shaped((chips // 2, times * own, width), BF16),) * 2,
        ),
        in_specs=[SMEM] * 2 + [VMEM] * 2 + [pl.BlockSpec(memory_space=pltpu.HBM)] * len(far),
        out_specs=(VMEM,) * 7,
        scratch_shapes=[
            *[pltpu.VMEM(v.shape, v.dtype) for v in far],
            pltpu.VMEM((chips, units, width), BF16),
            pltpu.VMEM((chips, own, hidden_units), BF16),
            pltpu.VMEM((2 * rows, hidden_units), BF16),
            pltpu.SemaphoreType.DMA((len(far),)),
        ],
        cost_estimate=COST,
        compiler_params=pltpu.CompilerParams(vmem_limit_bytes=24 << 20),
        name="hidden_back",
    )(table_a, table_d, low, low_other, *far)


def reduce_grads_kernel(low_mine_ref, low_other_ref, active_ref, grad_ref):
    width = low_mine_ref.shape[1]
    low = jnp.concatenate([low_mine_ref[...], low_other_ref[...]], axis=0)
    for i in range(active_ref.shape[1] // width):
        at = slice(i * width, (i + 1) * width)
        grad_ref[at, :] = contract_rows(active_ref[:, at], low).astype(BF16)


def expand_grads_kernel(mid_mine_ref, mid_other_ref, low_ref, grad_ref):
    width = mid_mine_ref.shape[1]
    mid = jnp.concatenate([mid_mine_ref[...], mid_other_ref[...]], axis=0)
    for i in range(low_ref.shape[1] // width):
        at = slice(i * width, (i + 1) * width)
        grad_ref[:, at] = contract_rows(mid, low_ref[:, at]).astype(BF16)


def output_back_kernel(
    core_ref, normal_ref, scale_ref, grad_ref, near_sum_ref, far_sum_ref, near_ref, far_ref, vector_ref,
    hidden_ref, low_ref, mine_ref, other_ref, sums_ref,
):
    side = near_ref.shape[1]
    core = core_ref[0]
    even = core == 0
    normal = normal_ref[...]
    grad_middle = grad_ref[...] + near_sum_ref[...] + far_sum_ref[...].astype(F32)
    grad = normalize_back(grad_middle * row(vector_ref, GAIN_1), normal, scale_ref[:, :1])
    hidden_ref[...] = grad
    low = grad.astype(BF16)
    low_ref[...] = low
    low_near = jnp.where(even, low[:, :side], low[:, side:])
    low_far = jnp.where(even, low[:, side:], low[:, :side])
    here, there = pl.ds(core * side, side), pl.ds((1 - core) * side, side)

    def product(rows):
        return times_transpose(low_near, near_ref[rows, :]) + times_transpose(low_far, far_ref[rows, :])

    mine_ref[...] = product(here).astype(BF16)
    other_ref[...] = product(there).astype(BF16)
    sums_ref[...] = jnp.zeros_like(sums_ref)
    sums_ref[OUTPUT_B : OUTPUT_B + 1, :] = columns(grad)
    sums_ref[GAIN_1 : GAIN_1 + 1, :] = columns(grad_middle * normal)
    sums_ref[SHIFT_1 : SHIFT_1 + 1, :] = columns(grad_middle)


def output_grads_kernel(core_ref, mine_ref, other_ref, low_ref, near_ref, far_ref):
    side = mine_ref.shape[1]
    core = core_ref[0]
    even = core == 0
    here, there = pl.ds(core * side, side), pl.ds((1 - core) * side, side)
    for rows, ref in ((here, mine_ref), (there, other_ref)):
        product = contract_rows(ref[...], low_ref[...])
        near_ref[rows, :] = jnp.where(even, product[:, :side], product[:, side:])
        far_ref[rows, :] = jnp.where(even, product[:, side:], product[:, :side]).astype(BF16)


def join_units_kernel(units, core_ref, mine_ref, other_ref, out_ref):
    times, width = mine_ref.shape[0], mine_ref.shape[2]
    even = core_ref[0] == 0
    for i in range(times):
        mine, other = mine_ref[i], other_ref[i]
        parts = (jnp.where(even, mine, other), jnp.where(even, other, mine))
        for j in range(width // units):
            at = (i * (width // units) + j) * 2 * units
            for k, part in enumerate(parts):
                out_ref[:, at + k * units : at + (k + 1) * units] = part[:, j * units : (j + 1) * units]


def finish_kernel(number_ref, mine_ref, other_ref, sums_ref, *out_refs):
    side = mine_ref.shape[2] // 2
    even = number_ref[0] % 2 == 0
    for i, ref in enumerate(out_refs[:4]):
        at = slice(i % 2 * side, (i % 2 + 1) * side)
        mine, other = mine_ref[i // 2, :, at], other_ref[i // 2, :, at]
        ref[:, :side] = jnp.where(even, mine, other)
        ref[:, side:] = jnp.where(even, other, mine)
    unpack_vectors(number_ref, sums_ref, out_refs[4:])


def query_back_kernel(mine_ref, other_ref, weight_ref, *refs):
    *dq_refs, near_ref, far_ref, grad_ref, sums_ref = refs
    rows = mine_ref.shape[0]
    grads = jnp.concatenate([ref[...] for ref in dq_refs], axis=1)
    product = times_transpose(grads, weight_ref[...])
    near_ref[...] = product[:rows]
    far_ref[...] = product[rows:].astype(BF16)
    both = jnp.concatenate([mine_ref[...], other_ref[...]], axis=0)
    grad_ref[...] = contract_rows(both, grads).astype(BF16)
    sums_ref[...] = jnp.broadcast_to(columns(grads.astype(F32)), sums_ref.shape)


def body(
    layer_input,
    cotangent,
    lengths,
    query_weight,
    query_bias,
    key_weight,
    value_weight,
    value_bias,
    output_weight,
    output_bias,
    attn_gain,
    attn_shift,
    expand_weight,
    expand_bias,
    reduce_weight,
    reduce_bias,
    final_gain,
    final_shift,
):
    place = Place()
    core = place.core
    core_s = core.reshape(1)
    number_s = place.number.reshape(1)
    chips = place.count // 2
    inputs = layer_input[0]
    rows, width = inputs.shape
    side = width // 2
    own = query_weight.shape[0]
    units = reduce_weight.shape[0]
    hidden_units = units * chips
    times = hidden_units // width
    length = lengths[0]
    even = core == 0

    masks = [place.others(place.weight_stages, k) for k in range(2)]
    usual = len(place.weight_stages) == 4 and len(place.token_stages) == 3
    turns = WEIGHT_TURNS if usual else {}

    def chip_table(bit=None):
        blocks = np.arange(chips)
        if bit is not None:
            blocks = np.concatenate([blocks[blocks >> bit & 1 == i] for i in range(2)])
        return (place.number ^ jnp.where(even, masks[0][blocks], masks[1][blocks])) // 2

    def first_bit(name):
        return turns[name][0] if name in turns else len(place.weight_stages) - 1

    table = chip_table()
    token_masks = [place.others(place.token_stages, k) for k in range(2)]
    near_ctx = place.context ^ jnp.where(even, token_masks[0], token_masks[1])
    far_ctx = (place.context ^ 1) ^ jnp.where(even, token_masks[1], token_masks[0])
    blocks = jnp.concatenate([near_ctx, far_ctx])
    positions = (blocks[:, None] * rows + jnp.arange(rows, dtype=jnp.int32)).reshape(-1, 1)
    mask = jnp.where(positions < length, 0.0, MASKED).astype(BF16)
    mask = jnp.where(jnp.arange(2 * HEAD_DIM) % HEAD_DIM == 0, mask, 0)

    def joined(mine, other):
        return jnp.where(
            even, jnp.concatenate([mine, other], 1), jnp.concatenate([other, mine], 1)
        ).reshape(-1, width)

    vector_list = [query_bias, value_bias, output_bias, attn_gain, attn_shift, reduce_bias, final_gain, final_shift]
    attention_mine, attention_other, expand_mine, expand_other, vectors = prepare(
        number_s,
        [key_weight, value_weight, query_weight, output_weight],
        expand_weight,
        vector_list + [expand_bias],
    )
    vector_swap = place.swap(vectors, 0)
    vectors = vectors + jnp.where(jnp.arange(VECTOR_ROWS)[:, None] < 8, vector_swap, 0)

    stages = place.weight_stages
    token_stages = place.token_stages
    order = Order(place, STRICT[0])

    other_inputs = place.swap(inputs, 0)
    attention_swapped = place.swap(attention_other, 0)
    if FIRST_WAITS:
        order.last = (attention_swapped,)
    attention_blocks = Gather(order, joined(attention_mine, attention_swapped), stages, vectors)
    block_rows = attention_blocks.held.shape[0]
    expand_rows = joined(expand_mine, place.swap(expand_other, 0))
    expand_blocks = Gather(order, expand_rows[None], stages)
    reduce_blocks = Gather(order, reduce_weight[None], stages)
    token_blocks = Gather(order, inputs[None], token_stages)
    chains = {"X": token_blocks, "B": attention_blocks, "A": expand_blocks, "D": reduce_blocks}
    play(FORWARD[0] if usual else plain_events(chains), chains)

    aligned = (2 * own) % 16 == 0
    tile = 16 if aligned else 2 * own

    def tiles(array):
        array = array if aligned else array[: array.shape[0] // block_rows * block_rows]
        return array.reshape(-1, tile, width)

    weights_kv, weights_q, output_near, bias = call(
        place_attention_kernel,
        "place_attention",
        (
            shaped((chips, 2 * own, width), BF16),
            shaped((chips, 2 * own, side), BF16),
            shaped((chips, 2 * own, side), BF16),
            shaped((8, 3 * side), F32),
        ),
        table,
        core_s,
        tiles(attention_blocks.held),
        tiles(attention_blocks.got),
        attention_blocks.vectors,
        scalars=2,
    )
    vectors = attention_blocks.vectors
    weights_kv = weights_kv.reshape(width, width)
    weights_q = weights_q.reshape(width, side)
    output_near = output_near.reshape(width, side)
    if usual:
        play(FORWARD[1], chains)

    sequence_near = jnp.concatenate([token_blocks.held, token_blocks.got]).reshape(-1, width)
    sequence_far = place.swap(sequence_near, 0)
    keys = project(sequence_near, sequence_far, weights_kv, bias)
    if usual:
        play(FORWARD[2], chains)
    query = jnp.concatenate([inputs, other_inputs])
    query = (dot(query, weights_q) + bias[:1, 2 * side :]).astype(BF16)
    attended, logs = attend(query, keys, mask)
    if usual:
        play(FORWARD[3], chains)
    output_far = place.swap(output_near, 0)
    expand_matrix, reduce_matrix = call(
        place_hidden_kernel,
        "place_hidden",
        (shaped((chips, 2 * own, hidden_units), BF16), shaped((chips, units, width), BF16)),
        table,
        expand_blocks.held,
        expand_blocks.got,
        reduce_blocks.held,
        reduce_blocks.got,
        scalars=1,
    )
    expand_matrix = expand_matrix.reshape(width, hidden_units)
    reduce_matrix = reduce_matrix.reshape(hidden_units, width)
    attended_low = attended.astype(BF16)
    attended_mine = attended_low[:rows]
    attended_other = place.swap(attended_low[rows:], 0)

    normal_one, scale_one, middle_low = call(
        output_kernel,
        "output",
        (shaped((rows, width), F32), shaped((rows, 128), F32), shaped((rows, width), BF16)),
        core_s,
        Far(inputs),
        attended_mine,
        attended_other,
        Far(output_near),
        output_far,
        Far(vectors),
        scalars=1,
    )

    middle_other = place.swap(middle_low, 0)
    active, slope, base, far = call(
        hidden_kernel,
        "hidden",
        (
            shaped((2 * rows, hidden_units), BF16),
            shaped((2 * rows, hidden_units), BF16),
            shaped((rows, width), F32),
            shaped((rows, width), BF16),
        ),
        middle_low,
        middle_other,
        normal_one,
        expand_matrix,
        reduce_matrix,
        vectors,
        scratch=[
            pltpu.VMEM((2 * rows, hidden_units), BF16),
            pltpu.VMEM((2 * rows, hidden_units), BF16),
            pltpu.VMEM((rows, width), F32),
            pltpu.SemaphoreType.DMA((2 * times + 1,)),
        ],
        stored=(0, 1, 2),
    )
    far = place.swap(far, 0)
    start_s = jnp.stack([place.context * rows, length])
    layer_output, grad_combined, combined_low, sums_two = call(
        final_kernel,
        "final",
        (
            shaped((rows, width), BF16),
            shaped((rows, width), F32),
            shaped((rows, width), BF16),
            shaped((8, width), F32),
        ),
        start_s,
        Far(base),
        far,
        Far(cotangent[0]),
        Far(vectors),
        scalars=1,
        room=8,
    )
    combined_other = place.swap(combined_low, 0)
    table_d, table_a = chip_table(first_bit("D")), chip_table(first_bit("A"))
    if (2 * own) % 16 == 0:
        near, far, sums_expand, reduce_keep, reduce_send, expand_keep, expand_send = hidden_back(
            table_a,
            table_d,
            combined_low,
            combined_other,
            active,
            slope,
            reduce_matrix,
            expand_matrix,
            middle_low,
            middle_other,
            units,
        )
    else:
        grad_expanded, near, far, sums_expand = call(
            hidden_back_plain_kernel,
            "hidden_back",
            (
                shaped((2 * rows, hidden_units), BF16),
                shaped((rows, width), F32),
                shaped((rows, width), BF16),
                shaped((8, width), F32),
            ),
            combined_low,
            combined_other,
            expand_matrix,
            reduce_matrix,
            slope,
        )
        grads = call(
            reduce_grads_kernel,
            "reduce_grads",
            shaped((hidden_units, width), BF16),
            combined_low,
            combined_other,
            active,
        )
        out = (shaped((chips // 2, units, width), BF16),) * 2
        reduce_keep, reduce_send = call(
            split_reduce_kernel, "split_reduce", out, table_d, grads.reshape(chips, units, width), scalars=1
        )
        grads = call(
            expand_grads_kernel,
            "expand_grads",
            shaped((width, hidden_units), BF16),
            middle_low,
            middle_other,
            grad_expanded,
        )
        out = (shaped((chips // 2, times * 2 * own, width), BF16),) * 2
        expand_keep, expand_send = call(
            split_expand_kernel, "split_expand", out, table_a, grads.reshape(chips, 2 * own, hidden_units), scalars=1
        )
    far = place.swap(far, 0)

    grad_hidden, hidden_low, grad_mine, grad_other, sums_one = call(
        output_back_kernel,
        "output_back",
        (
            shaped((rows, width), F32),
            shaped((rows, width), BF16),
            shaped((rows, side), BF16),
            shaped((rows, side), BF16),
            shaped((8, width), F32),
        ),
        core_s,
        Far(normal_one),
        Far(scale_one),
        grad_combined,
        near,
        far,
        Far(output_near),
        Far(output_far),
        Far(vectors),
        scalars=1,
    )
    grad_heads = jnp.concatenate([grad_mine, place.swap(grad_other, 0)])
    output_near_grad, output_far_grad = call(
        output_grads_kernel,
        "output_grads",
        (shaped((width, side), F32), shaped((width, side), BF16)),
        core_s,
        Far(attended_mine),
        Far(attended_other),
        hidden_low,
        scalars=1,
    )
    grad_output = (output_near_grad + place.swap(output_far_grad, 0).astype(F32)).astype(BF16)

    def own_half(array, axis):
        first, second = lax.index_in_dim(array, 0, axis, False), lax.index_in_dim(array, 1, axis, False)
        return jnp.where(even, first, second), jnp.where(even, second, first)

    order = Order(place, STRICT[1])
    chains = {
        "D": Scatter(order, reduce_keep, reduce_send, stages, turn=turns.get("D")),
        "A": Scatter(order, expand_keep, expand_send, stages, turn=turns.get("A")),
    }
    if usual:
        play("DA", chains)

    def held_back(kernel, array):
        return order.wait(array) if usual and WAITS[kernel] else array

    parts = []
    pairs = side // (2 * HEAD_DIM)
    for which in range(pairs):
        parts.append(attend_back(which, held_back(which, query), keys, grad_heads, attended, logs, mask))
        if usual:
            play(BACKWARD[which], chains)
    grad_query, grad_keys, grad_values, value_bias_sums = zip(*parts)
    parts = grad_keys + grad_values
    near, far, grad_query_w, query_bias_sum = call(
        query_back_kernel,
        "query_back",
        (
            shaped((rows, width), F32),
            shaped((rows, width), BF16),
            shaped((width, side), BF16),
            shaped((8, side), F32),
        ),
        Far(inputs),
        Far(other_inputs),
        Far(weights_q),
        *grad_query,
    )
    query_part = grad_hidden + near + place.swap(far, 0).astype(F32)

    mine_rows = jnp.stack([query_bias_sum[0], jnp.concatenate([v[0] for v in value_bias_sums])])
    zero = jnp.zeros_like(mine_rows)
    mine_rows = jnp.where(even, jnp.concatenate([mine_rows, zero], 1), jnp.concatenate([zero, mine_rows], 1))
    vector_sums = jnp.concatenate([mine_rows, (sums_one + sums_two)[2:], sums_expand])
    vector_swap = place.swap(vector_sums, 0)
    vector_sums = vector_sums + jnp.where(jnp.arange(VECTOR_ROWS)[:, None] < 8, vector_swap, 0)

    far_part = keys_inputs(1, (held_back(4, parts[0]), *parts[1:]), weights_kv)
    far_got = place.swap(far_part, 0)
    near_part = keys_inputs(0, (held_back(5, parts[0]), *parts[1:]), weights_kv)
    blocks_shape = (sequence_near.shape[0] // rows, rows, width)
    turn = range(len(token_stages))[::-1]
    if usual:
        kinds = "ab"[:TOKEN_NEAR] + "y" + "ab"[TOKEN_NEAR:]
        turn = [kinds.index(kind) for kind in TOKEN_TURN]
    x_keep, x_send = fold(near_part.reshape(blocks_shape), far_got.reshape(blocks_shape), turn[0])
    chains["X"] = Scatter(order, x_keep, x_send, token_stages, turn=turn)
    if usual:
        play(BACKWARD[3], chains)

    inputs_first = (x_send,) if usual and INPUTS_FIRST else ()
    keep, send = keys_weights(
        chip_table(first_bit("B")),
        after(held_back(3, sequence_near), *inputs_first),
        sequence_far,
        grad_query_w.reshape(chips, 2 * own, side),
        grad_output.reshape(chips, 2 * own, side),
        parts,
    )
    keep = keep.reshape(-1, width)
    send = jnp.concatenate([send.reshape(-1, width), vector_sums.astype(BF16)])
    chains["B"] = Scatter(order, keep, send, stages, vector_sums, turns.get("B"))
    play(BACKWARD[4].rstrip("|b") if usual else plain_events(chains), chains)
    reduce_out = chains["D"].keep[0]
    expand_sum = chains["A"].keep[0].reshape(times, 2, own, width)
    input_grad = query_part + chains["X"].keep[0]

    expand_mine, expand_other = own_half(expand_sum, 1)
    expand_out = call(
        functools.partial(join_units_kernel, units),
        "join_units",
        shaped((own, 2 * hidden_units), F32),
        core_s,
        expand_mine,
        place.swap(expand_other, 0),
        scalars=1,
    )

    if usual:
        chains["B"].done(expand_out, input_grad)
    keep, vector_sums = chains["B"].keep, chains["B"].vectors
    pieces = keep.reshape(2, 2, own, width)
    pieces_mine, pieces_other = own_half(pieces, 1)
    pieces_other = place.swap(pieces_other, 0)
    outs = call(
        finish_kernel,
        "finish",
        [shaped((own, width), F32)] * 4 + [shaped((1, own), F32)] * 8 + [shaped((1, units), F32)],
        number_s,
        pieces_mine,
        pieces_other,
        vector_sums,
        scalars=1,
    )
    weights_out, outs = outs[:4], outs[4:]
    outs = [v.reshape(-1) for v in outs]
    return (
        layer_output[None],
        input_grad[None],
        weights_out[2],
        outs[QUERY_B],
        weights_out[0],
        weights_out[1],
        outs[VALUE_B],
        weights_out[3],
        outs[OUTPUT_B],
        outs[GAIN_1],
        outs[SHIFT_1],
        expand_out,
        outs[EXPAND_B],
        reduce_out,
        outs[REDUCE_B],
        outs[GAIN_2],
        outs[SHIFT_2],
    )


def solution(mesh):
    tokens = P("seq", "ctx", None)
    matrix = P(("seq", "ctx"), None)
    vector = P(("seq", "ctx"))
    weights = (
        matrix,
        vector,
        matrix,
        matrix,
        vector,
        matrix,
        vector,
        vector,
        vector,
        matrix,
        vector,
        matrix,
        vector,
        vector,
        vector,
    )
    return jax.shard_map(
        body,
        mesh=mesh,
        in_specs=(tokens, tokens, P("seq")) + weights,
        out_specs=(tokens, tokens) + weights,
        check_vma=False,
    )
```

```python
import functools

import jax
import jax.numpy as jnp
import numpy as np
from jax import lax
from jax.experimental import pallas as pl
from jax.experimental.pallas import tpu as pltpu
from jax.sharding import PartitionSpec as P

HEADS = 12
HEAD_DIM = 64
EPSILON = 1e-12
MASKED = -1000000000.0
EVERY = ("seq", "ctx")
F32 = jnp.float32
BF16 = jnp.bfloat16
VMEM = pl.BlockSpec(memory_space=pltpu.VMEM)
SMEM = pl.BlockSpec(memory_space=pltpu.SMEM)
QUERY_B, VALUE_B, OUTPUT_B, GAIN_1, SHIFT_1, REDUCE_B, GAIN_2, SHIFT_2, EXPAND_B = range(9)
VECTOR_ROWS = 16
SMALL_BYTES = 16 << 20
COST = pl.CostEstimate(flops=1000, bytes_accessed=1000, transcendentals=0)
FORWARD = ('XBADbxad|BAba|BADXbadx|BDXbd|', 'xAD', '', 'ad|')
BACKWARD = ('', '', 'a|A', 'da|DX', 'B|Adab|DABx|aXdbBDxd|Xb|B|xb')
TOKEN_NEAR = 0
TOKEN_TURN = 'mix'
WEIGHT_TURNS = {'D': (1, 0, 3, 2), 'A': (3, 2, 1, 0), 'B': (3, 2, 1, 0)}
WAITS = (False, False, False, False, False, False)
FIRST_WAITS = False
INPUTS_FIRST = False
REDUCE_FIRST = False
STRICT = (True, False)


def dot(left, right):
    return jnp.dot(left, right, preferred_element_type=F32)


def contract_rows(left, right):
    return lax.dot_general(left, right, (((0,), (0,)), ((), ())), preferred_element_type=F32)


def times_transpose(left, right):
    return lax.dot_general(left, right, (((1,), (1,)), ((), ())), preferred_element_type=F32)


def shaped(shape, dtype):
    return jax.ShapeDtypeStruct(tuple(shape), dtype)


def after(array, *earlier):
    return lax.optimization_barrier((array, *earlier))[0]


def in_hbm(array):
    return pltpu.with_memory_space_constraint(array, pltpu.HBM)


class Far:
    def __init__(self, array):
        self.array = array


def fetching(kernel, scalars, far, count, *refs):
    inputs, rest = list(refs[:count]), refs[count : len(refs) - len(far) - 1]
    held, sems = refs[len(refs) - len(far) - 1 : -1], refs[-1]
    copies = [pltpu.make_async_copy(inputs[at], room, sems.at[i]) for i, (at, room) in enumerate(zip(far, held))]
    for copy in copies:
        copy.start()
    for copy in copies:
        copy.wait()
    for at, room in zip(far, held):
        inputs[at] = room
    kernel(*inputs, *rest)


def call(kernel, name, outs, *args, scalars=0, scratch=(), room=16, stored=()):
    many = isinstance(outs, (tuple, list))
    far = [i for i, a in enumerate(args) if isinstance(a, Far)]
    args = [a.array if isinstance(a, Far) else a for a in args]
    flat = tuple(outs) if many else (outs,)
    small = sum(a.size * a.dtype.itemsize for a in (*args, *flat)) < SMALL_BYTES
    specs = [SMEM] * scalars + [VMEM] * (len(args) - scalars)
    scratch = list(scratch)
    if far and small:
        kernel = functools.partial(fetching, kernel, scalars, far, len(args))
        for at in far:
            specs[at] = pl.BlockSpec(memory_space=pltpu.HBM)
            args[at] = pltpu.with_memory_space_constraint(args[at], pltpu.HBM)
            scratch.append(pltpu.VMEM(args[at].shape, args[at].dtype))
        scratch.append(pltpu.SemaphoreType.DMA((len(far),)))
    out_specs = [VMEM] * len(flat)
    for at in stored:
        out_specs[at] = pl.BlockSpec(memory_space=pltpu.HBM)
        flat = flat[:at] + (pltpu.HBM(flat[at].shape, flat[at].dtype),) + flat[at + 1 :]
    return pl.pallas_call(
        kernel,
        out_shape=flat if many else flat[0],
        in_specs=specs,
        out_specs=tuple(out_specs) if many else out_specs[0],
        scratch_shapes=scratch,
        cost_estimate=COST,
        compiler_params=pltpu.CompilerParams(vmem_limit_bytes=room << 20 if small else None),
        name=name,
    )(*args)


def limit(tokens, mebibytes):
    return pltpu.CompilerParams(vmem_limit_bytes=mebibytes << 20 if tokens <= 4096 else None)


class Place:
    def __init__(self):
        self.ctx = lax.axis_size("ctx")
        self.count = lax.axis_size("seq") * self.ctx
        self.bits = self.count.bit_length() - 1
        self.context = lax.axis_index("ctx")
        self.number = lax.axis_index("seq") * self.ctx + self.context
        self.core = self.number & 1
        top = self.bits - 1
        middle = list(range(2, top))
        self.weight_stages = list(zip(middle[::-1], middle)) + [(1, top), (top, 1)]
        self.token_stages = list(zip(middle[::-1], middle))
        self.token_stages.insert(min(TOKEN_NEAR, len(middle)), (1, 1))

    def swap(self, array, even, odd=None):
        odd = even if odd is None else odd
        pairs = [(i, i ^ (1 << (odd if i & 1 else even))) for i in range(self.count)]
        return lax.ppermute(array, EVERY, pairs)

    def others(self, stages, core):
        masks = [0]
        for stage in stages:
            masks = masks + [m ^ (1 << stage[core]) for m in masks]
        return np.array(masks, np.int32)


class Order:
    def __init__(self, place, strict):
        self.place = place
        self.strict = strict
        self.last = ()
        self.ended = ()

    def close(self):
        if self.ended:
            self.last, self.ended = self.ended, ()

    def wait(self, array):
        return after(array, *self.last) if self.last else array

    def start(self, array, stage):
        return self.place.swap(self.wait(array), *stage)

    def done(self, got):
        used = self.wait(got) if self.strict else got
        self.ended += (got,)
        return used

    def ran(self, out):
        self.ended += (out,)
        return out


class Gather:
    def __init__(self, order, blocks, stages, vectors=None):
        self.order, self.held, self.stages, self.vectors = order, blocks, list(stages), vectors
        self.got = None

    def start(self):
        sent = self.held if self.vectors is None else jnp.concatenate([self.held, self.vectors])
        self.got = self.order.start(sent, self.stages.pop(0))

    def done(self):
        self.got = self.order.done(self.got)
        got = self.got
        if self.vectors is not None:
            self.vectors = self.vectors + got[-VECTOR_ROWS:]
            got = got[:-VECTOR_ROWS]
        if self.stages:
            self.held = jnp.concatenate([self.held, got])


class Scatter:
    def __init__(self, order, keep, send, stages, vectors=None, turn=None):
        self.order, self.keep, self.send, self.vectors = order, keep, send, vectors
        turn = list(range(len(stages)))[::-1] if turn is None else list(turn)
        self.stages = [stages[i] for i in turn]
        left = sorted(turn)
        self.bits = []
        for i in turn:
            self.bits.append(left.index(i))
            left.remove(i)
        self.bits.pop(0)

    def start(self):
        self.got = self.order.start(self.send, self.stages.pop(0))

    def done(self, *earlier):
        got = self.order.done(self.got)
        got = after(got, *earlier) if earlier else got
        last = not self.stages
        if self.vectors is None:
            out = fold(self.keep, got, None if last else self.bits.pop(0))
            self.keep, self.send = (out, None) if last else out
        elif last:
            self.keep, self.vectors = fold_vectors(self.keep, got, self.vectors, None)
        else:
            bit = (self.bits.pop(0), 2 << len(self.bits))
            self.keep, self.send, self.vectors = fold_vectors(self.keep, got, self.vectors, bit)


def play(events, chains):
    for event in events:
        if event == "|":
            next(iter(chains.values())).order.close()
            continue
        chain = chains[event.upper()]
        if event.isupper():
            chain.start()
        else:
            chain.done()


def plain_events(chains):
    events = ""
    left = {name: len(chain.stages) for name, chain in chains.items()}
    while any(left.values()):
        names = [n for n in left if left[n]]
        events += "".join(names) + "".join(names).lower() + "|"
        for n in names:
            left[n] -= 1
    return events


def prepare_kernel(units, number_ref, *refs):
    count = EXPAND_B + 6
    in_refs, outs = refs[:count], refs[count : count + 5]
    rows_ref, split_ref = refs[count + 5 : count + 7]
    held_refs, sems = refs[count + 7 : -1], refs[-1]
    copies = [pltpu.make_async_copy(i, h, sems.at[at]) for at, (i, h) in enumerate(zip(in_refs, held_refs))]
    for copy in copies:
        copy.start()
    key_mine_ref, key_other_ref, expand_mine_ref, expand_other_ref, vectors_ref = outs
    number = number_ref[0]
    even = number % 2 == 0
    rows_ref[...] = jnp.zeros_like(rows_ref)
    for copy in copies:
        copy.wait()
    weights, expand_ref, vectors = held_refs[:4], held_refs[4], held_refs[5:]
    own, width = weights[0].shape
    side = width // 2
    for i, ref in enumerate(weights):
        first, second = ref[:, :side], ref[:, side:]
        at = slice(i % 2 * side, (i % 2 + 1) * side)
        key_mine_ref[i // 2, :, at] = jnp.where(even, first, second)
        key_other_ref[i // 2, :, at] = jnp.where(even, second, first)
    for i in range(expand_ref.shape[1] // units):
        at = i // 2 * units
        split_ref[i % 2, :, at : at + units] = expand_ref[:, i * units : (i + 1) * units].astype(F32)
    for i in range(expand_mine_ref.shape[0]):
        at = slice(i * width, (i + 1) * width)
        first, second = split_ref[0, :, at], split_ref[1, :, at]
        expand_mine_ref[i] = jnp.where(even, first, second).astype(BF16)
        expand_other_ref[i] = jnp.where(even, second, first).astype(BF16)
    for i, ref in enumerate(vectors[:-1]):
        rows_ref[i : i + 1, :own] = ref[...].astype(F32)
    rows_ref[EXPAND_B : EXPAND_B + 1, :units] = vectors[-1][...].astype(F32)
    first = pltpu.roll(rows_ref[:8, :], number * own, 1)
    offset = (number // 2) * units
    second = pltpu.roll(rows_ref[8:, :], offset % width, 1)
    here = lax.broadcasted_iota(jnp.int32, second.shape, 0) == offset // width
    second = jnp.where(here, jnp.broadcast_to(second[:1], second.shape), 0.0)
    vectors_ref[...] = jnp.concatenate([first, second], 0).astype(BF16)


def prepare(number, weights, expand, vectors):
    own, width = weights[0].shape
    units = vectors[-1].shape[0]
    arrays = [*weights, expand, *[v.reshape(1, -1) for v in vectors]]
    arrays = [pltpu.with_memory_space_constraint(v, pltpu.HBM) for v in arrays]
    times = expand.shape[1] // 2 // width
    halves = [shaped((2, own, width), BF16)] * 2 + [shaped((times, own, width), BF16)] * 2
    return pl.pallas_call(
        functools.partial(prepare_kernel, units),
        out_shape=(*halves, shaped((VECTOR_ROWS, width), BF16)),
        in_specs=[SMEM] + [pl.BlockSpec(memory_space=pltpu.HBM)] * len(arrays),
        out_specs=(VMEM,) * 5,
        scratch_shapes=[
            pltpu.VMEM((VECTOR_ROWS, width), F32),
            pltpu.VMEM((2, own, expand.shape[1] // 2), F32),
            *[pltpu.VMEM(v.shape, v.dtype) for v in arrays],
            pltpu.SemaphoreType.DMA((len(arrays),)),
        ],
        cost_estimate=COST,
        compiler_params=pltpu.CompilerParams(vmem_limit_bytes=8 << 20),
        name="prepare",
    )(number, *arrays)


def unpack_vectors(number_ref, sums_ref, out_refs):
    own, units, width = out_refs[0].shape[1], out_refs[-1].shape[1], sums_ref.shape[1]
    number = number_ref[0]
    first = pltpu.roll(sums_ref[:8, :], width - number * own, 1)
    for i, ref in enumerate(out_refs[:-1]):
        ref[...] = first[i : i + 1, :own]
    offset = (number // 2) * units
    here = lax.broadcasted_iota(jnp.int32, (VECTOR_ROWS - 8, width), 0) == offset // width
    row = jnp.sum(jnp.where(here, sums_ref[8:, :], 0.0), axis=0, keepdims=True)
    row = pltpu.roll(jnp.broadcast_to(row, (8, width)), width - offset % width, 1)
    out_refs[-1][...] = row[:1, :units]


def place_attention_kernel(table_ref, core_ref, mine_ref, other_ref, vector_ref, kv_ref, q_ref, o_ref, bias_ref):
    half = kv_ref.shape[0] // 2
    rows, side = q_ref.shape[1], q_ref.shape[2]
    tile = mine_ref.shape[1]
    tiles = rows // tile

    def body(j, carry):
        for ref, at in ((mine_ref, j), (other_ref, j + half)):
            chip = table_ref[at]
            for i in range(tiles):
                to = slice(i * tile, (i + 1) * tile)
                kv_ref[chip, to] = ref[j * (2 * tiles) + i]
                q_ref[chip, to] = ref[j * (2 * tiles) + tiles + i, :, :side]
                o_ref[chip, to] = ref[j * (2 * tiles) + tiles + i, :, side:]
        return carry

    lax.fori_loop(0, half, body, 0)
    values = vector_ref[...].astype(F32)
    values = jnp.where(core_ref[0] == 0, values[:8, :side], values[:8, side:])
    bias_ref[:, :side] = jnp.zeros((8, side), F32)
    bias_ref[:, side : 2 * side] = jnp.broadcast_to(values[VALUE_B : VALUE_B + 1], (8, side))
    bias_ref[:, 2 * side :] = jnp.broadcast_to(values[QUERY_B : QUERY_B + 1], (8, side))


def place_hidden_kernel(table_ref, mine_a_ref, other_a_ref, mine_d_ref, other_d_ref, expand_ref, reduce_ref):
    half = mine_a_ref.shape[0]
    rows, width = expand_ref.shape[1], mine_a_ref.shape[2]

    def body(j, carry):
        for a_ref, d_ref, at in ((mine_a_ref, mine_d_ref, j), (other_a_ref, other_d_ref, j + half)):
            chip = table_ref[at]
            for i in range(expand_ref.shape[2] // width):
                expand_ref[chip, :, i * width : (i + 1) * width] = a_ref[j, i * rows : (i + 1) * rows]
            reduce_ref[chip] = d_ref[j]
        return carry

    lax.fori_loop(0, half, body, 0)


def split_expand_kernel(table_ref, expand_ref, mine_ref, other_ref):
    half = mine_ref.shape[0]
    rows, width = expand_ref.shape[1], mine_ref.shape[2]

    def body(j, carry):
        for ref, at in ((mine_ref, j), (other_ref, j + half)):
            chip = table_ref[at]
            for i in range(expand_ref.shape[2] // width):
                ref[j, i * rows : (i + 1) * rows] = expand_ref[chip, :, i * width : (i + 1) * width]
        return carry

    lax.fori_loop(0, half, body, 0)


def split_reduce_kernel(table_ref, reduce_ref, mine_ref, other_ref):
    half = mine_ref.shape[0]

    def body(j, carry):
        mine_ref[j] = reduce_ref[table_ref[j]]
        other_ref[j] = reduce_ref[table_ref[j + half]]
        return carry

    lax.fori_loop(0, half, body, 0)


def split_attention_kernel(table_ref, kv_ref, q_ref, o_ref, mine_ref, other_ref):
    half = mine_ref.shape[0]
    rows, side = q_ref.shape[1], q_ref.shape[2]

    def body(j, carry):
        for ref, at in ((mine_ref, j), (other_ref, j + half)):
            chip = table_ref[at]
            ref[j, :rows] = kv_ref[chip]
            ref[j, rows:, :side] = q_ref[chip]
            ref[j, rows:, side:] = o_ref[chip]
        return carry

    lax.fori_loop(0, half, body, 0)


def fold_kernel(bit, keep_ref, got_ref, *out_refs):
    if len(out_refs) == 1:
        out_refs[0][...] = keep_ref[...].astype(F32) + got_ref[...].astype(F32)
        return
    low = 1 << bit
    for j in range(out_refs[0].shape[0]):
        block = j % low + j // low * 2 * low
        for i, ref in enumerate(out_refs):
            at = block + i * low
            ref[j] = (keep_ref[at].astype(F32) + got_ref[at].astype(F32)).astype(BF16)


def fold(keep, got, bit):
    blocks = keep.shape[0]
    out = shaped(keep.shape, F32) if blocks == 1 else (shaped((blocks // 2,) + keep.shape[1:], BF16),) * 2
    return call(functools.partial(fold_kernel, bit), "fold", out, keep, got)


def fold_mixed_kernel(core_ref, keep_ref, got_ref, *out_refs):
    core = core_ref[0]
    for j in range(4):
        low, high = j % 2, j // 2 * 4
        for i, ref in enumerate(out_refs):
            at = jnp.where(core == 0, high + low * 2 + i, high + low + 2 * i)
            ref[j] = (keep_ref[at].astype(F32) + got_ref[at].astype(F32)).astype(BF16)


def fold_vectors_kernel(bit, keep_ref, got_ref, vector_ref, *out_refs):
    rows = keep_ref.shape[0]
    vectors = vector_ref[...] + got_ref[rows:, :].astype(F32)
    out_refs[-1][...] = vectors
    if len(out_refs) == 2:
        out_refs[0][...] = keep_ref[...].astype(F32) + got_ref[:rows, :].astype(F32)
        return
    bit, blocks = bit
    size, low = rows // blocks, 1 << bit
    for j in range(blocks // 2):
        block = j % low + j // low * 2 * low
        for i in range(2):
            at = (block + i * low) * size
            total = keep_ref[at : at + size, :].astype(F32) + got_ref[at : at + size, :].astype(F32)
            out_refs[i][j * size : (j + 1) * size, :] = total.astype(BF16)
    out_refs[1][rows // 2 :, :] = vectors.astype(BF16)


def fold_vectors(keep, got, vectors, bit):
    rows, width = keep.shape
    if bit is None:
        out = (shaped((rows, width), F32), shaped(vectors.shape, F32))
    else:
        out = (
            shaped((rows // 2, width), BF16),
            shaped((rows // 2 + VECTOR_ROWS, width), BF16),
            shaped(vectors.shape, F32),
        )
    return call(functools.partial(fold_vectors_kernel, bit), "fold_vectors", out, keep, got, vectors)


def project_kernel(mine_ref, other_ref, weight_ref, bias_ref, out_ref):
    width = weight_ref.shape[1]
    bias = bias_ref[:1, :width]

    @pl.when(pl.program_id(0) == 0)
    def _():
        out_ref[...] = (dot(mine_ref[...], weight_ref[...]) + bias).astype(BF16)

    @pl.when(pl.program_id(0) == 1)
    def _():
        out_ref[...] = (dot(other_ref[...], weight_ref[...]) + bias).astype(BF16)


def project(mine, other, weight, bias):
    rows, width = mine.shape
    step = min(rows, 512)
    steps = rows // step
    return pl.pallas_call(
        project_kernel,
        out_shape=shaped((2 * rows, width), BF16),
        grid=(2, steps),
        in_specs=[
            pl.BlockSpec((step, width), lambda i, j: (jnp.where(i == 0, j, steps - 1), 0)),
            pl.BlockSpec((step, width), lambda i, j: (jnp.where(i == 0, 0, j), 0)),
            pl.BlockSpec(weight.shape, lambda i, j: (0, 0)),
            pl.BlockSpec(bias.shape, lambda i, j: (0, 0)),
        ],
        out_specs=pl.BlockSpec((step, width), lambda i, j: (i * steps + j, 0)),
        cost_estimate=COST,
        compiler_params=limit(2 * rows, 20),
        name="project",
    )(mine, other, weight, bias)


def head_scores(half, query, key, mask):
    column = lax.broadcasted_iota(jnp.int32, (1, 2 * HEAD_DIM), 1)
    here = (column < HEAD_DIM) if half == 0 else (column >= HEAD_DIM)
    one = (column == HEAD_DIM * (1 - half)).astype(F32).astype(BF16)
    return times_transpose(jnp.where(here, key, mask), jnp.where(here, query, one))


def scaled(query):
    return (query.astype(F32) * 0.125).astype(BF16)


def attend_kernel(q_ref, k_ref, v_ref, mask_ref, out_ref, logs_ref):
    query = scaled(q_ref[...])
    outs = []
    for half in range(2):
        at = slice(half * HEAD_DIM, (half + 1) * HEAD_DIM)
        scores = head_scores(half, query, k_ref[...], mask_ref[...])
        top = jnp.max(scores, axis=0, keepdims=True)
        weights = jnp.exp(scores - top)
        total = jnp.sum(weights, axis=0, keepdims=True)
        outs.append(contract_rows(v_ref[:, at], weights.astype(BF16)) / total)
        logs_ref[0, half : half + 1, :] = top + jnp.log(total)
    out_ref[...] = jnp.transpose(jnp.concatenate(outs, 0))


def attend(query, keys, mask):
    rows, width = query.shape
    tokens = keys.shape[0]
    step = rows if tokens <= 4096 else 128
    pair = 2 * HEAD_DIM
    pairs = width // pair
    spec_q = pl.BlockSpec((step, pair), lambda h, i: (i, h))
    flops = 16 * rows * tokens * width
    return pl.pallas_call(
        attend_kernel,
        out_shape=(shaped((rows, width), F32), shaped((pairs, 8, rows), F32)),
        grid=(pairs, rows // step),
        in_specs=[
            spec_q,
            pl.BlockSpec((tokens, pair), lambda h, i: (0, h)),
            pl.BlockSpec((tokens, pair), lambda h, i: (0, h + pairs)),
            pl.BlockSpec((tokens, 128), lambda h, i: (0, 0)),
        ],
        out_specs=[spec_q, pl.BlockSpec((1, 8, step), lambda h, i: (h, 0, i))],
        cost_estimate=COST,
        compiler_params=limit(tokens, 28),
        name="attend",
    )(query, keys, keys, mask)


def attend_back_kernel(
    q_ref, k_ref, v_ref, g_ref, o_ref, logs_ref, mask_ref, dq_ref, dk_ref, dv_ref, bias_ref, dk_sum, dv_sum
):
    step = pl.program_id(0)
    column = lax.broadcasted_iota(jnp.int32, (1, 2 * HEAD_DIM), 1)
    low_query, none = scaled(q_ref[...]), jnp.zeros((), BF16)

    @pl.when(step == 0)
    def _():
        dk_sum[...] = jnp.zeros_like(dk_sum)
        dv_sum[...] = jnp.zeros_like(dv_sum)

    products = jnp.transpose(g_ref[...].astype(F32) * o_ref[...])
    grads, dk, dv = [], None, None
    for half in range(2):
        at = slice(half * HEAD_DIM, (half + 1) * HEAD_DIM)
        here = (column < HEAD_DIM) if half == 0 else (column >= HEAD_DIM)
        grad = jnp.where(here, g_ref[...], none)
        scores = head_scores(half, low_query, k_ref[...], mask_ref[...])
        probs = jnp.exp(scores - logs_ref[0, half : half + 1, :])
        dots = jnp.sum(products[at], axis=0, keepdims=True)
        grad_scores = (probs * (times_transpose(v_ref[...], grad) - dots)).astype(BF16)
        grads.append(contract_rows(k_ref[...], grad_scores)[at])
        dk_part = dot(grad_scores, jnp.where(here, q_ref[...], none))
        dv_part = dot(probs.astype(BF16), grad)
        if dk_sum.shape[0] > 4096:
            dk_sum[...] += dk_part
            dv_sum[...] += dv_part
        else:
            dk, dv = (dk_part, dv_part) if half == 0 else (dk + dk_part, dv + dv_part)
    if dk is not None:
        dk_sum[...] += dk
        dv_sum[...] += dv
    dq_ref[...] = jnp.transpose(jnp.concatenate(grads, 0) * 0.125).astype(BF16)

    @pl.when(step == pl.num_programs(0) - 1)
    def _():
        dk_ref[...] = (dk_sum[...] * 0.125).astype(BF16)
        dv_ref[...] = dv_sum[...].astype(BF16)
        bias_ref[...] = jnp.broadcast_to(columns(dv_sum[...]), bias_ref.shape)


def attend_back(which, query, keys, grad, attended, logs, mask):
    rows, width = query.shape
    tokens = keys.shape[0]
    step = rows if tokens <= 4096 else 128
    pair = 2 * HEAD_DIM
    pairs = width // pair
    single = {"pipeline_mode": pl.Buffered(1)} if tokens > 4096 else {}
    spec_q = pl.BlockSpec((step, pair), lambda i: (i, which))
    spec_dq = pl.BlockSpec((step, pair), lambda i: (i, 0))
    spec_k = pl.BlockSpec((tokens, pair), lambda i: (0, which), **single)
    spec_v = pl.BlockSpec((tokens, pair), lambda i: (0, which + pairs), **single)
    spec_dk = pl.BlockSpec((tokens, pair), lambda i: (0, 0))
    flops = 40 * rows * tokens * pair
    return pl.pallas_call(
        attend_back_kernel,
        out_shape=(
            shaped((rows, pair), BF16),
            shaped((tokens, pair), BF16),
            shaped((tokens, pair), BF16),
            shaped((8, pair), F32),
        ),
        grid=(rows // step,),
        in_specs=[
            spec_q,
            spec_k,
            spec_v,
            spec_q,
            spec_q,
            pl.BlockSpec((1, 8, step), lambda i: (which, 0, i)),
            pl.BlockSpec((tokens, 128), lambda i: (0, 0), **single),
        ],
        out_specs=[spec_dq, spec_dk, spec_dk, pl.BlockSpec((8, pair), lambda i: (0, 0))],
        scratch_shapes=[pltpu.VMEM((tokens, pair), F32), pltpu.VMEM((tokens, pair), F32)],
        cost_estimate=COST,
        compiler_params=limit(tokens, 28),
        name="attend_back",
    )(query, keys, keys, grad, attended, logs, mask)


def keys_inputs_kernel(*refs):
    *part_refs, own_ref, weight_ref, out_ref = refs
    total = None
    for i, ref in enumerate(part_refs):
        width = ref.shape[1]
        if i % 2:
            continue
        both = jnp.concatenate([ref[...], part_refs[i + 1][...]], axis=1)
        term = times_transpose(both, weight_ref[:, i * width : (i + 2) * width])
        total = term if total is None else total + term
    out_ref[...] = total.astype(BF16)

    @pl.when(pl.program_id(0) == 0)
    def _():
        rows = own_ref.shape[0]
        out_ref[:rows, :] = (total[:rows] + own_ref[...]).astype(BF16)


def keys_inputs(which, parts, own, weight):
    tokens, pair = parts[0].shape
    tokens //= 2
    width = weight.shape[0]
    step = min(tokens, 512)
    spec = pl.BlockSpec((step, pair), lambda i: (i + which * (tokens // step), 0))
    whole = [pl.BlockSpec(v.shape, lambda i: (0, 0)) for v in (own, weight)]
    return pl.pallas_call(
        keys_inputs_kernel,
        out_shape=shaped((tokens, width), BF16),
        grid=(tokens // step,),
        in_specs=[spec] * len(parts) + whole,
        out_specs=pl.BlockSpec((step, width), lambda i: (i, 0)),
        cost_estimate=COST,
        compiler_params=limit(tokens, 20),
        name="keys_inputs",
    )(*parts, own, weight)


def keys_weights_kernel(table_ref, mine_ref, other_ref, q_ref, o_ref, *refs):
    *part_refs, keep_ref, send_ref, sum_ref, held_ref = refs
    first = (pl.program_id(0) == 0) & (pl.program_id(1) == 0)
    last = (pl.program_id(0) == 1) & (pl.program_id(1) == pl.num_programs(1) - 1)
    both = jnp.concatenate([ref[...] for ref in part_refs], axis=1)
    chips, rows, width = held_ref.shape
    half, side = chips // 2, width // 2

    @pl.when(first)
    def _():
        sum_ref[...] = contract_rows(mine_ref[...], both)

    @pl.when((pl.program_id(0) == 0) & (pl.program_id(1) > 0))
    def _():
        sum_ref[...] += contract_rows(mine_ref[...], both)

    @pl.when(pl.program_id(0) == 1)
    def _():
        sum_ref[...] += contract_rows(other_ref[...], both)

    @pl.when(last)
    def _():
        held_ref[...] = sum_ref[...].astype(BF16).reshape(held_ref.shape)

        def body(j, carry):
            for ref, at in ((keep_ref, j), (send_ref, j + half)):
                chip = table_ref[at]
                ref[j, :rows] = held_ref[chip]
                ref[j, rows:, :side] = q_ref[chip]
                ref[j, rows:, side:] = o_ref[chip]
            return carry

        lax.fori_loop(0, half, body, 0)


def flat_keys_weights_kernel(mine_ref, other_ref, *refs):
    *part_refs, grad_ref, sum_ref = refs
    first = (pl.program_id(0) == 0) & (pl.program_id(1) == 0)
    last = (pl.program_id(0) == 1) & (pl.program_id(1) == pl.num_programs(1) - 1)
    both = jnp.concatenate([ref[...] for ref in part_refs], axis=1)

    @pl.when(first)
    def _():
        sum_ref[...] = jnp.zeros_like(sum_ref)

    @pl.when(pl.program_id(0) == 0)
    def _():
        sum_ref[...] += contract_rows(mine_ref[...], both)

    @pl.when(pl.program_id(0) == 1)
    def _():
        sum_ref[...] += contract_rows(other_ref[...], both)

    @pl.when(last)
    def _():
        grad_ref[...] = sum_ref[...].astype(BF16)


def keys_weights(table, mine, other, grad_q, grad_o, parts):
    rows, width = mine.shape
    pair = parts[0].shape[1]
    chips, own = grad_q.shape[:2]
    step = min(rows, 512)
    steps = rows // step
    fused = own % 16 == 0
    block = shaped((chips // 2, 2 * own, width), BF16)
    tokens = [
        pl.BlockSpec((step, width), lambda i, j, *t: (jnp.where(i == 0, j, steps - 1), 0)),
        pl.BlockSpec((step, width), lambda i, j, *t: (jnp.where(i == 0, 0, j), 0)),
    ]
    spec = pl.BlockSpec((step, pair), lambda i, j, *t: (i * steps + j, 0))
    whole = pl.BlockSpec((chips, own, width // 2), lambda i, j, *t: (0, 0, 0))
    blocks = pl.BlockSpec(block.shape, lambda i, j, *t: (0, 0, 0))
    cost = COST
    if fused:
        return pl.pallas_call(
            keys_weights_kernel,
            out_shape=(block, block),
            grid_spec=pltpu.PrefetchScalarGridSpec(
                num_scalar_prefetch=1,
                grid=(2, steps),
                in_specs=tokens + [whole, whole] + [spec] * len(parts),
                out_specs=[blocks, blocks],
                scratch_shapes=[pltpu.VMEM((width, width), F32), pltpu.VMEM((chips, own, width), BF16)],
            ),
            cost_estimate=cost,
            compiler_params=limit(2 * rows, 24),
            name="keys_weights",
        )(table, mine, other, grad_q, grad_o, *parts)
    grad = pl.pallas_call(
        flat_keys_weights_kernel,
        out_shape=shaped((width, width), BF16),
        grid=(2, steps),
        in_specs=tokens + [spec] * len(parts),
        out_specs=pl.BlockSpec((width, width), lambda i, j: (0, 0)),
        scratch_shapes=[pltpu.VMEM((width, width), F32)],
        cost_estimate=cost,
        name="keys_weights",
    )(mine, other, *parts)
    return call(
        split_attention_kernel,
        "split_attention",
        (block, block),
        table,
        grad.reshape(chips, own, width),
        grad_q,
        grad_o,
        scalars=1,
    )


def normalize(values):
    center = values - jnp.mean(values, axis=-1, keepdims=True)
    scale = lax.rsqrt(jnp.mean(center * center, axis=-1, keepdims=True) + EPSILON)
    return center * scale, scale


def normalize_back(grad, normal, scale):
    return scale * (
        grad
        - jnp.mean(grad, axis=-1, keepdims=True)
        - normal * jnp.mean(grad * normal, axis=-1, keepdims=True)
    )


def row(ref, which):
    return ref[which : which + 1, :].astype(F32)


def columns(values):
    return jnp.sum(values, axis=0, keepdims=True)


def output_kernel(
    core_ref, inputs_ref, mine_ref, other_ref, near_ref, far_ref, vector_ref, normal_ref, scale_ref, low_ref
):
    side = mine_ref.shape[1]
    core = core_ref[0]
    here, there = pl.ds(core * side, side), pl.ds((1 - core) * side, side)

    def product(ref):
        return dot(mine_ref[...], ref[here, :]) + dot(other_ref[...], ref[there, :])

    near, far = product(near_ref), product(far_ref)
    even = core == 0
    hidden = jnp.concatenate([jnp.where(even, near, far), jnp.where(even, far, near)], axis=1)
    hidden = inputs_ref[...].astype(F32) + hidden + row(vector_ref, OUTPUT_B)
    normal, scale = normalize(hidden)
    normal_ref[...] = normal
    scale_ref[...] = jnp.broadcast_to(scale, scale_ref.shape)
    low_ref[...] = (normal * row(vector_ref, GAIN_1) + row(vector_ref, SHIFT_1)).astype(BF16)


def hidden_kernel(
    mine_ref, other_ref, normal_ref, expand_ref, reduce_ref, vector_ref, active_ref, slope_ref, base_ref, far_ref,
    active_held, slope_held, base_held, sems,
):
    rows = mine_ref.shape[0]
    width = mine_ref.shape[1]
    both = jnp.concatenate([mine_ref[...], other_ref[...]], axis=0)
    total, copies = None, []
    for i in range(expand_ref.shape[1] // width):
        at = slice(i * width, (i + 1) * width)
        value = dot(both, expand_ref[:, at]) + row(vector_ref, EXPAND_B + i)
        normal = 0.5 + 0.5 * lax.erf(value * np.float32(0.7071067811865476))
        active = (value * normal).astype(BF16)
        active_held[:, at] = active
        density = jnp.exp(value * value * -0.5) * np.float32(0.3989422804014327)
        slope_held[:, at] = (normal + value * density).astype(BF16)
        for j, (held, ref) in enumerate(((active_held, active_ref), (slope_held, slope_ref))):
            copies.append(pltpu.make_async_copy(held.at[:, at], ref.at[:, at], sems.at[2 * i + j]))
            copies[-1].start()
        term = dot(active, reduce_ref[at, :])
        total = term if total is None else total + term
    middle = normal_ref[...] * row(vector_ref, GAIN_1) + row(vector_ref, SHIFT_1)
    base_held[...] = middle + total[:rows] + row(vector_ref, REDUCE_B)
    copies.append(pltpu.make_async_copy(base_held, base_ref, sems.at[len(copies)]))
    copies[-1].start()
    far_ref[...] = total[rows:].astype(BF16)
    for copy in copies:
        copy.wait()


def final_kernel(
    start_ref, base_ref, far_ref, cotangent_ref, vector_ref, out_ref, grad_ref, low_ref, sums_ref
):
    combined = base_ref[...] + far_ref[...].astype(F32)
    normal, scale = normalize(combined)
    gain = row(vector_ref, GAIN_2)
    out_ref[...] = (normal * gain + row(vector_ref, SHIFT_2)).astype(BF16)
    place = start_ref[0] + lax.broadcasted_iota(jnp.int32, combined.shape, 0)
    upstream = jnp.where(place < start_ref[1], cotangent_ref[...].astype(F32), 0.0)
    grad = normalize_back(upstream * gain, normal, scale)
    grad_ref[...] = grad
    low_ref[...] = grad.astype(BF16)
    sums_ref[...] = jnp.zeros_like(sums_ref)
    sums_ref[REDUCE_B : REDUCE_B + 1, :] = columns(grad)
    sums_ref[GAIN_2 : GAIN_2 + 1, :] = columns(upstream * normal)
    sums_ref[SHIFT_2 : SHIFT_2 + 1, :] = columns(upstream)


def hidden_back_kernel(table_a_ref, table_d_ref, *refs):
    cl_mine_ref, cl_other_ref, *far = refs[:8]
    outs, held, sems = refs[8:15], refs[15:-1], refs[-1]
    copies = [pltpu.make_async_copy(i, h, sems.at[at]) for at, (i, h) in enumerate(zip(far, held))]
    for copy in copies:
        copy.start()
    active_ref, slope_ref, reduce_ref, expand_ref, mid_mine_ref, mid_other_ref = held[:6]
    near_ref, far_ref, sums_ref, d_keep_ref, d_send_ref, a_keep_ref, a_send_ref = outs
    d_held_ref, a_held_ref, low_ref = held[6:]
    rows, width = cl_mine_ref.shape
    times = expand_ref.shape[1] // width
    both = jnp.concatenate([cl_mine_ref[...], cl_other_ref[...]], axis=0)
    sums_ref[...] = jnp.zeros_like(sums_ref)
    copies[0].wait()
    units = d_held_ref.shape[1]
    for i in range(times):
        part = contract_rows(active_ref[:, i * width : (i + 1) * width], both).astype(BF16)
        d_held_ref[i * width // units : (i + 1) * width // units] = part.reshape(width // units, units, width)
    split_reduce_kernel(table_d_ref, d_held_ref, d_keep_ref, d_send_ref)
    for copy in copies[1:3]:
        copy.wait()
    total = None
    for i in range(times):
        at = slice(i * width, (i + 1) * width)
        active = times_transpose(both, reduce_ref[at, :]).astype(BF16)
        grad = (active.astype(F32) * slope_ref[:, at].astype(F32)).astype(BF16)
        low_ref[:, at] = grad
        sums_ref[i : i + 1, :] = columns(grad.astype(F32))
    copies[3].wait()
    for i in range(times):
        at = slice(i * width, (i + 1) * width)
        term = times_transpose(low_ref[:, at], expand_ref[:, at])
        total = term if total is None else total + term
    near_ref[...] = total[:rows]
    far_ref[...] = total[rows:].astype(BF16)
    for copy in copies[4:]:
        copy.wait()
    mid = jnp.concatenate([mid_mine_ref[...], mid_other_ref[...]], axis=0)
    own = a_held_ref.shape[1]
    for i in range(times):
        at = slice(i * width, (i + 1) * width)
        a_held_ref[:, :, at] = contract_rows(mid, low_ref[:, at]).astype(BF16).reshape(width // own, own, width)
    split_expand_kernel(table_a_ref, a_held_ref, a_keep_ref, a_send_ref)


def hidden_back_plain_kernel(mine_ref, other_ref, expand_ref, reduce_ref, slope_ref, low_ref, near_ref, far_ref, sums_ref):
    rows, width = mine_ref.shape
    both = jnp.concatenate([mine_ref[...], other_ref[...]], axis=0)
    total = None
    sums_ref[...] = jnp.zeros_like(sums_ref)
    for i in range(expand_ref.shape[1] // width):
        at = slice(i * width, (i + 1) * width)
        active = times_transpose(both, reduce_ref[at, :]).astype(BF16)
        grad = (active.astype(F32) * slope_ref[:, at].astype(F32)).astype(BF16)
        low_ref[:, at] = grad
        sums_ref[i : i + 1, :] = columns(grad.astype(F32))
        term = times_transpose(grad, expand_ref[:, at])
        total = term if total is None else total + term
    near_ref[...] = total[:rows]
    far_ref[...] = total[rows:].astype(BF16)


def hidden_back(table_a, table_d, low, low_other, active, slope, reduce, expand, middle, middle_other, units):
    rows, width = low.shape
    hidden_units = reduce.shape[0]
    chips, own, times = hidden_units // units, width * units // hidden_units, hidden_units // width
    far = [active, slope, reduce, expand, middle, middle_other]
    far = [pltpu.with_memory_space_constraint(v, pltpu.HBM) for v in far]
    return pl.pallas_call(
        hidden_back_kernel,
        out_shape=(
            shaped((rows, width), F32),
            shaped((rows, width), BF16),
            shaped((8, width), F32),
            *(shaped((chips // 2, units, width), BF16),) * 2,
            *(shaped((chips // 2, times * own, width), BF16),) * 2,
        ),
        in_specs=[SMEM] * 2 + [VMEM] * 2 + [pl.BlockSpec(memory_space=pltpu.HBM)] * len(far),
        out_specs=(VMEM,) * 7,
        scratch_shapes=[
            *[pltpu.VMEM(v.shape, v.dtype) for v in far],
            pltpu.VMEM((chips, units, width), BF16),
            pltpu.VMEM((chips, own, hidden_units), BF16),
            pltpu.VMEM((2 * rows, hidden_units), BF16),
            pltpu.SemaphoreType.DMA((len(far),)),
        ],
        cost_estimate=COST,
        compiler_params=pltpu.CompilerParams(vmem_limit_bytes=24 << 20),
        name="hidden_back",
    )(table_a, table_d, low, low_other, *far)


def reduce_grads_kernel(low_mine_ref, low_other_ref, active_ref, grad_ref):
    width = low_mine_ref.shape[1]
    low = jnp.concatenate([low_mine_ref[...], low_other_ref[...]], axis=0)
    for i in range(active_ref.shape[1] // width):
        at = slice(i * width, (i + 1) * width)
        grad_ref[at, :] = contract_rows(active_ref[:, at], low).astype(BF16)


def expand_grads_kernel(mid_mine_ref, mid_other_ref, low_ref, grad_ref):
    width = mid_mine_ref.shape[1]
    mid = jnp.concatenate([mid_mine_ref[...], mid_other_ref[...]], axis=0)
    for i in range(low_ref.shape[1] // width):
        at = slice(i * width, (i + 1) * width)
        grad_ref[:, at] = contract_rows(mid, low_ref[:, at]).astype(BF16)


def output_back_kernel(
    core_ref, normal_ref, scale_ref, grad_ref, near_sum_ref, far_sum_ref, near_ref, far_ref, vector_ref,
    hidden_ref, low_ref, mine_ref, other_ref, sums_ref,
):
    side = near_ref.shape[1]
    core = core_ref[0]
    even = core == 0
    normal = normal_ref[...]
    grad_middle = grad_ref[...] + near_sum_ref[...] + far_sum_ref[...].astype(F32)
    grad = normalize_back(grad_middle * row(vector_ref, GAIN_1), normal, scale_ref[:, :1])
    hidden_ref[...] = grad
    low = grad.astype(BF16)
    low_ref[...] = low
    low_near = jnp.where(even, low[:, :side], low[:, side:])
    low_far = jnp.where(even, low[:, side:], low[:, :side])
    here, there = pl.ds(core * side, side), pl.ds((1 - core) * side, side)

    def product(rows):
        return times_transpose(low_near, near_ref[rows, :]) + times_transpose(low_far, far_ref[rows, :])

    mine_ref[...] = product(here).astype(BF16)
    other_ref[...] = product(there).astype(BF16)
    sums_ref[...] = jnp.zeros_like(sums_ref)
    sums_ref[OUTPUT_B : OUTPUT_B + 1, :] = columns(grad)
    sums_ref[GAIN_1 : GAIN_1 + 1, :] = columns(grad_middle * normal)
    sums_ref[SHIFT_1 : SHIFT_1 + 1, :] = columns(grad_middle)


def output_grads_kernel(core_ref, mine_ref, other_ref, low_ref, near_ref, far_ref):
    side = mine_ref.shape[1]
    core = core_ref[0]
    even = core == 0
    here, there = pl.ds(core * side, side), pl.ds((1 - core) * side, side)
    for rows, ref in ((here, mine_ref), (there, other_ref)):
        product = contract_rows(ref[...], low_ref[...])
        near_ref[rows, :] = jnp.where(even, product[:, :side], product[:, side:])
        far_ref[rows, :] = jnp.where(even, product[:, side:], product[:, :side]).astype(BF16)


def join_units(units, even, mine_ref, other_ref, out_ref):
    times, width = mine_ref.shape[0], mine_ref.shape[2]
    for i in range(times):
        mine, other = mine_ref[i], other_ref[2 + i]
        parts = (jnp.where(even, mine, other), jnp.where(even, other, mine))
        for j in range(width // units):
            at = (i * (width // units) + j) * 2 * units
            for k, part in enumerate(parts):
                out_ref[:, at + k * units : at + (k + 1) * units] = part[:, j * units : (j + 1) * units]


def finish_kernel(units, number_ref, mine_ref, expand_ref, other_ref, sums_ref, expand_out_ref, *out_refs):
    side = mine_ref.shape[2] // 2
    even = number_ref[0] % 2 == 0
    for i, ref in enumerate(out_refs[:4]):
        at = slice(i % 2 * side, (i % 2 + 1) * side)
        mine, other = mine_ref[i // 2, :, at], other_ref[i // 2, :, at]
        ref[:, :side] = jnp.where(even, mine, other)
        ref[:, side:] = jnp.where(even, other, mine)
    join_units(units, even, expand_ref, other_ref, expand_out_ref)
    unpack_vectors(number_ref, sums_ref, out_refs[4:])


def query_back_kernel(mine_ref, other_ref, weight_ref, *refs):
    *dq_refs, near_ref, far_ref, grad_ref, sums_ref = refs
    rows = mine_ref.shape[0]
    grads = jnp.concatenate([ref[...] for ref in dq_refs], axis=1)
    product = times_transpose(grads, weight_ref[...])
    near_ref[...] = product[:rows]
    far_ref[...] = product[rows:]
    both = jnp.concatenate([mine_ref[...], other_ref[...]], axis=0)
    grad_ref[...] = contract_rows(both, grads).astype(BF16)
    sums_ref[...] = jnp.broadcast_to(columns(grads.astype(F32)), sums_ref.shape)


def body(
    layer_input,
    cotangent,
    lengths,
    query_weight,
    query_bias,
    key_weight,
    value_weight,
    value_bias,
    output_weight,
    output_bias,
    attn_gain,
    attn_shift,
    expand_weight,
    expand_bias,
    reduce_weight,
    reduce_bias,
    final_gain,
    final_shift,
):
    place = Place()
    core = place.core
    core_s = core.reshape(1)
    number_s = place.number.reshape(1)
    chips = place.count // 2
    inputs = layer_input[0]
    rows, width = inputs.shape
    side = width // 2
    own = query_weight.shape[0]
    units = reduce_weight.shape[0]
    hidden_units = units * chips
    times = hidden_units // width
    length = lengths[0]
    even = core == 0

    masks = [place.others(place.weight_stages, k) for k in range(2)]
    usual = len(place.weight_stages) == 4 and len(place.token_stages) == 3
    turns = WEIGHT_TURNS if usual else {}

    def chip_table(bit=None):
        blocks = np.arange(chips)
        if bit is not None:
            blocks = np.concatenate([blocks[blocks >> bit & 1 == i] for i in range(2)])
        return (place.number ^ jnp.where(even, masks[0][blocks], masks[1][blocks])) // 2

    def first_bit(name):
        return turns[name][0] if name in turns else len(place.weight_stages) - 1

    table = chip_table()
    token_masks = [place.others(place.token_stages, k) for k in range(2)]
    near_ctx = place.context ^ jnp.where(even, token_masks[0], token_masks[1])
    far_ctx = (place.context ^ 1) ^ jnp.where(even, token_masks[1], token_masks[0])
    blocks = jnp.concatenate([near_ctx, far_ctx])
    positions = (blocks[:, None] * rows + jnp.arange(rows, dtype=jnp.int32)).reshape(-1, 1)
    mask = jnp.where(positions < length, 0.0, MASKED).astype(BF16)
    mask = jnp.where(jnp.arange(2 * HEAD_DIM) % HEAD_DIM == 0, mask, 0)

    def joined(mine, other):
        return jnp.where(
            even, jnp.concatenate([mine, other], 1), jnp.concatenate([other, mine], 1)
        ).reshape(-1, width)

    vector_list = [query_bias, value_bias, output_bias, attn_gain, attn_shift, reduce_bias, final_gain, final_shift]
    attention_mine, attention_other, expand_mine, expand_other, vectors = prepare(
        number_s,
        [key_weight, value_weight, query_weight, output_weight],
        expand_weight,
        vector_list + [expand_bias],
    )
    vector_swap = place.swap(vectors, 0)
    vectors = vectors + jnp.where(jnp.arange(VECTOR_ROWS)[:, None] < 8, vector_swap, 0)

    stages = place.weight_stages
    token_stages = place.token_stages
    order = Order(place, STRICT[0])

    other_inputs = place.swap(inputs, 0)
    attention_swapped = place.swap(attention_other, 0)
    if FIRST_WAITS:
        order.last = (attention_swapped,)
    attention_blocks = Gather(order, joined(attention_mine, attention_swapped), stages, vectors)
    block_rows = attention_blocks.held.shape[0]
    expand_rows = joined(expand_mine, place.swap(expand_other, 0))
    expand_blocks = Gather(order, expand_rows[None], stages)
    reduce_blocks = Gather(order, reduce_weight[None], stages)
    token_blocks = Gather(order, inputs[None], token_stages)
    chains = {"X": token_blocks, "B": attention_blocks, "A": expand_blocks, "D": reduce_blocks}
    play(FORWARD[0] if usual else plain_events(chains), chains)

    aligned = (2 * own) % 16 == 0
    tile = 16 if aligned else 2 * own

    def tiles(array):
        array = array if aligned else array[: array.shape[0] // block_rows * block_rows]
        return array.reshape(-1, tile, width)

    weights_kv, weights_q, output_near, bias = call(
        place_attention_kernel,
        "place_attention",
        (
            shaped((chips, 2 * own, width), BF16),
            shaped((chips, 2 * own, side), BF16),
            shaped((chips, 2 * own, side), BF16),
            shaped((8, 3 * side), F32),
        ),
        table,
        core_s,
        tiles(attention_blocks.held),
        tiles(attention_blocks.got),
        attention_blocks.vectors,
        scalars=2,
    )
    vectors = attention_blocks.vectors
    weights_kv = weights_kv.reshape(width, width)
    weights_q = weights_q.reshape(width, side)
    output_near = output_near.reshape(width, side)
    if usual:
        play(FORWARD[1], chains)

    sequence_near = jnp.concatenate([token_blocks.held, token_blocks.got]).reshape(-1, width)
    sequence_far = place.swap(sequence_near, 0)
    keys = project(sequence_near, sequence_far, weights_kv, bias)
    if usual:
        play(FORWARD[2], chains)
    query = jnp.concatenate([inputs, other_inputs])
    query = (dot(query, weights_q) + bias[:1, 2 * side :]).astype(BF16)
    attended, logs = attend(query, keys, mask)
    if usual:
        play(FORWARD[3], chains)
    output_far = place.swap(output_near, 0)
    expand_matrix, reduce_matrix = call(
        place_hidden_kernel,
        "place_hidden",
        (shaped((chips, 2 * own, hidden_units), BF16), shaped((chips, units, width), BF16)),
        table,
        expand_blocks.held,
        expand_blocks.got,
        reduce_blocks.held,
        reduce_blocks.got,
        scalars=1,
    )
    expand_matrix = expand_matrix.reshape(width, hidden_units)
    reduce_matrix = reduce_matrix.reshape(hidden_units, width)
    attended_low = attended.astype(BF16)
    attended_mine = attended_low[:rows]
    attended_other = place.swap(attended_low[rows:], 0)

    normal_one, scale_one, middle_low = call(
        output_kernel,
        "output",
        (shaped((rows, width), F32), shaped((rows, 128), F32), shaped((rows, width), BF16)),
        core_s,
        Far(inputs),
        attended_mine,
        attended_other,
        Far(output_near),
        output_far,
        Far(vectors),
        scalars=1,
    )

    middle_other = place.swap(middle_low, 0)
    active, slope, base, far = call(
        hidden_kernel,
        "hidden",
        (
            shaped((2 * rows, hidden_units), BF16),
            shaped((2 * rows, hidden_units), BF16),
            shaped((rows, width), F32),
            shaped((rows, width), BF16),
        ),
        middle_low,
        middle_other,
        normal_one,
        expand_matrix,
        reduce_matrix,
        vectors,
        scratch=[
            pltpu.VMEM((2 * rows, hidden_units), BF16),
            pltpu.VMEM((2 * rows, hidden_units), BF16),
            pltpu.VMEM((rows, width), F32),
            pltpu.SemaphoreType.DMA((2 * times + 1,)),
        ],
        stored=(0, 1, 2),
    )
    far = place.swap(far, 0)
    start_s = jnp.stack([place.context * rows, length])
    layer_output, grad_combined, combined_low, sums_two = call(
        final_kernel,
        "final",
        (
            shaped((rows, width), BF16),
            shaped((rows, width), F32),
            shaped((rows, width), BF16),
            shaped((8, width), F32),
        ),
        start_s,
        Far(base),
        far,
        Far(cotangent[0]),
        Far(vectors),
        scalars=1,
        room=8,
    )
    combined_other = place.swap(combined_low, 0)
    table_d, table_a = chip_table(first_bit("D")), chip_table(first_bit("A"))
    if (2 * own) % 16 == 0:
        near, far, sums_expand, reduce_keep, reduce_send, expand_keep, expand_send = hidden_back(
            table_a,
            table_d,
            combined_low,
            combined_other,
            active,
            slope,
            reduce_matrix,
            expand_matrix,
            middle_low,
            middle_other,
            units,
        )
    else:
        grad_expanded, near, far, sums_expand = call(
            hidden_back_plain_kernel,
            "hidden_back",
            (
                shaped((2 * rows, hidden_units), BF16),
                shaped((rows, width), F32),
                shaped((rows, width), BF16),
                shaped((8, width), F32),
            ),
            combined_low,
            combined_other,
            expand_matrix,
            reduce_matrix,
            slope,
        )
        grads = call(
            reduce_grads_kernel,
            "reduce_grads",
            shaped((hidden_units, width), BF16),
            combined_low,
            combined_other,
            active,
        )
        out = (shaped((chips // 2, units, width), BF16),) * 2
        reduce_keep, reduce_send = call(
            split_reduce_kernel, "split_reduce", out, table_d, grads.reshape(chips, units, width), scalars=1
        )
        grads = call(
            expand_grads_kernel,
            "expand_grads",
            shaped((width, hidden_units), BF16),
            middle_low,
            middle_other,
            grad_expanded,
        )
        out = (shaped((chips // 2, times * 2 * own, width), BF16),) * 2
        expand_keep, expand_send = call(
            split_expand_kernel, "split_expand", out, table_a, grads.reshape(chips, 2 * own, hidden_units), scalars=1
        )
    far = place.swap(far, 0)

    grad_hidden, hidden_low, grad_mine, grad_other, sums_one = call(
        output_back_kernel,
        "output_back",
        (
            shaped((rows, width), F32),
            shaped((rows, width), BF16),
            shaped((rows, side), BF16),
            shaped((rows, side), BF16),
            shaped((8, width), F32),
        ),
        core_s,
        Far(normal_one),
        Far(scale_one),
        grad_combined,
        near,
        far,
        Far(output_near),
        Far(output_far),
        Far(vectors),
        scalars=1,
    )
    grad_heads = jnp.concatenate([grad_mine, place.swap(grad_other, 0)])
    output_near_grad, output_far_grad = call(
        output_grads_kernel,
        "output_grads",
        (shaped((width, side), F32), shaped((width, side), BF16)),
        core_s,
        Far(attended_mine),
        Far(attended_other),
        hidden_low,
        scalars=1,
    )
    grad_output = (output_near_grad + place.swap(output_far_grad, 0).astype(F32)).astype(BF16)

    def own_half(array, axis):
        first, second = lax.index_in_dim(array, 0, axis, False), lax.index_in_dim(array, 1, axis, False)
        return jnp.where(even, first, second), jnp.where(even, second, first)

    order = Order(place, STRICT[1])
    chains = {
        "D": Scatter(order, reduce_keep, reduce_send, stages, turn=turns.get("D")),
        "A": Scatter(order, expand_keep, expand_send, stages, turn=turns.get("A")),
    }
    if usual:
        play("DA", chains)

    def held_back(kernel, array):
        return order.wait(array) if usual and WAITS[kernel] else array

    parts = []
    pairs = side // (2 * HEAD_DIM)
    for which in range(pairs):
        parts.append(attend_back(which, held_back(which, query), keys, grad_heads, attended, logs, mask))
        if usual:
            play(BACKWARD[which], chains)
    grad_query, grad_keys, grad_values, value_bias_sums = zip(*parts)
    parts = grad_keys + grad_values
    near, far, grad_query_w, query_bias_sum = call(
        query_back_kernel,
        "query_back",
        (
            shaped((rows, width), F32),
            shaped((rows, width), F32),
            shaped((width, side), BF16),
            shaped((8, side), F32),
        ),
        Far(inputs),
        Far(other_inputs),
        Far(weights_q),
        *grad_query,
    )
    query_near, query_far = near, far

    mine_rows = jnp.stack([query_bias_sum[0], jnp.concatenate([v[0] for v in value_bias_sums])])
    zero = jnp.zeros_like(mine_rows)
    mine_rows = jnp.where(even, jnp.concatenate([mine_rows, zero], 1), jnp.concatenate([zero, mine_rows], 1))
    vector_sums = jnp.concatenate([mine_rows, (sums_one + sums_two)[2:], sums_expand])
    vector_swap = place.swap(vector_sums, 0)
    vector_sums = vector_sums + jnp.where(jnp.arange(VECTOR_ROWS)[:, None] < 8, vector_swap, 0)

    far_part = keys_inputs(1, (held_back(4, parts[0]), *parts[1:]), query_far, weights_kv)
    far_got = place.swap(far_part, 0)
    near_part = keys_inputs(0, (held_back(5, parts[0]), *parts[1:]), query_near, weights_kv)
    blocks_shape = (sequence_near.shape[0] // rows, rows, width)
    near_part, far_part = near_part.reshape(blocks_shape), far_got.reshape(blocks_shape)
    if usual and TOKEN_TURN == "mix":
        half_shape = (blocks_shape[0] // 2,) + blocks_shape[1:]
        x_keep, x_send = call(
            fold_mixed_kernel, "fold_mixed", (shaped(half_shape, BF16),) * 2, core_s, near_part, far_part, scalars=1
        )
        (near_even, near_odd), (even_bit, odd_bit), last_stage = token_stages
        mixed = [(even_bit, near_odd), last_stage, (near_even, odd_bit)]
        chains["X"] = Scatter(order, x_keep, x_send, mixed)
    else:
        turn = range(len(token_stages))[::-1]
        if usual:
            kinds = "ab"[:TOKEN_NEAR] + "y" + "ab"[TOKEN_NEAR:]
            turn = [kinds.index(kind) for kind in TOKEN_TURN]
        x_keep, x_send = fold(near_part, far_part, turn[0])
        chains["X"] = Scatter(order, x_keep, x_send, token_stages, turn=turn)
    if usual:
        play(BACKWARD[3], chains)

    inputs_first = (x_send,) if usual and INPUTS_FIRST else ()
    keep, send = keys_weights(
        chip_table(first_bit("B")),
        after(held_back(3, sequence_near), *inputs_first),
        sequence_far,
        grad_query_w.reshape(chips, 2 * own, side),
        grad_output.reshape(chips, 2 * own, side),
        parts,
    )
    keep = keep.reshape(-1, width)
    send = jnp.concatenate([send.reshape(-1, width), vector_sums.astype(BF16)])
    chains["B"] = Scatter(order, keep, send, stages, vector_sums, turns.get("B"))
    play(BACKWARD[4].rstrip("|b") if usual else plain_events(chains), chains)
    reduce_out = chains["D"].keep[0]
    expand_sum = chains["A"].keep[0].reshape(times, 2, own, width)
    input_grad = grad_hidden + chains["X"].keep[0]

    if usual:
        chains["B"].done(input_grad, *((reduce_out,) if REDUCE_FIRST else ()))
    keep, vector_sums = chains["B"].keep, chains["B"].vectors
    expand_mine, expand_other = own_half(expand_sum, 1)
    pieces = keep.reshape(2, 2, own, width)
    pieces_mine, pieces_other = own_half(pieces, 1)
    swapped = place.swap(jnp.concatenate([pieces_other, expand_other]), 0)
    expand_out, *outs = call(
        functools.partial(finish_kernel, units),
        "finish",
        [shaped((own, 2 * hidden_units), F32)]
        + [shaped((own, width), F32)] * 4
        + [shaped((1, own), F32)] * 8
        + [shaped((1, units), F32)],
        number_s,
        pieces_mine,
        expand_mine,
        swapped,
        vector_sums,
        scalars=1,
    )
    weights_out, outs = outs[:4], outs[4:]
    outs = [v.reshape(-1) for v in outs]
    return (
        layer_output[None],
        input_grad[None],
        weights_out[2],
        outs[QUERY_B],
        weights_out[0],
        weights_out[1],
        outs[VALUE_B],
        weights_out[3],
        outs[OUTPUT_B],
        outs[GAIN_1],
        outs[SHIFT_1],
        expand_out,
        outs[EXPAND_B],
        reduce_out,
        outs[REDUCE_B],
        outs[GAIN_2],
        outs[SHIFT_2],
    )


def solution(mesh):
    tokens = P("seq", "ctx", None)
    matrix = P(("seq", "ctx"), None)
    vector = P(("seq", "ctx"))
    weights = (
        matrix,
        vector,
        matrix,
        matrix,
        vector,
        matrix,
        vector,
        vector,
        vector,
        matrix,
        vector,
        matrix,
        vector,
        vector,
        vector,
    )
    return jax.shard_map(
        body,
        mesh=mesh,
        in_specs=(tokens, tokens, P("seq")) + weights,
        out_specs=(tokens, tokens) + weights,
        check_vma=False,
    )
```

```python
import functools

import jax
import jax.numpy as jnp
import numpy as np
from jax import lax
from jax.experimental import pallas as pl
from jax.experimental.pallas import tpu as pltpu
from jax.sharding import PartitionSpec as P

HEADS = 12
HEAD_DIM = 64
EPSILON = 1e-12
MASKED = -1000000000.0
EVERY = ("seq", "ctx")
F32 = jnp.float32
BF16 = jnp.bfloat16
VMEM = pl.BlockSpec(memory_space=pltpu.VMEM)
SMEM = pl.BlockSpec(memory_space=pltpu.SMEM)
QUERY_B, VALUE_B, OUTPUT_B, GAIN_1, SHIFT_1, REDUCE_B, GAIN_2, SHIFT_2, EXPAND_B = range(9)
VECTOR_ROWS = 16
SMALL_BYTES = 16 << 20
COST = pl.CostEstimate(flops=1000, bytes_accessed=1000, transcendentals=0)
FORWARD = ('XBADbxad|BAba|BADXbadx|BDXbd|', 'xAD', '', 'ad|')
BACKWARD = ('', '', 'a|A', 'da|DX', '|AdBab|DABxadXbDBxd|XbB|xb')
TOKEN_NEAR = 0
TOKEN_TURN = 'mix'
WEIGHT_TURNS = {'D': (1, 0, 3, 2), 'A': (3, 2, 1, 0), 'B': (3, 2, 1, 0)}
WAITS = (False, False, True, False, False, False)
FIRST_WAITS = False
INPUTS_FIRST = False
REDUCE_FIRST = False
OUTPUT_FIRST = False
VECTORS_LATE = True
STRICT = (True, False)


def dot(left, right):
    return jnp.dot(left, right, preferred_element_type=F32)


def contract_rows(left, right):
    return lax.dot_general(left, right, (((0,), (0,)), ((), ())), preferred_element_type=F32)


def times_transpose(left, right):
    return lax.dot_general(left, right, (((1,), (1,)), ((), ())), preferred_element_type=F32)


def shaped(shape, dtype):
    return jax.ShapeDtypeStruct(tuple(shape), dtype)


def after(array, *earlier):
    return lax.optimization_barrier((array, *earlier))[0]


def in_hbm(array):
    return pltpu.with_memory_space_constraint(array, pltpu.HBM)


class Far:
    def __init__(self, array):
        self.array = array


def fetching(kernel, scalars, far, count, *refs):
    inputs, rest = list(refs[:count]), refs[count : len(refs) - len(far) - 1]
    held, sems = refs[len(refs) - len(far) - 1 : -1], refs[-1]
    copies = [pltpu.make_async_copy(inputs[at], room, sems.at[i]) for i, (at, room) in enumerate(zip(far, held))]
    for copy in copies:
        copy.start()
    for copy in copies:
        copy.wait()
    for at, room in zip(far, held):
        inputs[at] = room
    kernel(*inputs, *rest)


def call(kernel, name, outs, *args, scalars=0, scratch=(), room=16, stored=()):
    many = isinstance(outs, (tuple, list))
    far = [i for i, a in enumerate(args) if isinstance(a, Far)]
    args = [a.array if isinstance(a, Far) else a for a in args]
    flat = tuple(outs) if many else (outs,)
    small = sum(a.size * a.dtype.itemsize for a in (*args, *flat)) < SMALL_BYTES
    specs = [SMEM] * scalars + [VMEM] * (len(args) - scalars)
    scratch = list(scratch)
    if far and small:
        kernel = functools.partial(fetching, kernel, scalars, far, len(args))
        for at in far:
            specs[at] = pl.BlockSpec(memory_space=pltpu.HBM)
            args[at] = pltpu.with_memory_space_constraint(args[at], pltpu.HBM)
            scratch.append(pltpu.VMEM(args[at].shape, args[at].dtype))
        scratch.append(pltpu.SemaphoreType.DMA((len(far),)))
    out_specs = [VMEM] * len(flat)
    for at in stored:
        out_specs[at] = pl.BlockSpec(memory_space=pltpu.HBM)
        flat = flat[:at] + (pltpu.HBM(flat[at].shape, flat[at].dtype),) + flat[at + 1 :]
    return pl.pallas_call(
        kernel,
        out_shape=flat if many else flat[0],
        in_specs=specs,
        out_specs=tuple(out_specs) if many else out_specs[0],
        scratch_shapes=scratch,
        cost_estimate=COST,
        compiler_params=pltpu.CompilerParams(vmem_limit_bytes=room << 20 if small else None),
        name=name,
    )(*args)


def limit(tokens, mebibytes):
    return pltpu.CompilerParams(vmem_limit_bytes=mebibytes << 20 if tokens <= 4096 else None)


class Place:
    def __init__(self):
        self.ctx = lax.axis_size("ctx")
        self.count = lax.axis_size("seq") * self.ctx
        self.bits = self.count.bit_length() - 1
        self.context = lax.axis_index("ctx")
        self.number = lax.axis_index("seq") * self.ctx + self.context
        self.core = self.number & 1
        top = self.bits - 1
        middle = list(range(2, top))
        self.weight_stages = list(zip(middle[::-1], middle)) + [(1, top), (top, 1)]
        self.token_stages = list(zip(middle[::-1], middle))
        self.token_stages.insert(min(TOKEN_NEAR, len(middle)), (1, 1))

    def swap(self, array, even, odd=None):
        odd = even if odd is None else odd
        pairs = [(i, i ^ (1 << (odd if i & 1 else even))) for i in range(self.count)]
        return lax.ppermute(array, EVERY, pairs)

    def others(self, stages, core):
        masks = [0]
        for stage in stages:
            masks = masks + [m ^ (1 << stage[core]) for m in masks]
        return np.array(masks, np.int32)


class Order:
    def __init__(self, place, strict):
        self.place = place
        self.strict = strict
        self.last = ()
        self.ended = ()

    def close(self):
        if self.ended:
            self.last, self.ended = self.ended, ()

    def wait(self, array):
        return after(array, *self.last) if self.last else array

    def start(self, array, stage):
        return self.place.swap(self.wait(array), *stage)

    def done(self, got):
        used = self.wait(got) if self.strict else got
        self.ended += (got,)
        return used

    def ran(self, out):
        self.ended += (out,)
        return out


class Gather:
    def __init__(self, order, blocks, stages, vectors=None):
        self.order, self.held, self.stages, self.vectors = order, blocks, list(stages), vectors
        self.got = None

    def start(self):
        sent = self.held if self.vectors is None else jnp.concatenate([self.held, self.vectors])
        self.got = self.order.start(sent, self.stages.pop(0))

    def done(self):
        self.got = self.order.done(self.got)
        got = self.got
        if self.vectors is not None:
            self.vectors = self.vectors + got[-VECTOR_ROWS:]
            got = got[:-VECTOR_ROWS]
        if self.stages:
            self.held = jnp.concatenate([self.held, got])


class Scatter:
    def __init__(self, order, keep, send, stages, vectors=None, turn=None):
        self.order, self.keep, self.send, self.vectors = order, keep, send, vectors
        turn = list(range(len(stages)))[::-1] if turn is None else list(turn)
        self.stages = [stages[i] for i in turn]
        left = sorted(turn)
        self.bits = []
        for i in turn:
            self.bits.append(left.index(i))
            left.remove(i)
        self.bits.pop(0)

    def start(self):
        self.got = self.order.start(self.send, self.stages.pop(0))

    def done(self, *earlier):
        got = self.order.done(self.got)
        got = after(got, *earlier) if earlier else got
        last = not self.stages
        if self.vectors is None:
            out = fold(self.keep, got, None if last else self.bits.pop(0))
            self.keep, self.send = (out, None) if last else out
        elif last:
            self.keep, self.vectors = fold_vectors(self.keep, got, self.vectors, None)
        else:
            bit = (self.bits.pop(0), 2 << len(self.bits))
            self.keep, self.send, self.vectors = fold_vectors(self.keep, got, self.vectors, bit)


def play(events, chains):
    for event in events:
        if event == "|":
            next(iter(chains.values())).order.close()
            continue
        chain = chains[event.upper()]
        if event.isupper():
            chain.start()
        else:
            chain.done()


def plain_events(chains):
    events = ""
    left = {name: len(chain.stages) for name, chain in chains.items()}
    while any(left.values()):
        names = [n for n in left if left[n]]
        events += "".join(names) + "".join(names).lower() + "|"
        for n in names:
            left[n] -= 1
    return events


def prepare_kernel(units, number_ref, *refs):
    count = EXPAND_B + 6
    in_refs, outs = refs[:count], refs[count : count + 5]
    rows_ref, split_ref = refs[count + 5 : count + 7]
    held_refs, sems = refs[count + 7 : -1], refs[-1]
    copies = [pltpu.make_async_copy(i, h, sems.at[at]) for at, (i, h) in enumerate(zip(in_refs, held_refs))]
    for copy in copies:
        copy.start()
    key_mine_ref, key_other_ref, expand_mine_ref, expand_other_ref, vectors_ref = outs
    number = number_ref[0]
    even = number % 2 == 0
    rows_ref[...] = jnp.zeros_like(rows_ref)
    for copy in copies:
        copy.wait()
    weights, expand_ref, vectors = held_refs[:4], held_refs[4], held_refs[5:]
    own, width = weights[0].shape
    side = width // 2
    for i, ref in enumerate(weights):
        first, second = ref[:, :side], ref[:, side:]
        at = slice(i % 2 * side, (i % 2 + 1) * side)
        key_mine_ref[i // 2, :, at] = jnp.where(even, first, second)
        key_other_ref[i // 2, :, at] = jnp.where(even, second, first)
    for i in range(expand_ref.shape[1] // units):
        at = i // 2 * units
        split_ref[i % 2, :, at : at + units] = expand_ref[:, i * units : (i + 1) * units].astype(F32)
    for i in range(expand_mine_ref.shape[0]):
        at = slice(i * width, (i + 1) * width)
        first, second = split_ref[0, :, at], split_ref[1, :, at]
        expand_mine_ref[i] = jnp.where(even, first, second).astype(BF16)
        expand_other_ref[i] = jnp.where(even, second, first).astype(BF16)
    for i, ref in enumerate(vectors[:-1]):
        rows_ref[i : i + 1, :own] = ref[...].astype(F32)
    rows_ref[EXPAND_B : EXPAND_B + 1, :units] = vectors[-1][...].astype(F32)
    first = pltpu.roll(rows_ref[:8, :], number * own, 1)
    offset = (number // 2) * units
    second = pltpu.roll(rows_ref[8:, :], offset % width, 1)
    here = lax.broadcasted_iota(jnp.int32, second.shape, 0) == offset // width
    second = jnp.where(here, jnp.broadcast_to(second[:1], second.shape), 0.0)
    vectors_ref[...] = jnp.concatenate([first, second], 0).astype(BF16)


def prepare(number, weights, expand, vectors):
    own, width = weights[0].shape
    units = vectors[-1].shape[0]
    arrays = [*weights, expand, *[v.reshape(1, -1) for v in vectors]]
    arrays = [pltpu.with_memory_space_constraint(v, pltpu.HBM) for v in arrays]
    times = expand.shape[1] // 2 // width
    halves = [shaped((2, own, width), BF16)] * 2 + [shaped((times, own, width), BF16)] * 2
    return pl.pallas_call(
        functools.partial(prepare_kernel, units),
        out_shape=(*halves, shaped((VECTOR_ROWS, width), BF16)),
        in_specs=[SMEM] + [pl.BlockSpec(memory_space=pltpu.HBM)] * len(arrays),
        out_specs=(VMEM,) * 5,
        scratch_shapes=[
            pltpu.VMEM((VECTOR_ROWS, width), F32),
            pltpu.VMEM((2, own, expand.shape[1] // 2), F32),
            *[pltpu.VMEM(v.shape, v.dtype) for v in arrays],
            pltpu.SemaphoreType.DMA((len(arrays),)),
        ],
        cost_estimate=COST,
        compiler_params=pltpu.CompilerParams(vmem_limit_bytes=8 << 20),
        name="prepare",
    )(number, *arrays)


def unpack_vectors(number_ref, sums_ref, out_refs):
    own, units, width = out_refs[0].shape[1], out_refs[-1].shape[1], sums_ref.shape[1]
    number = number_ref[0]
    first = pltpu.roll(sums_ref[:8, :], width - number * own, 1)
    for i, ref in enumerate(out_refs[:-1]):
        ref[...] = first[i : i + 1, :own]
    offset = (number // 2) * units
    here = lax.broadcasted_iota(jnp.int32, (VECTOR_ROWS - 8, width), 0) == offset // width
    row = jnp.sum(jnp.where(here, sums_ref[8:, :], 0.0), axis=0, keepdims=True)
    row = pltpu.roll(jnp.broadcast_to(row, (8, width)), width - offset % width, 1)
    out_refs[-1][...] = row[:1, :units]


def place_attention_kernel(table_ref, core_ref, mine_ref, other_ref, vector_ref, kv_ref, q_ref, o_ref, bias_ref):
    half = kv_ref.shape[0] // 2
    rows, side = q_ref.shape[1], q_ref.shape[2]
    tile = mine_ref.shape[1]
    tiles = rows // tile

    def body(j, carry):
        for ref, at in ((mine_ref, j), (other_ref, j + half)):
            chip = table_ref[at]
            for i in range(tiles):
                to = slice(i * tile, (i + 1) * tile)
                kv_ref[chip, to] = ref[j * (2 * tiles) + i]
                q_ref[chip, to] = ref[j * (2 * tiles) + tiles + i, :, :side]
                o_ref[chip, to] = ref[j * (2 * tiles) + tiles + i, :, side:]
        return carry

    lax.fori_loop(0, half, body, 0)
    values = vector_ref[...].astype(F32)
    values = jnp.where(core_ref[0] == 0, values[:8, :side], values[:8, side:])
    bias_ref[:, :side] = jnp.zeros((8, side), F32)
    bias_ref[:, side : 2 * side] = jnp.broadcast_to(values[VALUE_B : VALUE_B + 1], (8, side))
    bias_ref[:, 2 * side :] = jnp.broadcast_to(values[QUERY_B : QUERY_B + 1], (8, side))


def place_hidden_kernel(table_ref, mine_a_ref, other_a_ref, mine_d_ref, other_d_ref, expand_ref, reduce_ref):
    half = mine_a_ref.shape[0]
    rows, width = expand_ref.shape[1], mine_a_ref.shape[2]

    def body(j, carry):
        for a_ref, d_ref, at in ((mine_a_ref, mine_d_ref, j), (other_a_ref, other_d_ref, j + half)):
            chip = table_ref[at]
            for i in range(expand_ref.shape[2] // width):
                expand_ref[chip, :, i * width : (i + 1) * width] = a_ref[j, i * rows : (i + 1) * rows]
            reduce_ref[chip] = d_ref[j]
        return carry

    lax.fori_loop(0, half, body, 0)


def split_expand_kernel(table_ref, expand_ref, mine_ref, other_ref):
    half = mine_ref.shape[0]
    rows, width = expand_ref.shape[1], mine_ref.shape[2]

    def body(j, carry):
        for ref, at in ((mine_ref, j), (other_ref, j + half)):
            chip = table_ref[at]
            for i in range(expand_ref.shape[2] // width):
                ref[j, i * rows : (i + 1) * rows] = expand_ref[chip, :, i * width : (i + 1) * width]
        return carry

    lax.fori_loop(0, half, body, 0)


def split_reduce_kernel(table_ref, reduce_ref, mine_ref, other_ref):
    half = mine_ref.shape[0]

    def body(j, carry):
        mine_ref[j] = reduce_ref[table_ref[j]]
        other_ref[j] = reduce_ref[table_ref[j + half]]
        return carry

    lax.fori_loop(0, half, body, 0)


def split_attention_kernel(table_ref, kv_ref, q_ref, o_ref, mine_ref, other_ref):
    half = mine_ref.shape[0]
    rows, side = q_ref.shape[1], q_ref.shape[2]

    def body(j, carry):
        for ref, at in ((mine_ref, j), (other_ref, j + half)):
            chip = table_ref[at]
            ref[j, :rows] = kv_ref[chip]
            ref[j, rows:, :side] = q_ref[chip]
            ref[j, rows:, side:] = o_ref[chip]
        return carry

    lax.fori_loop(0, half, body, 0)


def fold_kernel(bit, keep_ref, got_ref, *out_refs):
    if len(out_refs) == 1:
        out_refs[0][...] = keep_ref[...].astype(F32) + got_ref[...].astype(F32)
        return
    low = 1 << bit
    for j in range(out_refs[0].shape[0]):
        block = j % low + j // low * 2 * low
        for i, ref in enumerate(out_refs):
            at = block + i * low
            ref[j] = (keep_ref[at].astype(F32) + got_ref[at].astype(F32)).astype(BF16)


def fold(keep, got, bit):
    blocks = keep.shape[0]
    out = shaped(keep.shape, F32) if blocks == 1 else (shaped((blocks // 2,) + keep.shape[1:], BF16),) * 2
    return call(functools.partial(fold_kernel, bit), "fold", out, keep, got)


def fold_mixed_kernel(core_ref, keep_ref, got_ref, *out_refs):
    core = core_ref[0]
    for j in range(4):
        low, high = j % 2, j // 2 * 4
        for i, ref in enumerate(out_refs):
            at = jnp.where(core == 0, high + low * 2 + i, high + low + 2 * i)
            ref[j] = (keep_ref[at].astype(F32) + got_ref[at].astype(F32)).astype(BF16)


def fold_vectors_kernel(bit, keep_ref, got_ref, vector_ref, *out_refs):
    rows = keep_ref.shape[0]
    vectors = vector_ref[...] + got_ref[rows:, :].astype(F32)
    out_refs[-1][...] = vectors
    if len(out_refs) == 2:
        out_refs[0][...] = keep_ref[...].astype(F32) + got_ref[:rows, :].astype(F32)
        return
    bit, blocks = bit
    size, low = rows // blocks, 1 << bit
    for j in range(blocks // 2):
        block = j % low + j // low * 2 * low
        for i in range(2):
            at = (block + i * low) * size
            total = keep_ref[at : at + size, :].astype(F32) + got_ref[at : at + size, :].astype(F32)
            out_refs[i][j * size : (j + 1) * size, :] = total.astype(BF16)
    out_refs[1][rows // 2 :, :] = vectors.astype(BF16)


def fold_vectors(keep, got, vectors, bit):
    rows, width = keep.shape
    if bit is None:
        out = (shaped((rows, width), F32), shaped(vectors.shape, F32))
    else:
        out = (
            shaped((rows // 2, width), BF16),
            shaped((rows // 2 + VECTOR_ROWS, width), BF16),
            shaped(vectors.shape, F32),
        )
    return call(functools.partial(fold_vectors_kernel, bit), "fold_vectors", out, keep, got, vectors)


def project_kernel(mine_ref, other_ref, weight_ref, bias_ref, out_ref):
    width = weight_ref.shape[1]
    bias = bias_ref[:1, :width]

    @pl.when(pl.program_id(0) == 0)
    def _():
        out_ref[...] = (dot(mine_ref[...], weight_ref[...]) + bias).astype(BF16)

    @pl.when(pl.program_id(0) == 1)
    def _():
        out_ref[...] = (dot(other_ref[...], weight_ref[...]) + bias).astype(BF16)


def project(mine, other, weight, bias):
    rows, width = mine.shape
    step = min(rows, 512)
    steps = rows // step
    return pl.pallas_call(
        project_kernel,
        out_shape=shaped((2 * rows, width), BF16),
        grid=(2, steps),
        in_specs=[
            pl.BlockSpec((step, width), lambda i, j: (jnp.where(i == 0, j, steps - 1), 0)),
            pl.BlockSpec((step, width), lambda i, j: (jnp.where(i == 0, 0, j), 0)),
            pl.BlockSpec(weight.shape, lambda i, j: (0, 0)),
            pl.BlockSpec(bias.shape, lambda i, j: (0, 0)),
        ],
        out_specs=pl.BlockSpec((step, width), lambda i, j: (i * steps + j, 0)),
        cost_estimate=COST,
        compiler_params=limit(2 * rows, 20),
        name="project",
    )(mine, other, weight, bias)


def head_scores(half, query, key, mask):
    column = lax.broadcasted_iota(jnp.int32, (1, 2 * HEAD_DIM), 1)
    here = (column < HEAD_DIM) if half == 0 else (column >= HEAD_DIM)
    one = (column == HEAD_DIM * (1 - half)).astype(F32).astype(BF16)
    return times_transpose(jnp.where(here, key, mask), jnp.where(here, query, one))


def scaled(query):
    return (query.astype(F32) * 0.125).astype(BF16)


def attend_kernel(q_ref, k_ref, v_ref, mask_ref, out_ref, logs_ref):
    query = scaled(q_ref[...])
    outs = []
    for half in range(2):
        at = slice(half * HEAD_DIM, (half + 1) * HEAD_DIM)
        scores = head_scores(half, query, k_ref[...], mask_ref[...])
        top = jnp.max(scores, axis=0, keepdims=True)
        weights = jnp.exp(scores - top)
        total = jnp.sum(weights, axis=0, keepdims=True)
        outs.append(contract_rows(v_ref[:, at], weights.astype(BF16)) / total)
        logs_ref[0, half : half + 1, :] = top + jnp.log(total)
    out_ref[...] = jnp.transpose(jnp.concatenate(outs, 0))


def attend(query, keys, mask):
    rows, width = query.shape
    tokens = keys.shape[0]
    step = rows if tokens <= 4096 else 128
    pair = 2 * HEAD_DIM
    pairs = width // pair
    spec_q = pl.BlockSpec((step, pair), lambda h, i: (i, h))
    flops = 16 * rows * tokens * width
    return pl.pallas_call(
        attend_kernel,
        out_shape=(shaped((rows, width), F32), shaped((pairs, 8, rows), F32)),
        grid=(pairs, rows // step),
        in_specs=[
            spec_q,
            pl.BlockSpec((tokens, pair), lambda h, i: (0, h)),
            pl.BlockSpec((tokens, pair), lambda h, i: (0, h + pairs)),
            pl.BlockSpec((tokens, 128), lambda h, i: (0, 0)),
        ],
        out_specs=[spec_q, pl.BlockSpec((1, 8, step), lambda h, i: (h, 0, i))],
        cost_estimate=COST,
        compiler_params=limit(tokens, 28),
        name="attend",
    )(query, keys, keys, mask)


def attend_back_kernel(
    q_ref, k_ref, v_ref, g_ref, o_ref, logs_ref, mask_ref, dq_ref, dk_ref, dv_ref, bias_ref, dk_sum, dv_sum
):
    step = pl.program_id(0)
    column = lax.broadcasted_iota(jnp.int32, (1, 2 * HEAD_DIM), 1)
    low_query, none = scaled(q_ref[...]), jnp.zeros((), BF16)

    @pl.when(step == 0)
    def _():
        dk_sum[...] = jnp.zeros_like(dk_sum)
        dv_sum[...] = jnp.zeros_like(dv_sum)

    products = jnp.transpose(g_ref[...].astype(F32) * o_ref[...])
    grads, dk, dv = [], None, None
    for half in range(2):
        at = slice(half * HEAD_DIM, (half + 1) * HEAD_DIM)
        here = (column < HEAD_DIM) if half == 0 else (column >= HEAD_DIM)
        grad = jnp.where(here, g_ref[...], none)
        scores = head_scores(half, low_query, k_ref[...], mask_ref[...])
        probs = jnp.exp(scores - logs_ref[0, half : half + 1, :])
        dots = jnp.sum(products[at], axis=0, keepdims=True)
        grad_scores = (probs * (times_transpose(v_ref[...], grad) - dots)).astype(BF16)
        grads.append(contract_rows(k_ref[...], grad_scores)[at])
        dk_part = dot(grad_scores, jnp.where(here, q_ref[...], none))
        dv_part = dot(probs.astype(BF16), grad)
        if dk_sum.shape[0] > 4096:
            dk_sum[...] += dk_part
            dv_sum[...] += dv_part
        else:
            dk, dv = (dk_part, dv_part) if half == 0 else (dk + dk_part, dv + dv_part)
    if dk is not None:
        dk_sum[...] += dk
        dv_sum[...] += dv
    dq_ref[...] = jnp.transpose(jnp.concatenate(grads, 0) * 0.125).astype(BF16)

    @pl.when(step == pl.num_programs(0) - 1)
    def _():
        dk_ref[...] = (dk_sum[...] * 0.125).astype(BF16)
        dv_ref[...] = dv_sum[...].astype(BF16)
        bias_ref[...] = jnp.broadcast_to(columns(dv_sum[...]), bias_ref.shape)


def attend_back(which, query, keys, grad, attended, logs, mask):
    rows, width = query.shape
    tokens = keys.shape[0]
    step = rows if tokens <= 4096 else 128
    pair = 2 * HEAD_DIM
    pairs = width // pair
    single = {"pipeline_mode": pl.Buffered(1)} if tokens > 4096 else {}
    spec_q = pl.BlockSpec((step, pair), lambda i: (i, which))
    spec_dq = pl.BlockSpec((step, pair), lambda i: (i, 0))
    spec_k = pl.BlockSpec((tokens, pair), lambda i: (0, which), **single)
    spec_v = pl.BlockSpec((tokens, pair), lambda i: (0, which + pairs), **single)
    spec_dk = pl.BlockSpec((tokens, pair), lambda i: (0, 0))
    flops = 40 * rows * tokens * pair
    return pl.pallas_call(
        attend_back_kernel,
        out_shape=(
            shaped((rows, pair), BF16),
            shaped((tokens, pair), BF16),
            shaped((tokens, pair), BF16),
            shaped((8, pair), F32),
        ),
        grid=(rows // step,),
        in_specs=[
            spec_q,
            spec_k,
            spec_v,
            spec_q,
            spec_q,
            pl.BlockSpec((1, 8, step), lambda i: (which, 0, i)),
            pl.BlockSpec((tokens, 128), lambda i: (0, 0), **single),
        ],
        out_specs=[spec_dq, spec_dk, spec_dk, pl.BlockSpec((8, pair), lambda i: (0, 0))],
        scratch_shapes=[pltpu.VMEM((tokens, pair), F32), pltpu.VMEM((tokens, pair), F32)],
        cost_estimate=COST,
        compiler_params=limit(tokens, 28),
        name="attend_back",
    )(query, keys, keys, grad, attended, logs, mask)


def keys_inputs_kernel(*refs):
    *part_refs, own_ref, weight_ref, out_ref = refs
    total = None
    for i, ref in enumerate(part_refs):
        width = ref.shape[1]
        if i % 2:
            continue
        both = jnp.concatenate([ref[...], part_refs[i + 1][...]], axis=1)
        term = times_transpose(both, weight_ref[:, i * width : (i + 2) * width])
        total = term if total is None else total + term
    out_ref[...] = total.astype(BF16)

    @pl.when(pl.program_id(0) == 0)
    def _():
        rows = own_ref.shape[0]
        out_ref[:rows, :] = (total[:rows] + own_ref[...]).astype(BF16)


def keys_inputs(which, parts, own, weight):
    tokens, pair = parts[0].shape
    tokens //= 2
    width = weight.shape[0]
    step = min(tokens, 512)
    spec = pl.BlockSpec((step, pair), lambda i: (i + which * (tokens // step), 0))
    whole = [pl.BlockSpec(v.shape, lambda i: (0, 0)) for v in (own, weight)]
    return pl.pallas_call(
        keys_inputs_kernel,
        out_shape=shaped((tokens, width), BF16),
        grid=(tokens // step,),
        in_specs=[spec] * len(parts) + whole,
        out_specs=pl.BlockSpec((step, width), lambda i: (i, 0)),
        cost_estimate=COST,
        compiler_params=limit(tokens, 20),
        name="keys_inputs",
    )(*parts, own, weight)


def keys_weights_kernel(table_ref, mine_ref, other_ref, q_ref, o_ref, *refs):
    *part_refs, keep_ref, send_ref, sum_ref, held_ref = refs
    first = (pl.program_id(0) == 0) & (pl.program_id(1) == 0)
    last = (pl.program_id(0) == 1) & (pl.program_id(1) == pl.num_programs(1) - 1)
    both = jnp.concatenate([ref[...] for ref in part_refs], axis=1)
    chips, rows, width = held_ref.shape
    half, side = chips // 2, width // 2

    @pl.when(first)
    def _():
        sum_ref[...] = contract_rows(mine_ref[...], both)

    @pl.when((pl.program_id(0) == 0) & (pl.program_id(1) > 0))
    def _():
        sum_ref[...] += contract_rows(mine_ref[...], both)

    @pl.when(pl.program_id(0) == 1)
    def _():
        sum_ref[...] += contract_rows(other_ref[...], both)

    @pl.when(last)
    def _():
        held_ref[...] = sum_ref[...].astype(BF16).reshape(held_ref.shape)

        def body(j, carry):
            for ref, at in ((keep_ref, j), (send_ref, j + half)):
                chip = table_ref[at]
                ref[j, :rows] = held_ref[chip]
                ref[j, rows:, :side] = q_ref[chip]
                ref[j, rows:, side:] = o_ref[chip]
            return carry

        lax.fori_loop(0, half, body, 0)


def flat_keys_weights_kernel(mine_ref, other_ref, *refs):
    *part_refs, grad_ref, sum_ref = refs
    first = (pl.program_id(0) == 0) & (pl.program_id(1) == 0)
    last = (pl.program_id(0) == 1) & (pl.program_id(1) == pl.num_programs(1) - 1)
    both = jnp.concatenate([ref[...] for ref in part_refs], axis=1)

    @pl.when(first)
    def _():
        sum_ref[...] = jnp.zeros_like(sum_ref)

    @pl.when(pl.program_id(0) == 0)
    def _():
        sum_ref[...] += contract_rows(mine_ref[...], both)

    @pl.when(pl.program_id(0) == 1)
    def _():
        sum_ref[...] += contract_rows(other_ref[...], both)

    @pl.when(last)
    def _():
        grad_ref[...] = sum_ref[...].astype(BF16)


def keys_weights(table, mine, other, grad_q, grad_o, parts):
    rows, width = mine.shape
    pair = parts[0].shape[1]
    chips, own = grad_q.shape[:2]
    step = min(rows, 512)
    steps = rows // step
    fused = own % 16 == 0
    block = shaped((chips // 2, 2 * own, width), BF16)
    tokens = [
        pl.BlockSpec((step, width), lambda i, j, *t: (jnp.where(i == 0, j, steps - 1), 0)),
        pl.BlockSpec((step, width), lambda i, j, *t: (jnp.where(i == 0, 0, j), 0)),
    ]
    spec = pl.BlockSpec((step, pair), lambda i, j, *t: (i * steps + j, 0))
    whole = pl.BlockSpec((chips, own, width // 2), lambda i, j, *t: (0, 0, 0))
    blocks = pl.BlockSpec(block.shape, lambda i, j, *t: (0, 0, 0))
    cost = COST
    if fused:
        return pl.pallas_call(
            keys_weights_kernel,
            out_shape=(block, block),
            grid_spec=pltpu.PrefetchScalarGridSpec(
                num_scalar_prefetch=1,
                grid=(2, steps),
                in_specs=tokens + [whole, whole] + [spec] * len(parts),
                out_specs=[blocks, blocks],
                scratch_shapes=[pltpu.VMEM((width, width), F32), pltpu.VMEM((chips, own, width), BF16)],
            ),
            cost_estimate=cost,
            compiler_params=limit(2 * rows, 24),
            name="keys_weights",
        )(table, mine, other, grad_q, grad_o, *parts)
    grad = pl.pallas_call(
        flat_keys_weights_kernel,
        out_shape=shaped((width, width), BF16),
        grid=(2, steps),
        in_specs=tokens + [spec] * len(parts),
        out_specs=pl.BlockSpec((width, width), lambda i, j: (0, 0)),
        scratch_shapes=[pltpu.VMEM((width, width), F32)],
        cost_estimate=cost,
        name="keys_weights",
    )(mine, other, *parts)
    return call(
        split_attention_kernel,
        "split_attention",
        (block, block),
        table,
        grad.reshape(chips, own, width),
        grad_q,
        grad_o,
        scalars=1,
    )


def normalize(values):
    center = values - jnp.mean(values, axis=-1, keepdims=True)
    scale = lax.rsqrt(jnp.mean(center * center, axis=-1, keepdims=True) + EPSILON)
    return center * scale, scale


def normalize_back(grad, normal, scale):
    return scale * (
        grad
        - jnp.mean(grad, axis=-1, keepdims=True)
        - normal * jnp.mean(grad * normal, axis=-1, keepdims=True)
    )


def row(ref, which):
    return ref[which : which + 1, :].astype(F32)


def columns(values):
    return jnp.sum(values, axis=0, keepdims=True)


def output_kernel(
    core_ref, inputs_ref, mine_ref, other_ref, near_ref, far_ref, vector_ref, normal_ref, scale_ref, low_ref
):
    side = mine_ref.shape[1]
    core = core_ref[0]
    here, there = pl.ds(core * side, side), pl.ds((1 - core) * side, side)

    def product(ref):
        return dot(mine_ref[...], ref[here, :]) + dot(other_ref[...], ref[there, :])

    near, far = product(near_ref), product(far_ref)
    even = core == 0
    hidden = jnp.concatenate([jnp.where(even, near, far), jnp.where(even, far, near)], axis=1)
    hidden = inputs_ref[...].astype(F32) + hidden + row(vector_ref, OUTPUT_B)
    normal, scale = normalize(hidden)
    normal_ref[...] = normal
    scale_ref[...] = jnp.broadcast_to(scale, scale_ref.shape)
    low_ref[...] = (normal * row(vector_ref, GAIN_1) + row(vector_ref, SHIFT_1)).astype(BF16)


def hidden_kernel(
    mine_ref, other_ref, normal_ref, expand_ref, reduce_ref, vector_ref, active_ref, slope_ref, base_ref, far_ref,
    active_held, slope_held, base_held, sems,
):
    rows = mine_ref.shape[0]
    width = mine_ref.shape[1]
    both = jnp.concatenate([mine_ref[...], other_ref[...]], axis=0)
    total, copies = None, []
    for i in range(expand_ref.shape[1] // width):
        at = slice(i * width, (i + 1) * width)
        value = dot(both, expand_ref[:, at]) + row(vector_ref, EXPAND_B + i)
        normal = 0.5 + 0.5 * lax.erf(value * np.float32(0.7071067811865476))
        active = (value * normal).astype(BF16)
        active_held[:, at] = active
        density = jnp.exp(value * value * -0.5) * np.float32(0.3989422804014327)
        slope_held[:, at] = (normal + value * density).astype(BF16)
        for j, (held, ref) in enumerate(((active_held, active_ref), (slope_held, slope_ref))):
            copies.append(pltpu.make_async_copy(held.at[:, at], ref.at[:, at], sems.at[2 * i + j]))
            copies[-1].start()
        term = dot(active, reduce_ref[at, :])
        total = term if total is None else total + term
    middle = normal_ref[...] * row(vector_ref, GAIN_1) + row(vector_ref, SHIFT_1)
    base_held[...] = middle + total[:rows] + row(vector_ref, REDUCE_B)
    copies.append(pltpu.make_async_copy(base_held, base_ref, sems.at[len(copies)]))
    copies[-1].start()
    far_ref[...] = total[rows:].astype(BF16)
    for copy in copies:
        copy.wait()


def final_kernel(
    start_ref, base_ref, far_ref, cotangent_ref, vector_ref, out_ref, grad_ref, low_ref, sums_ref
):
    combined = base_ref[...] + far_ref[...].astype(F32)
    normal, scale = normalize(combined)
    gain = row(vector_ref, GAIN_2)
    out_ref[...] = (normal * gain + row(vector_ref, SHIFT_2)).astype(BF16)
    place = start_ref[0] + lax.broadcasted_iota(jnp.int32, combined.shape, 0)
    upstream = jnp.where(place < start_ref[1], cotangent_ref[...].astype(F32), 0.0)
    grad = normalize_back(upstream * gain, normal, scale)
    grad_ref[...] = grad
    low_ref[...] = grad.astype(BF16)
    sums_ref[...] = jnp.zeros_like(sums_ref)
    sums_ref[REDUCE_B : REDUCE_B + 1, :] = columns(grad)
    sums_ref[GAIN_2 : GAIN_2 + 1, :] = columns(upstream * normal)
    sums_ref[SHIFT_2 : SHIFT_2 + 1, :] = columns(upstream)


def hidden_back_kernel(table_a_ref, table_d_ref, *refs):
    cl_mine_ref, cl_other_ref, *far = refs[:8]
    outs, held, sems = refs[8:15], refs[15:-1], refs[-1]
    copies = [pltpu.make_async_copy(i, h, sems.at[at]) for at, (i, h) in enumerate(zip(far, held))]
    for copy in copies:
        copy.start()
    active_ref, slope_ref, reduce_ref, expand_ref, mid_mine_ref, mid_other_ref = held[:6]
    near_ref, far_ref, sums_ref, d_keep_ref, d_send_ref, a_keep_ref, a_send_ref = outs
    d_held_ref, a_held_ref, low_ref = held[6:]
    rows, width = cl_mine_ref.shape
    times = expand_ref.shape[1] // width
    both = jnp.concatenate([cl_mine_ref[...], cl_other_ref[...]], axis=0)
    sums_ref[...] = jnp.zeros_like(sums_ref)
    copies[0].wait()
    units = d_held_ref.shape[1]
    for i in range(times):
        part = contract_rows(active_ref[:, i * width : (i + 1) * width], both).astype(BF16)
        d_held_ref[i * width // units : (i + 1) * width // units] = part.reshape(width // units, units, width)
    split_reduce_kernel(table_d_ref, d_held_ref, d_keep_ref, d_send_ref)
    for copy in copies[1:3]:
        copy.wait()
    total = None
    for i in range(times):
        at = slice(i * width, (i + 1) * width)
        active = times_transpose(both, reduce_ref[at, :]).astype(BF16)
        grad = (active.astype(F32) * slope_ref[:, at].astype(F32)).astype(BF16)
        low_ref[:, at] = grad
        sums_ref[i : i + 1, :] = columns(grad.astype(F32))
    copies[3].wait()
    for i in range(times):
        at = slice(i * width, (i + 1) * width)
        term = times_transpose(low_ref[:, at], expand_ref[:, at])
        total = term if total is None else total + term
    near_ref[...] = total[:rows]
    far_ref[...] = total[rows:].astype(BF16)
    for copy in copies[4:]:
        copy.wait()
    mid = jnp.concatenate([mid_mine_ref[...], mid_other_ref[...]], axis=0)
    own = a_held_ref.shape[1]
    for i in range(times):
        at = slice(i * width, (i + 1) * width)
        a_held_ref[:, :, at] = contract_rows(mid, low_ref[:, at]).astype(BF16).reshape(width // own, own, width)
    split_expand_kernel(table_a_ref, a_held_ref, a_keep_ref, a_send_ref)


def hidden_back_plain_kernel(mine_ref, other_ref, expand_ref, reduce_ref, slope_ref, low_ref, near_ref, far_ref, sums_ref):
    rows, width = mine_ref.shape
    both = jnp.concatenate([mine_ref[...], other_ref[...]], axis=0)
    total = None
    sums_ref[...] = jnp.zeros_like(sums_ref)
    for i in range(expand_ref.shape[1] // width):
        at = slice(i * width, (i + 1) * width)
        active = times_transpose(both, reduce_ref[at, :]).astype(BF16)
        grad = (active.astype(F32) * slope_ref[:, at].astype(F32)).astype(BF16)
        low_ref[:, at] = grad
        sums_ref[i : i + 1, :] = columns(grad.astype(F32))
        term = times_transpose(grad, expand_ref[:, at])
        total = term if total is None else total + term
    near_ref[...] = total[:rows]
    far_ref[...] = total[rows:].astype(BF16)


def hidden_back(table_a, table_d, low, low_other, active, slope, reduce, expand, middle, middle_other, units):
    rows, width = low.shape
    hidden_units = reduce.shape[0]
    chips, own, times = hidden_units // units, width * units // hidden_units, hidden_units // width
    far = [active, slope, reduce, expand, middle, middle_other]
    far = [pltpu.with_memory_space_constraint(v, pltpu.HBM) for v in far]
    return pl.pallas_call(
        hidden_back_kernel,
        out_shape=(
            shaped((rows, width), F32),
            shaped((rows, width), BF16),
            shaped((8, width), F32),
            *(shaped((chips // 2, units, width), BF16),) * 2,
            *(shaped((chips // 2, times * own, width), BF16),) * 2,
        ),
        in_specs=[SMEM] * 2 + [VMEM] * 2 + [pl.BlockSpec(memory_space=pltpu.HBM)] * len(far),
        out_specs=(VMEM,) * 7,
        scratch_shapes=[
            *[pltpu.VMEM(v.shape, v.dtype) for v in far],
            pltpu.VMEM((chips, units, width), BF16),
            pltpu.VMEM((chips, own, hidden_units), BF16),
            pltpu.VMEM((2 * rows, hidden_units), BF16),
            pltpu.SemaphoreType.DMA((len(far),)),
        ],
        cost_estimate=COST,
        compiler_params=pltpu.CompilerParams(vmem_limit_bytes=24 << 20),
        name="hidden_back",
    )(table_a, table_d, low, low_other, *far)


def reduce_grads_kernel(low_mine_ref, low_other_ref, active_ref, grad_ref):
    width = low_mine_ref.shape[1]
    low = jnp.concatenate([low_mine_ref[...], low_other_ref[...]], axis=0)
    for i in range(active_ref.shape[1] // width):
        at = slice(i * width, (i + 1) * width)
        grad_ref[at, :] = contract_rows(active_ref[:, at], low).astype(BF16)


def expand_grads_kernel(mid_mine_ref, mid_other_ref, low_ref, grad_ref):
    width = mid_mine_ref.shape[1]
    mid = jnp.concatenate([mid_mine_ref[...], mid_other_ref[...]], axis=0)
    for i in range(low_ref.shape[1] // width):
        at = slice(i * width, (i + 1) * width)
        grad_ref[:, at] = contract_rows(mid, low_ref[:, at]).astype(BF16)


def output_back_kernel(
    core_ref, normal_ref, scale_ref, grad_ref, near_sum_ref, far_sum_ref, near_ref, far_ref, vector_ref,
    hidden_ref, low_ref, mine_ref, other_ref, sums_ref,
):
    side = near_ref.shape[1]
    core = core_ref[0]
    even = core == 0
    normal = normal_ref[...]
    grad_middle = grad_ref[...] + near_sum_ref[...] + far_sum_ref[...].astype(F32)
    grad = normalize_back(grad_middle * row(vector_ref, GAIN_1), normal, scale_ref[:, :1])
    hidden_ref[...] = grad
    low = grad.astype(BF16)
    low_ref[...] = low
    low_near = jnp.where(even, low[:, :side], low[:, side:])
    low_far = jnp.where(even, low[:, side:], low[:, :side])
    here, there = pl.ds(core * side, side), pl.ds((1 - core) * side, side)

    def product(rows):
        return times_transpose(low_near, near_ref[rows, :]) + times_transpose(low_far, far_ref[rows, :])

    mine_ref[...] = product(here).astype(BF16)
    other_ref[...] = product(there).astype(BF16)
    sums_ref[...] = jnp.zeros_like(sums_ref)
    sums_ref[OUTPUT_B : OUTPUT_B + 1, :] = columns(grad)
    sums_ref[GAIN_1 : GAIN_1 + 1, :] = columns(grad_middle * normal)
    sums_ref[SHIFT_1 : SHIFT_1 + 1, :] = columns(grad_middle)


def output_grads_kernel(core_ref, mine_ref, other_ref, low_ref, near_ref, far_ref):
    side = mine_ref.shape[1]
    core = core_ref[0]
    even = core == 0
    here, there = pl.ds(core * side, side), pl.ds((1 - core) * side, side)
    for rows, ref in ((here, mine_ref), (there, other_ref)):
        product = contract_rows(ref[...], low_ref[...])
        near_ref[rows, :] = jnp.where(even, product[:, :side], product[:, side:])
        far_ref[rows, :] = jnp.where(even, product[:, side:], product[:, :side]).astype(BF16)


def join_units(units, even, mine_ref, other_ref, out_ref):
    times, width = mine_ref.shape[0], mine_ref.shape[2]
    for i in range(times):
        mine, other = mine_ref[i], other_ref[2 + i]
        parts = (jnp.where(even, mine, other), jnp.where(even, other, mine))
        for j in range(width // units):
            at = (i * (width // units) + j) * 2 * units
            for k, part in enumerate(parts):
                out_ref[:, at + k * units : at + (k + 1) * units] = part[:, j * units : (j + 1) * units]


def finish_kernel(units, number_ref, mine_ref, expand_ref, other_ref, sums_ref, expand_out_ref, *out_refs):
    side = mine_ref.shape[2] // 2
    even = number_ref[0] % 2 == 0
    for i, ref in enumerate(out_refs[:4]):
        at = slice(i % 2 * side, (i % 2 + 1) * side)
        mine, other = mine_ref[i // 2, :, at], other_ref[i // 2, :, at]
        ref[:, :side] = jnp.where(even, mine, other)
        ref[:, side:] = jnp.where(even, other, mine)
    join_units(units, even, expand_ref, other_ref, expand_out_ref)
    unpack_vectors(number_ref, sums_ref, out_refs[4:])


def query_back_kernel(mine_ref, other_ref, weight_ref, *refs):
    *dq_refs, near_ref, far_ref, grad_ref, sums_ref = refs
    rows = mine_ref.shape[0]
    grads = jnp.concatenate([ref[...] for ref in dq_refs], axis=1)
    product = times_transpose(grads, weight_ref[...])
    near_ref[...] = product[:rows]
    far_ref[...] = product[rows:]
    both = jnp.concatenate([mine_ref[...], other_ref[...]], axis=0)
    grad_ref[...] = contract_rows(both, grads).astype(BF16)
    sums_ref[...] = jnp.broadcast_to(columns(grads.astype(F32)), sums_ref.shape)


def body(
    layer_input,
    cotangent,
    lengths,
    query_weight,
    query_bias,
    key_weight,
    value_weight,
    value_bias,
    output_weight,
    output_bias,
    attn_gain,
    attn_shift,
    expand_weight,
    expand_bias,
    reduce_weight,
    reduce_bias,
    final_gain,
    final_shift,
):
    place = Place()
    core = place.core
    core_s = core.reshape(1)
    number_s = place.number.reshape(1)
    chips = place.count // 2
    inputs = layer_input[0]
    rows, width = inputs.shape
    side = width // 2
    own = query_weight.shape[0]
    units = reduce_weight.shape[0]
    hidden_units = units * chips
    times = hidden_units // width
    length = lengths[0]
    even = core == 0

    masks = [place.others(place.weight_stages, k) for k in range(2)]
    usual = len(place.weight_stages) == 4 and len(place.token_stages) == 3
    turns = WEIGHT_TURNS if usual else {}

    def chip_table(bit=None):
        blocks = np.arange(chips)
        if bit is not None:
            blocks = np.concatenate([blocks[blocks >> bit & 1 == i] for i in range(2)])
        return (place.number ^ jnp.where(even, masks[0][blocks], masks[1][blocks])) // 2

    def first_bit(name):
        return turns[name][0] if name in turns else len(place.weight_stages) - 1

    table = chip_table()
    token_masks = [place.others(place.token_stages, k) for k in range(2)]
    near_ctx = place.context ^ jnp.where(even, token_masks[0], token_masks[1])
    far_ctx = (place.context ^ 1) ^ jnp.where(even, token_masks[1], token_masks[0])
    blocks = jnp.concatenate([near_ctx, far_ctx])
    positions = (blocks[:, None] * rows + jnp.arange(rows, dtype=jnp.int32)).reshape(-1, 1)
    mask = jnp.where(positions < length, 0.0, MASKED).astype(BF16)
    mask = jnp.where(jnp.arange(2 * HEAD_DIM) % HEAD_DIM == 0, mask, 0)

    def joined(mine, other):
        return jnp.where(
            even, jnp.concatenate([mine, other], 1), jnp.concatenate([other, mine], 1)
        ).reshape(-1, width)

    vector_list = [query_bias, value_bias, output_bias, attn_gain, attn_shift, reduce_bias, final_gain, final_shift]
    attention_mine, attention_other, expand_mine, expand_other, vectors = prepare(
        number_s,
        [key_weight, value_weight, query_weight, output_weight],
        expand_weight,
        vector_list + [expand_bias],
    )
    vector_swap = place.swap(vectors, 0)
    vectors = vectors + jnp.where(jnp.arange(VECTOR_ROWS)[:, None] < 8, vector_swap, 0)

    stages = place.weight_stages
    token_stages = place.token_stages
    order = Order(place, STRICT[0])

    other_inputs = place.swap(inputs, 0)
    attention_swapped = place.swap(attention_other, 0)
    if FIRST_WAITS:
        order.last = (attention_swapped,)
    attention_blocks = Gather(order, joined(attention_mine, attention_swapped), stages, vectors)
    block_rows = attention_blocks.held.shape[0]
    expand_rows = joined(expand_mine, place.swap(expand_other, 0))
    expand_blocks = Gather(order, expand_rows[None], stages)
    reduce_blocks = Gather(order, reduce_weight[None], stages)
    token_blocks = Gather(order, inputs[None], token_stages)
    chains = {"X": token_blocks, "B": attention_blocks, "A": expand_blocks, "D": reduce_blocks}
    play(FORWARD[0] if usual else plain_events(chains), chains)

    aligned = (2 * own) % 16 == 0
    tile = 16 if aligned else 2 * own

    def tiles(array):
        array = array if aligned else array[: array.shape[0] // block_rows * block_rows]
        return array.reshape(-1, tile, width)

    weights_kv, weights_q, output_near, bias = call(
        place_attention_kernel,
        "place_attention",
        (
            shaped((chips, 2 * own, width), BF16),
            shaped((chips, 2 * own, side), BF16),
            shaped((chips, 2 * own, side), BF16),
            shaped((8, 3 * side), F32),
        ),
        table,
        core_s,
        tiles(attention_blocks.held),
        tiles(attention_blocks.got),
        attention_blocks.vectors,
        scalars=2,
    )
    vectors = attention_blocks.vectors
    weights_kv = weights_kv.reshape(width, width)
    weights_q = weights_q.reshape(width, side)
    output_near = output_near.reshape(width, side)
    if usual:
        play(FORWARD[1], chains)

    sequence_near = jnp.concatenate([token_blocks.held, token_blocks.got]).reshape(-1, width)
    sequence_far = place.swap(sequence_near, 0)
    keys = project(sequence_near, sequence_far, weights_kv, bias)
    if usual:
        play(FORWARD[2], chains)
    query = jnp.concatenate([inputs, other_inputs])
    query = (dot(query, weights_q) + bias[:1, 2 * side :]).astype(BF16)
    attended, logs = attend(query, keys, mask)
    if usual:
        play(FORWARD[3], chains)
    output_far = place.swap(output_near, 0)
    expand_matrix, reduce_matrix = call(
        place_hidden_kernel,
        "place_hidden",
        (shaped((chips, 2 * own, hidden_units), BF16), shaped((chips, units, width), BF16)),
        table,
        expand_blocks.held,
        expand_blocks.got,
        reduce_blocks.held,
        reduce_blocks.got,
        scalars=1,
    )
    expand_matrix = expand_matrix.reshape(width, hidden_units)
    reduce_matrix = reduce_matrix.reshape(hidden_units, width)
    attended_low = attended.astype(BF16)
    attended_mine = attended_low[:rows]
    attended_other = place.swap(attended_low[rows:], 0)

    normal_one, scale_one, middle_low = call(
        output_kernel,
        "output",
        (shaped((rows, width), F32), shaped((rows, 128), F32), shaped((rows, width), BF16)),
        core_s,
        Far(inputs),
        attended_mine,
        attended_other,
        Far(output_near),
        output_far,
        Far(vectors),
        scalars=1,
    )

    middle_other = place.swap(middle_low, 0)
    active, slope, base, far = call(
        hidden_kernel,
        "hidden",
        (
            shaped((2 * rows, hidden_units), BF16),
            shaped((2 * rows, hidden_units), BF16),
            shaped((rows, width), F32),
            shaped((rows, width), BF16),
        ),
        middle_low,
        middle_other,
        normal_one,
        expand_matrix,
        reduce_matrix,
        vectors,
        scratch=[
            pltpu.VMEM((2 * rows, hidden_units), BF16),
            pltpu.VMEM((2 * rows, hidden_units), BF16),
            pltpu.VMEM((rows, width), F32),
            pltpu.SemaphoreType.DMA((2 * times + 1,)),
        ],
        stored=(0, 1, 2),
    )
    far = place.swap(far, 0)
    start_s = jnp.stack([place.context * rows, length])
    layer_output, grad_combined, combined_low, sums_two = call(
        final_kernel,
        "final",
        (
            shaped((rows, width), BF16),
            shaped((rows, width), F32),
            shaped((rows, width), BF16),
            shaped((8, width), F32),
        ),
        start_s,
        Far(base),
        far,
        Far(cotangent[0]),
        Far(vectors),
        scalars=1,
        room=8,
    )
    combined_other = place.swap(combined_low, 0)
    table_d, table_a = chip_table(first_bit("D")), chip_table(first_bit("A"))
    if (2 * own) % 16 == 0:
        near, far, sums_expand, reduce_keep, reduce_send, expand_keep, expand_send = hidden_back(
            table_a,
            table_d,
            combined_low,
            combined_other,
            active,
            slope,
            reduce_matrix,
            expand_matrix,
            middle_low,
            middle_other,
            units,
        )
    else:
        grad_expanded, near, far, sums_expand = call(
            hidden_back_plain_kernel,
            "hidden_back",
            (
                shaped((2 * rows, hidden_units), BF16),
                shaped((rows, width), F32),
                shaped((rows, width), BF16),
                shaped((8, width), F32),
            ),
            combined_low,
            combined_other,
            expand_matrix,
            reduce_matrix,
            slope,
        )
        grads = call(
            reduce_grads_kernel,
            "reduce_grads",
            shaped((hidden_units, width), BF16),
            combined_low,
            combined_other,
            active,
        )
        out = (shaped((chips // 2, units, width), BF16),) * 2
        reduce_keep, reduce_send = call(
            split_reduce_kernel, "split_reduce", out, table_d, grads.reshape(chips, units, width), scalars=1
        )
        grads = call(
            expand_grads_kernel,
            "expand_grads",
            shaped((width, hidden_units), BF16),
            middle_low,
            middle_other,
            grad_expanded,
        )
        out = (shaped((chips // 2, times * 2 * own, width), BF16),) * 2
        expand_keep, expand_send = call(
            split_expand_kernel, "split_expand", out, table_a, grads.reshape(chips, 2 * own, hidden_units), scalars=1
        )
    far = place.swap(far, 0)

    grad_hidden, hidden_low, grad_mine, grad_other, sums_one = call(
        output_back_kernel,
        "output_back",
        (
            shaped((rows, width), F32),
            shaped((rows, width), BF16),
            shaped((rows, side), BF16),
            shaped((rows, side), BF16),
            shaped((8, width), F32),
        ),
        core_s,
        Far(normal_one),
        Far(scale_one),
        grad_combined,
        near,
        far,
        Far(output_near),
        Far(output_far),
        Far(vectors),
        scalars=1,
    )
    grad_heads = jnp.concatenate([grad_mine, place.swap(grad_other, 0)])
    output_near_grad, output_far_grad = call(
        output_grads_kernel,
        "output_grads",
        (shaped((width, side), F32), shaped((width, side), BF16)),
        core_s,
        Far(attended_mine),
        Far(attended_other),
        hidden_low,
        scalars=1,
    )
    grad_output = (output_near_grad + place.swap(output_far_grad, 0).astype(F32)).astype(BF16)

    def own_half(array, axis):
        first, second = lax.index_in_dim(array, 0, axis, False), lax.index_in_dim(array, 1, axis, False)
        return jnp.where(even, first, second), jnp.where(even, second, first)

    order = Order(place, STRICT[1])
    if OUTPUT_FIRST:
        order.last = (hidden_low,)
    chains = {
        "D": Scatter(order, reduce_keep, reduce_send, stages, turn=turns.get("D")),
        "A": Scatter(order, expand_keep, expand_send, stages, turn=turns.get("A")),
    }
    if usual:
        play("DA", chains)

    def held_back(kernel, array):
        return order.wait(array) if usual and WAITS[kernel] else array

    parts = []
    pairs = side // (2 * HEAD_DIM)
    for which in range(pairs):
        parts.append(attend_back(which, held_back(which, query), keys, grad_heads, attended, logs, mask))
        if usual:
            play(BACKWARD[which], chains)
    grad_query, grad_keys, grad_values, value_bias_sums = zip(*parts)
    parts = grad_keys + grad_values
    near, far, grad_query_w, query_bias_sum = call(
        query_back_kernel,
        "query_back",
        (
            shaped((rows, width), F32),
            shaped((rows, width), F32),
            shaped((width, side), BF16),
            shaped((8, side), F32),
        ),
        Far(inputs),
        Far(other_inputs),
        Far(weights_q),
        *grad_query,
    )
    query_near, query_far = near, far

    mine_rows = jnp.stack([query_bias_sum[0], jnp.concatenate([v[0] for v in value_bias_sums])])
    zero = jnp.zeros_like(mine_rows)
    mine_rows = jnp.where(even, jnp.concatenate([mine_rows, zero], 1), jnp.concatenate([zero, mine_rows], 1))
    vector_sums = jnp.concatenate([mine_rows, (sums_one + sums_two)[2:], sums_expand])
    vector_swap = place.swap(vector_sums, 0)

    far_part = keys_inputs(1, (held_back(4, parts[0]), *parts[1:]), query_far, weights_kv)
    far_got = place.swap(far_part, 0)
    near_part = keys_inputs(0, (held_back(5, parts[0]), *parts[1:]), query_near, weights_kv)
    blocks_shape = (sequence_near.shape[0] // rows, rows, width)
    near_part, far_part = near_part.reshape(blocks_shape), far_got.reshape(blocks_shape)
    if usual and TOKEN_TURN == "mix":
        half_shape = (blocks_shape[0] // 2,) + blocks_shape[1:]
        x_keep, x_send = call(
            fold_mixed_kernel, "fold_mixed", (shaped(half_shape, BF16),) * 2, core_s, near_part, far_part, scalars=1
        )
        (near_even, near_odd), (even_bit, odd_bit), last_stage = token_stages
        mixed = [(even_bit, near_odd), last_stage, (near_even, odd_bit)]
        chains["X"] = Scatter(order, x_keep, x_send, mixed)
    else:
        turn = range(len(token_stages))[::-1]
        if usual:
            kinds = "ab"[:TOKEN_NEAR] + "y" + "ab"[TOKEN_NEAR:]
            turn = [kinds.index(kind) for kind in TOKEN_TURN]
        x_keep, x_send = fold(near_part, far_part, turn[0])
        chains["X"] = Scatter(order, x_keep, x_send, token_stages, turn=turn)
    if usual:
        play(BACKWARD[3], chains)

    inputs_first = (x_send,) if usual and INPUTS_FIRST else ()
    keep, send = keys_weights(
        chip_table(first_bit("B")),
        after(held_back(3, sequence_near), *inputs_first),
        sequence_far,
        grad_query_w.reshape(chips, 2 * own, side),
        grad_output.reshape(chips, 2 * own, side),
        parts,
    )
    vector_swap = after(vector_swap, keep) if VECTORS_LATE else vector_swap
    vector_sums = vector_sums + jnp.where(jnp.arange(VECTOR_ROWS)[:, None] < 8, vector_swap, 0)
    keep = keep.reshape(-1, width)
    send = jnp.concatenate([send.reshape(-1, width), vector_sums.astype(BF16)])
    chains["B"] = Scatter(order, keep, send, stages, vector_sums, turns.get("B"))
    play(BACKWARD[4].rstrip("|b") if usual else plain_events(chains), chains)
    reduce_out = chains["D"].keep[0]
    expand_sum = chains["A"].keep[0].reshape(times, 2, own, width)
    input_grad = grad_hidden + chains["X"].keep[0]

    if usual:
        chains["B"].done(input_grad, *((reduce_out,) if REDUCE_FIRST else ()))
    keep, vector_sums = chains["B"].keep, chains["B"].vectors
    expand_mine, expand_other = own_half(expand_sum, 1)
    pieces = keep.reshape(2, 2, own, width)
    pieces_mine, pieces_other = own_half(pieces, 1)
    swapped = place.swap(jnp.concatenate([pieces_other, expand_other]), 0)
    expand_out, *outs = call(
        functools.partial(finish_kernel, units),
        "finish",
        [shaped((own, 2 * hidden_units), F32)]
        + [shaped((own, width), F32)] * 4
        + [shaped((1, own), F32)] * 8
        + [shaped((1, units), F32)],
        number_s,
        pieces_mine,
        expand_mine,
        swapped,
        vector_sums,
        scalars=1,
    )
    weights_out, outs = outs[:4], outs[4:]
    outs = [v.reshape(-1) for v in outs]
    return (
        layer_output[None],
        input_grad[None],
        weights_out[2],
        outs[QUERY_B],
        weights_out[0],
        weights_out[1],
        outs[VALUE_B],
        weights_out[3],
        outs[OUTPUT_B],
        outs[GAIN_1],
        outs[SHIFT_1],
        expand_out,
        outs[EXPAND_B],
        reduce_out,
        outs[REDUCE_B],
        outs[GAIN_2],
        outs[SHIFT_2],
    )


def solution(mesh):
    tokens = P("seq", "ctx", None)
    matrix = P(("seq", "ctx"), None)
    vector = P(("seq", "ctx"))
    weights = (
        matrix,
        vector,
        matrix,
        matrix,
        vector,
        matrix,
        vector,
        vector,
        vector,
        matrix,
        vector,
        matrix,
        vector,
        vector,
        vector,
    )
    return jax.shard_map(
        body,
        mesh=mesh,
        in_specs=(tokens, tokens, P("seq")) + weights,
        out_specs=(tokens, tokens) + weights,
        check_vma=False,
    )
```
